32 devices in a mesh: dp: 8 (over z, x), blk: 4 (over y, core).
Axes of the slice: x: 2, y: 2, z: 4, core: 2. Of those that a mesh axis runs over, the one named last changes fastest.
Arguments:
- h_in: bfloat16 [8, 512, 768], P('dp', 'blk'), may hold values from -6 to 6
- g_in: bfloat16 [8, 512, 768], P('dp', 'blk'), may hold values from -6 to 6
- memory: bfloat16 [8, 384, 768], P('dp', 'blk'), may hold values from -6 to 6
- cot_h: bfloat16 [8, 512, 768], P('dp', 'blk'), may hold values from -6 to 6
- cot_g: bfloat16 [8, 512, 768], P('dp', 'blk'), may hold values from -6 to 6
- perm_order: int32 [8, 512], P('dp', 'blk'), may hold values from 0 to 511, each once within a row
- target: int32 [8, 512], P('dp', 'blk'), may hold values from 0 to 1, as said below
- segment: int32 [8, 512], P('dp', 'blk'), may hold values from 0 to 1, as said below
- mem_flag: int32 [8], P('dp'), may hold values 0 or 1
- w_q: bfloat16 [768, 768], replicated, may hold values from -0.21875 to 0.21875
- w_k: bfloat16 [768, 768], replicated, may hold values from -0.21875 to 0.21875
- w_v: bfloat16 [768, 768], replicated, may hold values from -0.21875 to 0.21875
- w_r: bfloat16 [768, 768], replicated, may hold values from -0.21875 to 0.21875
- w_o: bfloat16 [768, 768], replicated, may hold values from -2.5 to 2.5
- r_w_bias: float32 [768], replicated, may hold values from -3 to 3
- r_r_bias: float32 [768], replicated, may hold values from -3 to 3
- r_s_bias: float32 [768], replicated, may hold values from -3 to 3
- seg_embed: float32 [2, 768], replicated, may hold values from -6 to 6
- ln1_gain: float32 [768], replicated, may hold values from 0.5 to 1.5
- ln1_bias: float32 [768], replicated, may hold values from -1.25 to 1.25
- w_1: bfloat16 [768, 3072], replicated, may hold values from -0.21875 to 0.21875
- b_1: float32 [3072], replicated, may hold values from -1.25 to 1.25
- w_2: bfloat16 [3072, 768], replicated, may hold values from -0.109375 to 0.109375
- b_2: float32 [768], replicated, may hold values from -1.25 to 1.25
- ln2_gain: float32 [768], replicated, may hold values from 0.5 to 1.5
- ln2_bias: float32 [768], replicated, may hold values from -1.25 to 1.25
Outputs:
- h_out: bfloat16 [8, 512, 768], P('dp', 'blk')
- g_out: bfloat16 [8, 512, 768], P('dp', 'blk')
- h_grad: float32 [8, 512, 768], P('dp', 'blk')
- g_grad: float32 [8, 512, 768], P('dp', 'blk')
- memory_grad: float32 [8, 384, 768], P('dp', 'blk')
- w_q_grad: float32 [589824], P(('dp', 'blk'))
- w_k_grad: float32 [589824], P(('dp', 'blk'))
- w_v_grad: float32 [589824], P(('dp', 'blk'))
- w_r_grad: float32 [589824], P(('dp', 'blk'))
- w_o_grad: float32 [589824], P(('dp', 'blk'))
- w_1_grad: float32 [2359296], P(('dp', 'blk'))
- w_2_grad: float32 [2359296], P(('dp', 'blk'))
- r_w_bias_grad: float32 [768], replicated
- r_r_bias_grad: float32 [768], replicated
- r_s_bias_grad: float32 [768], replicated
- seg_embed_grad: float32 [2, 768], replicated
- ln1_gain_grad: float32 [768], replicated
- ln1_bias_grad: float32 [768], replicated
- b_1_grad: float32 [3072], replicated
- b_2_grad: float32 [768], replicated
- ln2_gain_grad: float32 [768], replicated
- ln2_bias_grad: float32 [768], replicated
- rms_stats: float32 [6], replicated
The draws below stay inside these ranges and needn't reach their ends.
Inputs may be any that keep to these rules, and one draw needn't show every extreme that they name: target is 0 at positions 0 and 1 of each sequence and 1 at position 2. Each sequence's segment ids are 0 and then 1, the first 1 at a position from 128 to 384.
All inputs are finite; a program needn't handle non-finite values. No bound on the sum of `mem_flag` on one device may be relied on, other than what follows from the above.
Results may differ from the reference program's by a relative error of at most 0.03.
Values may be sent and summed in bfloat16 or wider, within the bound.
A program may use at most 192 MiB of HBM per device.

```python
import math
import jax
import jax.numpy as jnp
from jax import lax

D = 768
FF = 3072
HEADS = 12
HEAD_DIM = 64
L = 512
M = 384
SEQS = 8


def draw_target(key, part):
    places = lax.broadcasted_iota(jnp.int32, (SEQS, L), 1)
    picked = jax.random.randint(key, (SEQS, L), 0, 6)
    flags = jnp.where(picked == 0, 1, 0)
    flags = jnp.where(places < 2, 0, flags)
    flags = jnp.where(places == 2, 1, flags)
    return flags.astype(jnp.int32)


def draw_segment(key, part):
    places = lax.broadcasted_iota(jnp.int32, (SEQS, L), 1)
    border = jax.random.randint(key, (SEQS, 1), L // 4, 3 * L // 4 + 1)
    return jnp.where(places >= border, 1, 0).astype(jnp.int32)


def set_ends(result, key, smallest, top_value):
    index_at = [jax.random.randint(jax.random.fold_in(key, axis), (), 0, length) for axis, length in enumerate(result.shape)]
    main_axis = result.shape.index(max(result.shape))
    neighbour = index_at[:main_axis] + [(index_at[main_axis] + 1) % result.shape[main_axis]] + index_at[main_axis + 1:]
    return result.at[tuple(index_at)].set(smallest).at[tuple(neighbour)].set(top_value)


def block_scale(stream_key, dims, split, low, top_value):
    def one(dim, parts):
        steps = jax.random.uniform(jax.random.fold_in(jax.random.fold_in(stream_key, 6), dim), (parts,), jnp.float32, low / len(split), top_value / len(split))
        return jnp.repeat(jnp.exp(steps), dims[dim] // parts).reshape((-1,) + (1,) * (len(dims) - dim - 1))

    loudness = one(*split[0])
    for cut in split[1:]:
        loudness = loudness * one(*cut)
    return loudness


def bell_draw(rng, shape, deviation, most, shards=(), dtype=jnp.bfloat16):
    entries = jax.random.normal(rng, shape, jnp.float32) * deviation
    if len(shards) > 0:
        entries = block_scale(rng, shape, shards, -0.22, 0.18) * entries
    return jnp.clip(entries, min=-most, max=most).astype(dtype)


def setup_inputs(seed: int = 0) -> dict:
    key_of = jax.random.split(jax.random.key(seed), 27)
    return {
        "h_in": bell_draw(key_of[0], (SEQS, L, D), 1.0, 6.0, ((0, 8), (1, 4))),
        "g_in": bell_draw(key_of[1], (SEQS, L, D), 1.0, 6.0, ((0, 8), (1, 4))),
        "memory": bell_draw(key_of[2], (SEQS, M, D), 1.0, 6.0, ((0, 8), (1, 4))),
        "cot_h": bell_draw(key_of[3], (SEQS, L, D), 1.0, 6.0, ((0, 8), (1, 4))),
        "cot_g": bell_draw(key_of[4], (SEQS, L, D), 1.0, 6.0, ((0, 8), (1, 4))),
        "perm_order": jax.vmap(lambda own: jax.random.permutation(own, L))(jax.random.split(key_of[5], SEQS)).reshape((SEQS, L)).astype(jnp.int32),
        "target": draw_target(jax.random.fold_in(key_of[26], 71), 0),
        "segment": draw_segment(jax.random.fold_in(key_of[26], 71), 0),
        "mem_flag": set_ends((jax.random.randint(key_of[8], (SEQS,), 0, 4) < 3).astype(jnp.int32), jax.random.fold_in(key_of[8], 1), 0, 1),
        "w_q": bell_draw(key_of[9], (D, D), D ** -0.5, 0.21875),
        "w_k": bell_draw(key_of[10], (D, D), D ** -0.5, 0.21875),
        "w_v": bell_draw(key_of[11], (D, D), D ** -0.5, 0.21875),
        "w_r": bell_draw(key_of[12], (D, D), D ** -0.5, 0.21875),
        "w_o": bell_draw(key_of[13], (D, D), (max(D // 128, 1)) ** -0.5, 2.5),
        "r_w_bias": bell_draw(key_of[14], (D,), 0.5, 3.0, (), jnp.float32),
        "r_r_bias": bell_draw(key_of[15], (D,), 0.5, 3.0, (), jnp.float32),
        "r_s_bias": bell_draw(key_of[16], (D,), 0.5, 3.0, (), jnp.float32),
        "seg_embed": bell_draw(key_of[17], (2, D), 1.0, 6.0, (), jnp.float32),
        "ln1_gain": jnp.clip(1.0 + 0.1 * jax.random.normal(key_of[18], (D,), jnp.float32), 0.5, 1.5),
        "ln1_bias": bell_draw(key_of[19], (D,), 0.2, 1.25, (), jnp.float32),
        "w_1": bell_draw(key_of[20], (D, FF), D ** -0.5, 0.21875),
        "b_1": bell_draw(key_of[21], (FF,), 0.2, 1.25, (), jnp.float32),
        "w_2": bell_draw(key_of[22], (FF, D), FF ** -0.5, 0.109375),
        "b_2": bell_draw(key_of[23], (D,), 0.2, 1.25, (), jnp.float32),
        "ln2_gain": jnp.clip(1.0 + 0.1 * jax.random.normal(key_of[24], (D,), jnp.float32), 0.5, 1.5),
        "ln2_bias": bell_draw(key_of[25], (D,), 0.2, 1.25, (), jnp.float32),
    }


HIGHEST_MODE = lax.Precision.HIGHEST
EPSILON = 1e-12
NEGATIVE = -1e+30

@jax.custom_vjp
def low(v):
    return lax.optimization_barrier(v.astype(jnp.bfloat16)).astype(jnp.float32)

@jax.custom_vjp
def low_back(v):
    return v

def low_keep(v):
    return (low(v), None)

def low_pass(kept, grad):
    return (grad,)

def back_keep(v):
    return (v, None)

def back_low(kept, grad):
    return (low(grad),)
low.defvjp(low_keep, low_pass)
low_back.defvjp(back_keep, back_low)

def layer_norm(hidden, norm_gain, norm_bias):
    center = hidden - lax.optimization_barrier(jnp.mean(hidden, axis=-1, keepdims=True))
    spread = lax.optimization_barrier(jnp.mean(center * center, axis=-1, keepdims=True))
    return center * lax.rsqrt(spread + EPSILON) * norm_gain + norm_bias

def gelu_tanh(values):
    return jax.nn.gelu(values, approximate=True)

def position_table(first_dist, dist_count, model_width):
    distance = (first_dist - lax.iota(jnp.int32, dist_count)).astype(jnp.float32)
    inv_freq = jnp.exp(lax.iota(jnp.float32, model_width // 2) * (-2.0 * math.log(10000.0) / model_width))
    angles = distance[:, None] * inv_freq[None, :]
    return jnp.concatenate([jnp.sin(angles), jnp.cos(angles)], axis=1)

def shift_rows(table_rows, key_count):
    lead_dims = table_rows.shape[:-2]
    query_count, dist_count = table_rows.shape[-2:]
    flat_rows = table_rows.reshape(lead_dims + (query_count * dist_count,))
    flat_rows = lax.slice_in_dim(flat_rows, query_count - 1, query_count - 1 + query_count * (dist_count - 1), axis=flat_rows.ndim - 1)
    return flat_rows.reshape(lead_dims + (query_count, dist_count - 1))[..., :key_count]

def precise(form, left, right):
    return jnp.einsum(form, left, right, precision=HIGHEST_MODE)

def sequence_pass(params, rel_proj, h_row, g_row, mem_rows, order_row, target_row, seg_row, flag_value):
    w_q, w_k, w_v, w_o, r_w_bias, r_r_bias, r_s_bias, seg_embed, ln1_gain, ln1_bias, w_1, b_1, w_2, b_2, ln2_gain, ln2_bias = params
    seq_len = h_row.shape[0]
    mem_len = mem_rows.shape[0]
    keys_all = mem_len + seq_len
    score_scale = 1.0 / math.sqrt(HEAD_DIM)
    streams = jnp.stack([h_row, g_row])
    q_raw = low_back(precise('tqe,ef->tqf', streams, w_q))
    joined = jnp.concatenate([mem_rows, h_row], axis=0)
    key_rows = low_back(low(jnp.dot(joined, w_k, precision=HIGHEST_MODE))).reshape(keys_all, HEADS, HEAD_DIM)
    val_rows = low_back(low(jnp.dot(joined, w_v, precision=HIGHEST_MODE))).reshape(keys_all, HEADS, HEAD_DIM)
    q_word = low(q_raw + r_w_bias).reshape(2, seq_len, HEADS, HEAD_DIM)
    q_rel = low(q_raw + r_r_bias).reshape(2, seq_len, HEADS, HEAD_DIM)
    q_seg = (q_raw + r_s_bias).reshape(2, seq_len, HEADS, HEAD_DIM)
    content = low_back(precise('tqhd,khd->thqk', q_word, key_rows))
    rel_full = precise('tqhd,whd->thqw', q_rel, rel_proj.reshape(-1, HEADS, HEAD_DIM))
    position = low_back(shift_rows(rel_full, keys_all))
    seg_both = precise('tqhd,chd->thqc', q_seg, seg_embed.reshape(2, HEADS, HEAD_DIM))
    key_seg = jnp.concatenate([jnp.zeros((mem_len,), jnp.int32), seg_row.astype(jnp.int32)])
    mismatch = (seg_row.astype(jnp.int32)[:, None] != key_seg[None, :])[None, None]
    seg_term = jnp.where(mismatch, seg_both[..., 1:2], seg_both[..., 0:1])
    order_eff = jnp.where(target_row > 0, order_row, -1).astype(jnp.int32)
    visible = order_eff[None, :] <= order_eff[:, None]
    not_self = lax.iota(jnp.int32, seq_len)[:, None] != lax.iota(jnp.int32, seq_len)[None, :]
    tok_mask = jnp.stack([visible, visible & not_self])
    mem_mask = jnp.broadcast_to(flag_value > 0, (2, seq_len, mem_len))
    allowed = jnp.concatenate([mem_mask, tok_mask], axis=2)[:, None]
    scores = (content + position + seg_term) * score_scale
    attn_probs = jax.nn.softmax(jnp.where(allowed, scores, NEGATIVE), axis=-1)
    probs_low = low(attn_probs)
    attn_f = precise('thqk,khd->tqhd', probs_low, val_rows).reshape(2, seq_len, HEADS * HEAD_DIM)
    attn_out = low_back(low(attn_f))
    branch_att = low_back(precise('tqe,ef->tqf', attn_out, w_o))
    resid_one = branch_att + streams
    out_one = layer_norm(resid_one, ln1_gain, ln1_bias)
    ffn_in = low(out_one)
    pre_act = low_back(precise('tqe,ef->tqf', ffn_in, w_1) + b_1)
    activation = low(gelu_tanh(pre_act))
    branch_ffn = low_back(precise('tqf,fe->tqe', activation, w_2) + b_2)
    resid_two = branch_ffn + out_one
    out_two = layer_norm(resid_two, ln2_gain, ln2_bias)
    target_f = target_row.astype(jnp.float32)[:, None]
    stat_terms = jnp.stack([jnp.sum(branch_att[0] * branch_att[0]), jnp.sum(branch_ffn[0] * branch_ffn[0]), jnp.sum(out_two[0] * out_two[0]), jnp.sum(branch_att[1] * branch_att[1] * target_f), jnp.sum(branch_ffn[1] * branch_ffn[1] * target_f), jnp.sum(out_two[1] * out_two[1] * target_f), jnp.asarray(seq_len, jnp.float32), jnp.sum(target_f)])
    return (out_two, stat_terms)

def reference(h_in, g_in, memory, cot_h, cot_g, perm_order, target, segment, mem_flag, w_q, w_k, w_v, w_r, w_o, r_w_bias, r_r_bias, r_s_bias, seg_embed, ln1_gain, ln1_bias, w_1, b_1, w_2, b_2, ln2_gain, ln2_bias):
    params = tuple((member.astype(jnp.float32) for member in (w_q, w_k, w_v, w_r, w_o, r_w_bias, r_r_bias, r_s_bias, seg_embed, ln1_gain, ln1_bias, w_1, b_1, w_2, b_2, ln2_gain, ln2_bias)))
    checked = jax.checkpoint(sequence_pass)

    def forward(params, h_all, g_all, mem_all):
        pos_table = low(position_table(M + L - 1, L + M + L, D))
        rel_proj = low(jnp.dot(pos_table, params[3], precision=HIGHEST_MODE))
        rest = params[:3] + params[4:]

        def scan_step(running, inputs):
            out_two, stat_terms = checked(rest, rel_proj, *inputs)
            return (running + stat_terms, out_two)
        totals, outputs = lax.scan(scan_step, jnp.zeros((8,), jnp.float32), (h_all, g_all, mem_all, perm_order, target, segment, mem_flag))
        return ((outputs[:, 0], outputs[:, 1]), totals)
    primal_out, back_fn, totals = jax.vjp(forward, params, h_in.astype(jnp.float32), g_in.astype(jnp.float32), memory.astype(jnp.float32), has_aux=True)
    param_grads, h_grad, g_grad, memory_grad = back_fn((cot_h.astype(jnp.float32), cot_g.astype(jnp.float32)))
    denoms = jnp.stack([totals[6], totals[6], totals[6], totals[7], totals[7], totals[7]])
    rms_stats = jnp.sqrt(totals[:6] / (denoms * D))
    return (primal_out[0].astype(jnp.bfloat16), primal_out[1].astype(jnp.bfloat16), h_grad, g_grad, memory_grad, param_grads[0].reshape(-1), param_grads[1].reshape(-1), param_grads[2].reshape(-1), param_grads[3].reshape(-1), param_grads[4].reshape(-1), param_grads[11].reshape(-1), param_grads[13].reshape(-1), param_grads[5], param_grads[6], param_grads[7], param_grads[8], param_grads[9], param_grads[10], param_grads[12], param_grads[14], param_grads[15], param_grads[16], rms_stats)
```

```python
import functools
import math

import jax
import jax.numpy as jnp
from jax import lax
from jax.experimental import pallas as pl
from jax.experimental.pallas import tpu as pltpu
from jax.sharding import PartitionSpec as P

HEADS = 12
HEAD_DIM = 64
EPSILON = 1e-12
NEGATIVE = -1e30
SCALE = 1.0 / math.sqrt(HEAD_DIM)
F32 = jnp.float32
BF16 = jnp.bfloat16


def layer_norm(hidden, norm_gain, norm_bias):
    center = hidden - jnp.mean(hidden, axis=-1, keepdims=True)
    spread = jnp.mean(center * center, axis=-1, keepdims=True)
    return center * lax.rsqrt(spread + EPSILON) * norm_gain + norm_bias


def gelu_tanh(values):
    return jax.nn.gelu(values, approximate=True)


def position_table(first_dist, dist_count, model_width):
    distance = (first_dist - lax.iota(jnp.int32, dist_count)).astype(F32)
    inv_freq = jnp.exp(
        lax.iota(F32, model_width // 2) * (-2.0 * math.log(10000.0) / model_width)
    )
    angles = distance[:, None] * inv_freq[None, :]
    return jnp.concatenate([jnp.sin(angles), jnp.cos(angles)], axis=1)


def dot_nn(left, right):
    return lax.dot_general(left, right, (((1,), (0,)), ((), ())), preferred_element_type=F32)


def dot_nt(left, right):
    return lax.dot_general(left, right, (((1,), (1,)), ((), ())), preferred_element_type=F32)


def dot_tn(left, right):
    return lax.dot_general(left, right, (((0,), (0,)), ((), ())), preferred_element_type=F32)


def swap(values, axis, step):
    count = lax.axis_size(axis)
    return lax.ppermute(values, axis, [(i, i ^ step) for i in range(count)])


def bits_of(count):
    return [1 << k for k in range(count.bit_length() - 1)]


def seg_columns(q_seg, embed):
    return (
        jnp.sum(q_seg * embed[0:1], axis=1, keepdims=True),
        jnp.sum(q_seg * embed[1:2], axis=1, keepdims=True),
    )


def attn_fwd_kernel(
    heads,
    rows,
    mem_rows,
    blocks,
    place_ref,
    *refs,
):
    x_refs = refs[:blocks]
    (
        w_ref,
        rel_ref,
        bias_ref,
        embed_ref,
        key_order_ref,
        key_seg_ref,
        query_order_ref,
        query_seg_ref,
        out_ref,
        prob_ref,
        af_ref,
        q_ref,
        k_ref,
        v_ref,
        mask_ref,
    ) = refs[blocks:]
    piece = pl.program_id(0)
    block_id = place_ref[0]
    wide = heads * HEAD_DIM
    mem_all = mem_rows * blocks
    keys = k_ref.shape[1]
    span = rows + keys

    @pl.when(piece == 0)
    def _():
        lane = lax.broadcasted_iota(jnp.int32, (keys, HEAD_DIM), 1)
        extra = jnp.where(lane < 2, 1.0, jnp.where(lane < 4, key_seg_ref[...], 0.0)).astype(BF16)
        for h in range(heads):
            k_ref[h, :, HEAD_DIM:] = extra
        for i in range(blocks):
            owner = block_id ^ i
            mem_at = pl.ds(pl.multiple_of(owner * mem_rows, 32), mem_rows)
            tok_at = pl.ds(pl.multiple_of(mem_all + owner * rows, 32), rows)
            qkv = dot_nn(x_refs[i][...], w_ref[...])
            q_ref[i] = qkv[mem_rows:, :wide]
            low = qkv[: mem_rows + rows, wide:].astype(BF16)
            for h in range(heads):
                k_part = low[:, h * HEAD_DIM : (h + 1) * HEAD_DIM]
                v_part = low[:, wide + h * HEAD_DIM : wide + (h + 1) * HEAD_DIM]
                k_ref[h, mem_at, :HEAD_DIM] = k_part[:mem_rows]
                k_ref[h, tok_at, :HEAD_DIM] = k_part[mem_rows:]
                v_ref[h, mem_at, :] = v_part[:mem_rows]
                v_ref[h, tok_at, :] = v_part[mem_rows:]

    owner = block_id ^ piece
    tok_at = pl.ds(pl.multiple_of(owner * rows, 32), rows)
    visible = key_order_ref[...] <= query_order_ref[tok_at, :]
    key_at = lax.broadcasted_iota(jnp.int32, (rows, keys), 1) - mem_all - owner * rows
    other = key_at != lax.broadcasted_iota(jnp.int32, (rows, keys), 0)
    mask_ref[:rows, :] = jnp.where(visible, 0.0, NEGATIVE)
    mask_ref[rows:, :] = jnp.where(visible & other, 0.0, NEGATIVE)
    seg = query_seg_ref[tok_at, :]
    seg = jnp.concatenate([seg, seg], axis=0)
    rel_at = pl.ds(pl.multiple_of((blocks - 1) * rows - owner * rows, 32), span)
    lane = lax.broadcasted_iota(jnp.int32, (2 * rows, HEAD_DIM), 1)
    for h in range(heads):
        own = slice(h * HEAD_DIM, (h + 1) * HEAD_DIM)
        raw = q_ref[piece, :, own]
        q_word = ((raw + bias_ref[0:1, own]).astype(BF16) * SCALE).astype(BF16)
        q_rel = ((raw + bias_ref[1:2, own]).astype(BF16) * SCALE).astype(BF16)
        same, differ = seg_columns((raw + bias_ref[2:3, own]) * SCALE, embed_ref[:, own])
        gap = differ - same
        base = same + gap * seg
        slope = gap * (1.0 - 2.0 * seg)
        base_high = base.astype(BF16).astype(F32)
        slope_high = slope.astype(BF16).astype(F32)
        extra = jnp.where(
            lane == 0,
            base_high,
            jnp.where(
                lane == 1,
                base - base_high,
                jnp.where(lane == 2, slope_high, jnp.where(lane == 3, slope - slope_high, 0.0)),
            ),
        ).astype(BF16)
        q_aug = jnp.concatenate([q_word, extra], axis=1)
        rel = dot_nt(q_rel, rel_ref[h, rel_at, :])
        shift = span - (rows - 1)
        rel = jnp.concatenate(
            [
                pltpu.roll(rel[:rows], shift, 1, stride=1, stride_axis=0)[:, :keys],
                pltpu.roll(rel[rows:], shift, 1, stride=1, stride_axis=0)[:, :keys],
            ],
            axis=0,
        )
        scores = dot_nt(q_aug, k_ref[h]) + rel + mask_ref[...]
        weight = jnp.exp(scores - jnp.max(scores, axis=1, keepdims=True))
        probs = (weight * (1.0 / jnp.sum(weight, axis=1, keepdims=True))).astype(BF16)
        prob_ref[h, 0] = probs
        attn_f = dot_nn(probs, v_ref[h])
        af_ref[0, :, own] = attn_f
        out_ref[0, :, own] = attn_f.astype(BF16)


def flip_eights(values):
    index = 7 - lax.broadcasted_iota(jnp.int32, (8, values.shape[1]), 0)
    return jnp.take_along_axis(values, index, axis=0)


def spread_rows(values, rows, keys):
    span = rows + keys
    padded = jnp.concatenate([values, jnp.zeros((rows, rows), F32)], axis=1)
    groups = []
    for a in range(rows // 8):
        group = flip_eights(padded[8 * a : 8 * a + 8])
        group = pltpu.roll(group, (rows - 8 - 8 * a) % span, 1, stride=1, stride_axis=0)
        groups.append(flip_eights(group))
    return jnp.concatenate(groups, axis=0)


def attn_bwd_kernel(heads, rows, mem_rows, blocks, place_ref, *refs):
    gb_refs = refs[:blocks]
    (
        wo_ref,
        prob_ref,
        af_ref,
        q_ref,
        k_ref,
        v_ref,
        rel_ref,
        bias_ref,
        embed_ref,
        query_seg_ref,
        grads_ref,
        rel_grad_ref,
        small_ref,
        ga_ref,
        kt_ref,
        vt_ref,
        rt_ref,
    ) = refs[blocks:]
    piece = pl.program_id(0)
    block_id = place_ref[0]
    mem_all = mem_rows * blocks
    keys = k_ref.shape[1]
    span = rows + keys

    @pl.when(piece == 0)
    def _():
        for i in range(blocks):
            ga_ref[i] = dot_nt(gb_refs[i][...], wo_ref[...]).astype(BF16)
        kt_ref[...] = jnp.zeros_like(kt_ref)
        vt_ref[...] = jnp.zeros_like(vt_ref)
        rt_ref[...] = jnp.zeros_like(rt_ref)
        small_ref[...] = jnp.zeros_like(small_ref)

    owner = block_id ^ piece
    tok_at = pl.ds(pl.multiple_of(owner * rows, 32), rows)
    rel_start = pl.multiple_of((blocks - 1) * rows - owner * rows, 128)
    rel_at = pl.ds(rel_start, span)
    seg = query_seg_ref[tok_at, :]
    seg = jnp.concatenate([seg, seg], axis=0)
    for h in range(heads):
        own = slice(h * HEAD_DIM, (h + 1) * HEAD_DIM)
        raw = q_ref[piece, :, own]
        q_word = (raw + bias_ref[0:1, own]).astype(BF16)
        q_rel = (raw + bias_ref[1:2, own]).astype(BF16)
        q_seg = raw + bias_ref[2:3, own]
        embed = embed_ref[:, own]
        ga = ga_ref[piece, :, own]
        probs = prob_ref[h, 0]
        ga_f = ga.astype(F32) * SCALE
        row_dot = jnp.sum(ga_f * af_ref[0, :, own], axis=1, keepdims=True)
        grad_prob = dot_nt(ga_f.astype(BF16), v_ref[h])
        grad_score = probs.astype(F32) * (grad_prob - row_dot)
        grad_low = grad_score.astype(BF16)
        wide_word = dot_nn(grad_low, k_ref[h])
        grad_word = wide_word[:, :HEAD_DIM]
        total = wide_word[:, HEAD_DIM : HEAD_DIM + 1]
        ones = wide_word[:, HEAD_DIM + 2 : HEAD_DIM + 3]
        differ = ones + seg * (total - 2.0 * ones)
        same = total - differ
        grad_seg = same * embed[0:1] + differ * embed[1:2]
        spread = jnp.concatenate(
            [
                spread_rows(grad_score[:rows], rows, keys),
                spread_rows(grad_score[rows:], rows, keys),
            ],
            axis=0,
        ).astype(BF16)
        grad_rel = dot_nn(spread, rel_ref[h, rel_at, :])
        kt_ref[h] += dot_tn(q_word, grad_low)
        vt_ref[h] += dot_tn(ga, probs)
        rt_ref[h, :, pl.ds(rel_start, span)] += dot_tn(q_rel, spread)
        grads_ref[piece, : 2 * rows, own] = (grad_word + grad_rel + grad_seg).astype(BF16)
        small_ref[:, own] += jnp.concatenate(
            [
                jnp.sum(grad_word, axis=0, keepdims=True),
                jnp.sum(grad_rel, axis=0, keepdims=True),
                jnp.sum(grad_seg, axis=0, keepdims=True),
                jnp.sum(same * q_seg, axis=0, keepdims=True),
                jnp.sum(differ * q_seg, axis=0, keepdims=True),
                jnp.zeros((3, HEAD_DIM), F32),
            ],
            axis=0,
        )

    @pl.when(piece == blocks - 1)
    def _():
        for h in range(heads):
            own = slice(h * HEAD_DIM, (h + 1) * HEAD_DIM)
            rel_grad_ref[:, own] = rt_ref[h].T.astype(BF16)
            for base, acc in ((2 * rows, kt_ref), (3 * rows + mem_rows, vt_ref)):
                full = acc[h].T.astype(BF16)
                for i in range(blocks):
                    home = i ^ block_id
                    grads_ref[home, base : base + mem_rows, own] = full[
                        i * mem_rows : (i + 1) * mem_rows
                    ]
                    grads_ref[home, base + mem_rows : base + mem_rows + rows, own] = full[
                        mem_all + i * rows : mem_all + (i + 1) * rows
                    ]


def whole(shape):
    return pl.BlockSpec(shape, lambda *_: (0,) * len(shape))


def local(
    h_in,
    g_in,
    memory,
    cot_h,
    cot_g,
    perm_order,
    target,
    segment,
    mem_flag,
    w_q,
    w_k,
    w_v,
    w_r,
    w_o,
    r_w_bias,
    r_r_bias,
    r_s_bias,
    seg_embed,
    ln1_gain,
    ln1_bias,
    w_1,
    b_1,
    w_2,
    b_2,
    ln2_gain,
    ln2_bias,
):
    _, rows, width = h_in.shape
    mem_rows = memory.shape[1]
    hidden = w_1.shape[1]
    blocks = lax.axis_size("blk")
    groups = lax.axis_size("dp")
    block_id = lax.axis_index("blk")
    group_id = lax.axis_index("dp")
    tok_all = rows * blocks
    mem_all = mem_rows * blocks
    keys = mem_all + tok_all
    dist_count = tok_all + keys
    heads = HEADS // blocks
    wide = heads * HEAD_DIM
    both = 2 * rows
    chunk = mem_rows + 2 * rows
    share = groups * blocks
    place = block_id.astype(jnp.int32).reshape(1)

    def gather(values):
        pieces = [values]
        for step in bits_of(blocks):
            pieces = pieces + [swap(one, "blk", step) for one in pieces]
        return pieces

    def in_order(pieces):
        stacked = jnp.stack(pieces)
        return jnp.stack(
            [lax.dynamic_index_in_dim(stacked, block_id ^ i, 0, keepdims=False) for i in range(blocks)]
        )

    order_own = jnp.where(target > 0, perm_order, -1)
    x_own = jnp.concatenate([memory[0], h_in[0], g_in[0]], axis=0)
    small_pieces = gather(jnp.concatenate([order_own, segment], axis=0))
    x_pieces = gather(x_own)
    token_info = in_order(small_pieces)
    order_all = token_info[:, 0].reshape(tok_all)
    segment_all = token_info[:, 1].reshape(tok_all).astype(F32)
    mem_order = jnp.where(mem_flag[0] > 0, -2, 1 << 30) * jnp.ones((mem_all,), jnp.int32)
    key_order = jnp.concatenate([mem_order, order_all]).reshape(1, keys)
    key_seg = jnp.concatenate([jnp.zeros((mem_all,), F32), segment_all]).reshape(keys, 1)
    query_order = order_all.reshape(tok_all, 1)
    query_seg = segment_all.reshape(tok_all, 1)

    def column_slice(weight, index):
        return lax.dynamic_slice_in_dim(weight, index * wide, wide, axis=1)

    w_qkv = jnp.concatenate([column_slice(w, block_id) for w in (w_q, w_k, w_v)], axis=1)
    w_r_own = column_slice(w_r, block_id)
    wo_pieces = [
        lax.dynamic_slice_in_dim(w_o, (block_id ^ i) * wide, wide, axis=0) for i in range(blocks)
    ]
    biases = column_slice(jnp.stack([r_w_bias, r_r_bias, r_s_bias]), block_id)
    embeds = column_slice(seg_embed, block_id)
    pos_table = position_table(keys - 1, dist_count, width).astype(BF16)
    rel_heads = (
        jnp.einsum("wd,dhe->hwe", pos_table, w_r_own.reshape(width, heads, HEAD_DIM),
                   preferred_element_type=F32)
        .astype(BF16)
    )

    vmem = pltpu.CompilerParams(vmem_limit_bytes=60 << 20)
    attn_out, probs, attn_f, q_raw, k_aug, v_all = pl.pallas_call(
        functools.partial(attn_fwd_kernel, heads, rows, mem_rows, blocks),
        name="attn_fwd",
        grid_spec=pltpu.PrefetchScalarGridSpec(
            num_scalar_prefetch=1,
            grid=(blocks,),
            in_specs=[whole((chunk, width))] * blocks
            + [
                whole((width, 3 * wide)),
                whole((heads, dist_count, HEAD_DIM)),
                whole((3, wide)),
                whole((2, wide)),
                whole((1, keys)),
                whole((keys, 1)),
                whole((tok_all, 1)),
                whole((tok_all, 1)),
            ],
            out_specs=[
                pl.BlockSpec((1, both, wide), lambda p, _: (p, 0, 0)),
                pl.BlockSpec((heads, 1, both, keys), lambda p, _: (0, p, 0, 0)),
                pl.BlockSpec((1, both, wide), lambda p, _: (p, 0, 0)),
                whole((blocks, both, wide)),
                whole((heads, keys, 2 * HEAD_DIM)),
                whole((heads, keys, HEAD_DIM)),
            ],
            scratch_shapes=[pltpu.VMEM((both, keys), F32)],
        ),
        out_shape=[
            jax.ShapeDtypeStruct((blocks, both, wide), BF16),
            jax.ShapeDtypeStruct((heads, blocks, both, keys), BF16),
            jax.ShapeDtypeStruct((blocks, both, wide), F32),
            jax.ShapeDtypeStruct((blocks, both, wide), F32),
            jax.ShapeDtypeStruct((heads, keys, 2 * HEAD_DIM), BF16),
            jax.ShapeDtypeStruct((heads, keys, HEAD_DIM), BF16),
        ],
        compiler_params=vmem,
    )(
        place, *x_pieces, w_qkv, rel_heads, biases, embeds, key_order, key_seg, query_order,
        query_seg,
    )

    def exchange(pieces):
        return [pieces[0]] + [swap(pieces[i], "blk", i) for i in range(1, blocks)]

    attn_pieces = exchange([attn_out[i] for i in range(blocks)])
    branch_att = sum(dot_nn(a, w) for a, w in zip(attn_pieces, wo_pieces))
    streams = jnp.concatenate([h_in[0], g_in[0]], axis=0)
    resid_one = branch_att + streams.astype(F32)
    out_one = layer_norm(resid_one, ln1_gain, ln1_bias)
    ffn_in = out_one.astype(BF16)
    ffn_pieces = gather(ffn_in)
    pre_act = dot_nn(ffn_in, w_1) + b_1
    activation = gelu_tanh(pre_act).astype(BF16)
    branch_ffn = dot_nn(activation, w_2) + b_2
    resid_two = branch_ffn + out_one
    out_two = layer_norm(resid_two, ln2_gain, ln2_bias)
    target_f = target[0].astype(F32)[:, None]
    stat_weight = jnp.concatenate([jnp.ones((rows, 1), F32), target_f], axis=0)

    def stats_of(values):
        weighted = jnp.sum(values * values, axis=1, keepdims=True) * stat_weight
        return jnp.sum(weighted[:rows]), jnp.sum(weighted[rows:])

    att_stat, ffn_stat, out_stat = stats_of(branch_att), stats_of(branch_ffn), stats_of(out_two)
    stat_terms = jnp.stack(
        [
            att_stat[0],
            ffn_stat[0],
            out_stat[0],
            att_stat[1],
            ffn_stat[1],
            out_stat[1],
            jnp.asarray(rows, F32),
            jnp.sum(target_f),
        ]
    )
    cot = jnp.concatenate([cot_h[0], cot_g[0]], axis=0).astype(F32)
    grad_resid_two, grad_ln2_gain, grad_ln2_bias = jax.vjp(
        layer_norm, resid_two, ln2_gain, ln2_bias
    )[1](cot)
    grad_ffn = grad_resid_two.astype(BF16)
    grad_ffn_pieces = gather(grad_ffn)
    grad_b_2 = jnp.sum(grad_ffn.astype(F32), axis=0)
    grad_act = dot_nt(grad_ffn, w_2)
    grad_pre = jax.vjp(gelu_tanh, pre_act)[1](grad_act)[0].astype(BF16)
    grad_b_1 = jnp.sum(grad_pre.astype(F32), axis=0)
    grad_out_one = grad_resid_two + dot_nt(grad_pre, w_1)
    grad_resid_one, grad_ln1_gain, grad_ln1_bias = jax.vjp(
        layer_norm, resid_one, ln1_gain, ln1_bias
    )[1](grad_out_one)
    grad_branch = grad_resid_one.astype(BF16)
    branch_pieces = gather(grad_branch)

    part = hidden // share
    w_1_own = lax.dynamic_index_in_dim(
        w_1.reshape(width, groups, blocks, part), block_id, 2, keepdims=False
    ).reshape(width, groups * part)
    b_1_own = lax.dynamic_index_in_dim(
        b_1.reshape(groups, blocks, part), block_id, 1, keepdims=False
    ).reshape(groups * part)
    w_2_own = lax.dynamic_index_in_dim(
        w_2.reshape(groups, blocks, part, width), block_id, 1, keepdims=False
    ).reshape(groups * part, width)
    ffn_all = jnp.concatenate(ffn_pieces, axis=0)
    grad_ffn_all = jnp.concatenate(grad_ffn_pieces, axis=0)
    pre_slice = dot_nn(ffn_all, w_1_own) + b_1_own
    act_slice = gelu_tanh(pre_slice).astype(BF16)
    grad_act_slice = dot_nt(grad_ffn_all, w_2_own)
    grad_pre_slice = jax.vjp(gelu_tanh, pre_slice)[1](grad_act_slice)[0].astype(BF16)
    grad_w_1 = dot_tn(ffn_all, grad_pre_slice)
    grad_w_2 = dot_tn(act_slice, grad_ffn_all)

    def reduce_groups(values, steps):
        tail = values.shape[1:]
        held = values
        done = 0
        names = list(bits_of(groups))
        left = [s for s in reversed(names)]
        for step in steps:
            at = left.index(step)
            shaped = held.reshape((1 << at, 2, -1) + tail)
            mine = (group_id // step) % 2
            keep = lax.dynamic_index_in_dim(shaped, mine, 1, keepdims=False)
            give = lax.dynamic_index_in_dim(shaped, 1 - mine, 1, keepdims=False).astype(BF16)
            got = swap(give, "dp", step)
            held = keep.astype(F32) + got.astype(F32)
            left.pop(at)
            done += 1
        return held.reshape(tail)

    steps = bits_of(groups)
    first_order = steps
    second_order = [steps[1], steps[0]] + steps[2:]
    w_2_sum = reduce_groups(grad_w_2.reshape(groups, part, width), second_order)
    w_1_sum = reduce_groups(
        grad_w_1.reshape(groups, width // groups, groups * part), first_order
    )
    grad_w_o = sum(dot_tn(attn_out[i], branch_pieces[i]) for i in range(blocks))
    w_o_sum = reduce_groups(grad_w_o.reshape(groups, wide // groups, width), second_order)
    w_o_flat = lax.ppermute(
        w_o_sum,
        ("dp", "blk"),
        [(d * blocks + k, groups * k + d) for d in range(groups) for k in range(blocks)],
    ).reshape(-1)

    grads, rel_grad, head_small = pl.pallas_call(
        functools.partial(attn_bwd_kernel, heads, rows, mem_rows, blocks),
        name="attn_bwd",
        grid_spec=pltpu.PrefetchScalarGridSpec(
            num_scalar_prefetch=1,
            grid=(blocks,),
            in_specs=[whole((both, width))] * blocks
            + [
                whole((wide, width)),
                pl.BlockSpec((heads, 1, both, keys), lambda p, _: (0, p, 0, 0)),
                pl.BlockSpec((1, both, wide), lambda p, _: (p, 0, 0)),
                whole((blocks, both, wide)),
                whole((heads, keys, 2 * HEAD_DIM)),
                whole((heads, keys, HEAD_DIM)),
                whole((heads, dist_count, HEAD_DIM)),
                whole((3, wide)),
                whole((2, wide)),
                whole((tok_all, 1)),
            ],
            out_specs=[
                whole((blocks, 4 * rows + 2 * mem_rows, wide)),
                whole((dist_count, wide)),
                whole((8, wide)),
            ],
            scratch_shapes=[
                pltpu.VMEM((blocks, both, wide), BF16),
                pltpu.VMEM((heads, HEAD_DIM, keys), F32),
                pltpu.VMEM((heads, HEAD_DIM, keys), F32),
                pltpu.VMEM((heads, HEAD_DIM, dist_count), F32),
            ],
        ),
        out_shape=[
            jax.ShapeDtypeStruct((blocks, 4 * rows + 2 * mem_rows, wide), BF16),
            jax.ShapeDtypeStruct((dist_count, wide), BF16),
            jax.ShapeDtypeStruct((8, wide), F32),
        ],
        compiler_params=vmem,
    )(
        place, *branch_pieces, wo_pieces[0], probs, attn_f, q_raw, k_aug, v_all, rel_heads,
        biases, embeds, query_seg,
    )

    got = exchange([grads[i] for i in range(blocks)])
    k_at, v_at = both, both + mem_rows + rows
    end = both + 2 * (mem_rows + rows)
    grad_streams = grad_resid_one
    grad_rows = 0.0
    for i in range(blocks):
        wq_i, wk_i, wv_i = (column_slice(w, block_id ^ i) for w in (w_q, w_k, w_v))
        grad_streams = grad_streams + dot_nt(got[i][:both], wq_i)
        grad_rows = (
            grad_rows + dot_nt(got[i][k_at:v_at], wk_i) + dot_nt(got[i][v_at:end], wv_i)
        )
    h_grad = grad_streams[:rows] + grad_rows[mem_rows:]
    g_grad = grad_streams[rows:]
    memory_grad = grad_rows[:mem_rows]

    grad_w_q = sum(dot_tn(x_pieces[i][mem_rows:], grads[i, :both]) for i in range(blocks))
    grad_w_k = sum(
        dot_tn(x_pieces[i][: mem_rows + rows], grads[i, k_at:v_at]) for i in range(blocks)
    )
    grad_w_v = sum(
        dot_tn(x_pieces[i][: mem_rows + rows], grads[i, v_at:end]) for i in range(blocks)
    )
    grad_w_r = dot_tn(pos_table, rel_grad)
    head_grads = jnp.stack([grad_w_q, grad_w_k, grad_w_v, grad_w_r], axis=1)
    head_grads = head_grads.reshape(groups, width // groups, 4, wide)
    head_sum = reduce_groups(head_grads, first_order)

    def to_rows(values):
        cut = values.astype(BF16).reshape((blocks, -1) + values.shape[1:])
        pieces = [
            lax.dynamic_index_in_dim(cut, block_id ^ i, 0, keepdims=False) for i in range(blocks)
        ]
        return in_order(exchange(pieces)).astype(F32)

    w_1_rows = to_rows(w_1_sum)
    w_1_flat = (
        w_1_rows.reshape(blocks, -1, groups, part).transpose(1, 2, 0, 3).reshape(-1)
    )
    head_rows = to_rows(head_sum)
    head_flat = head_rows.transpose(2, 1, 0, 3).reshape(4, -1)

    def sum_over(values, axis):
        for step in bits_of(lax.axis_size(axis)):
            values = values + swap(values, axis, step)
        return values

    early = [grad_ln1_gain, grad_ln1_bias, grad_b_1, grad_b_2, grad_ln2_gain, grad_ln2_bias]
    early_sum = sum_over(sum_over(jnp.concatenate(early + [stat_terms]), "blk"), "dp")
    ends = []
    at = 0
    for one in early:
        ends.append(early_sum[at : at + one.shape[0]])
        at += one.shape[0]
    totals = early_sum[at:]
    late = in_order(gather(sum_over(head_small, "dp")))
    late = late.transpose(1, 0, 2).reshape(8, blocks * wide)
    denoms = jnp.stack([totals[6], totals[6], totals[6], totals[7], totals[7], totals[7]])
    rms_stats = jnp.sqrt(totals[:6] / (denoms * width))
    return (
        out_two[None, :rows].astype(BF16),
        out_two[None, rows:].astype(BF16),
        h_grad[None],
        g_grad[None],
        memory_grad[None],
        head_flat[0],
        head_flat[1],
        head_flat[2],
        head_flat[3],
        w_o_flat,
        w_1_flat,
        w_2_sum.reshape(-1),
        late[0],
        late[1],
        late[2],
        late[3:5],
        ends[0],
        ends[1],
        ends[2],
        ends[3],
        ends[4],
        ends[5],
        rms_stats,
    )


def solution(mesh):
    rows = P("dp", "blk", None)
    ints = P("dp", "blk")
    flat = P(("dp", "blk"))
    return jax.shard_map(
        local,
        mesh=mesh,
        in_specs=(rows,) * 5 + (ints,) * 3 + (P("dp"),) + (P(),) * 17,
        out_specs=(rows,) * 5 + (flat,) * 7 + (P(),) * 11,
        check_vma=False,
    )
```

```python
import functools
import math

import jax
import jax.numpy as jnp
import numpy as np
from jax import lax
from jax.experimental import pallas as pl
from jax.experimental.pallas import tpu as pltpu
from jax.sharding import PartitionSpec as P

HEADS = 12
HEAD_DIM = 64
EPSILON = 1e-12
NEGATIVE = -1e30
SCALE = 1.0 / math.sqrt(HEAD_DIM)
F32 = jnp.float32
BF16 = jnp.bfloat16
MESH_IDS = pl.DeviceIdType.MESH


def layer_norm(hidden, norm_gain, norm_bias):
    center = hidden - jnp.mean(hidden, axis=-1, keepdims=True)
    spread = jnp.mean(center * center, axis=-1, keepdims=True)
    return center * lax.rsqrt(spread + EPSILON) * norm_gain + norm_bias


def gelu_tanh(values):
    return jax.nn.gelu(values, approximate=True)


def position_units(top, dist_count, model_width, unit):
    freq = np.exp(np.arange(model_width // 2) * (-2.0 * math.log(10000.0) / model_width))
    coarse = (top - unit * np.arange(dist_count // unit))[:, None] * freq[None, :]
    fine = np.arange(unit)[:, None] * freq[None, :]
    return tuple(
        np.stack([np.sin(angle), np.cos(angle)]).astype(np.float32) for angle in (coarse, fine)
    )


def dot_nn(left, right):
    return lax.dot_general(left, right, (((1,), (0,)), ((), ())), preferred_element_type=F32)


def dot_nt(left, right):
    return lax.dot_general(left, right, (((1,), (1,)), ((), ())), preferred_element_type=F32)


def dot_tn(left, right):
    return lax.dot_general(left, right, (((0,), (0,)), ((), ())), preferred_element_type=F32)


def swap(values, axis, step):
    count = lax.axis_size(axis)
    return lax.ppermute(values, axis, [(i, i ^ step) for i in range(count)])


def bits_of(count):
    return [1 << k for k in range(count.bit_length() - 1)]


def seg_columns(q_seg, embed):
    return (
        jnp.sum(q_seg * embed[0:1], axis=1, keepdims=True),
        jnp.sum(q_seg * embed[1:2], axis=1, keepdims=True),
    )


def flip(index, step):
    for bit in (1 << k for k in range(step.bit_length())):
        if step & bit:
            index = index + bit - 2 * bit * ((index // bit) % 2)
    return index


def mix(index, other, blocks):
    total = 0
    for bit in bits_of(blocks):
        left = (index // bit) % 2
        right = (other // bit) % 2
        total = total + bit * (left + right - 2 * left * right)
    return total


def attn_fwd_kernel(
    heads,
    rows,
    mem_rows,
    blocks,
    mem_ref,
    h_ref,
    g_ref,
    info_ref,
    flag_ref,
    wq_ref,
    wk_ref,
    wv_ref,
    wr_ref,
    bias_in_ref,
    coarse_ref,
    fine_ref,
    prob_ref,
    af_ref,
    q_ref,
    k_ref,
    v_ref,
    rel_ref,
    got_ref,
    out_ref,
    x_ref,
    pos_ref,
    info_out_ref,
    bias_ref,
    w_buf,
    wr_buf,
    mask_ref,
    info_buf,
    x_buf,
    got_buf,
    key_order_ref,
    col_ref,
    x_send,
    x_recv,
    info_send,
    info_recv,
    out_send,
    out_recv,
    own_sem,
):
    step = pl.program_id(0)
    piece = blocks - 1 - step
    block_id = lax.axis_index("blk")
    group_id = lax.axis_index("dp")
    wide = heads * HEAD_DIM
    width = mem_ref.shape[1]
    mem_all = mem_rows * blocks
    keys = k_ref.shape[1]
    span = rows + keys
    steps = bits_of(blocks)
    sources = (mem_ref, h_ref, g_ref)
    spots = (
        pl.ds(0, mem_rows),
        pl.ds(mem_rows, rows),
        pl.ds(mem_rows + rows, rows),
    )

    def device(i):
        return (group_id, flip(block_id, i))

    def x_copy(hop, part, come):
        where = x_buf.at[flip(block_id, come), spots[part]]
        return pltpu.make_async_remote_copy(
            src_ref=sources[part] if come == 0 else where,
            dst_ref=where,
            send_sem=x_send.at[come + hop, part],
            recv_sem=x_recv.at[come + hop, part],
            device_id=device(hop),
            device_id_type=MESH_IDS,
        )

    def info_copy(i):
        return pltpu.make_async_remote_copy(
            src_ref=info_ref,
            dst_ref=info_buf.at[block_id],
            send_sem=info_send.at[i],
            recv_sem=info_recv.at[i],
            device_id=device(i),
            device_id_type=MESH_IDS,
        )

    def own_copy(part):
        return pltpu.make_async_copy(
            sources[part], x_buf.at[block_id, spots[part]], own_sem.at[part]
        )

    def out_copy(i):
        return pltpu.make_async_remote_copy(
            src_ref=out_ref.at[i],
            dst_ref=got_buf.at[i],
            send_sem=out_send.at[i],
            recv_sem=out_recv.at[i],
            device_id=device(i),
            device_id_type=MESH_IDS,
        )

    @pl.when(step == 0)
    def _():
        barrier = pltpu.get_barrier_semaphore()
        for i in range(1, blocks):
            pl.semaphore_signal(barrier, inc=1, device_id=device(i), device_id_type=MESH_IDS)
        pl.semaphore_wait(barrier, blocks - 1)
        for part in range(3):
            x_copy(steps[-1], part, 0).start()
        for i in range(1, blocks):
            info_copy(i).start()
        for hop in steps[:-1]:
            for part in range(3):
                x_copy(hop, part, 0).start()
        own_info = pltpu.make_async_copy(info_ref, info_buf.at[block_id], own_sem.at[3])
        own_info.start()
        for part in range(3):
            own_copy(part).start()
        for block in range(blocks):

            @pl.when(block_id == block)
            def _(block=block):
                at = slice(block * wide, (block + 1) * wide)
                w_buf[:, :wide] = wq_ref[:, at]
                w_buf[:, wide : 2 * wide] = wk_ref[:, at]
                w_buf[:, 2 * wide :] = wv_ref[:, at]
                wr_buf[...] = wr_ref[:, at]
                bias_ref[...] = bias_in_ref[:, at]

        dist_count = pos_ref.shape[0]
        half = width // 2
        fine_sin, fine_cos = fine_ref[0], fine_ref[1]
        unit = fine_ref.shape[1]

        def fill(a, carry):
            at = pl.ds(pl.multiple_of(a * unit, unit), unit)
            big_sin, big_cos = coarse_ref[0, pl.ds(a, 1), :], coarse_ref[1, pl.ds(a, 1), :]
            pos_ref[at, :half] = (big_sin * fine_cos - big_cos * fine_sin).astype(BF16)
            pos_ref[at, half:] = (big_cos * fine_cos + big_sin * fine_sin).astype(BF16)
            return carry

        lax.fori_loop(0, dist_count // unit, fill, 0)
        rel = dot_nn(pos_ref[...], wr_buf[...]).astype(BF16)
        for h in range(heads):
            rel_ref[h] = rel[:, h * HEAD_DIM : (h + 1) * HEAD_DIM]
        own_info.wait()
        for part in range(3):
            own_copy(part).wait()

        def project(i):
            owner = flip(block_id, i)
            mem_at = pl.ds(pl.multiple_of(owner * mem_rows, 32), mem_rows)
            tok_at = pl.ds(pl.multiple_of(mem_all + owner * rows, 32), rows)
            qkv = dot_nn(x_buf[owner], w_buf[...])
            q_ref[i] = qkv[mem_rows:, :wide]
            low = qkv[: mem_rows + rows, wide:].astype(BF16)
            for h in range(heads):
                k_part = low[:, h * HEAD_DIM : (h + 1) * HEAD_DIM]
                v_part = low[:, wide + h * HEAD_DIM : wide + (h + 1) * HEAD_DIM]
                k_ref[h, mem_at, :HEAD_DIM] = k_part[:mem_rows]
                k_ref[h, tok_at, :HEAD_DIM] = k_part[mem_rows:]
                v_ref[h, mem_at, :] = v_part[:mem_rows]
                v_ref[h, tok_at, :] = v_part[mem_rows:]

        project(0)
        have = [0]
        for at, hop in enumerate(steps):
            fresh = [i + hop for i in have]
            for come in fresh:
                for part in range(3):
                    x_copy(come, part, 0).wait_recv() if come in steps else x_copy(
                        hop, part, come - hop
                    ).wait_recv()
                    if hop == steps[-1] and come == hop:
                        for near in steps[:-1]:
                            x_copy(near, part, come).start()
                project(come)
            have = have + fresh
        for i in range(1, blocks):
            info_copy(i).wait()
        for part in range(3):
            for hop in steps:
                x_copy(hop, part, 0).wait_send()
            for near in steps[:-1]:
                x_copy(near, part, steps[-1]).wait_send()

        key_order_ref[:, :mem_all] = jnp.full((8, mem_all), -2, jnp.int32) + jnp.where(
            flag_ref[...] > 0, 0, 1 << 30
        )
        for block in range(blocks):
            at = slice(mem_all + block * rows, mem_all + (block + 1) * rows)
            key_order_ref[:, at] = info_buf[block]
            col_ref[pl.ds(block * rows, rows), :] = info_buf[block].astype(F32).T
        info_out_ref[...] = col_ref[...]
        lane = lax.broadcasted_iota(jnp.int32, (mem_all, HEAD_DIM), 1)
        mem_extra = jnp.where(lane < 2, 1.0, 0.0).astype(BF16)
        lane = lax.broadcasted_iota(jnp.int32, (keys - mem_all, HEAD_DIM), 1)
        tok_extra = jnp.where(
            lane < 2, 1.0, jnp.where(lane < 4, col_ref[:, 1:2], 0.0)
        ).astype(BF16)
        for h in range(heads):
            k_ref[h, :mem_all, HEAD_DIM:] = mem_extra
            k_ref[h, mem_all:, HEAD_DIM:] = tok_extra
        x_ref[...] = x_buf[...]

    owner = mix(block_id, piece, blocks)
    tok_at = pl.ds(pl.multiple_of(owner * rows, 32), rows)
    info = col_ref[tok_at, :]
    visible = key_order_ref[0:1, :].astype(F32) <= info[:, 0:1]
    key_at = lax.broadcasted_iota(jnp.int32, (rows, keys), 1) - mem_all - owner * rows
    other = key_at != lax.broadcasted_iota(jnp.int32, (rows, keys), 0)
    mask_ref[:rows, :] = jnp.where(visible, 0.0, NEGATIVE)
    mask_ref[rows:, :] = jnp.where(visible & other, 0.0, NEGATIVE)
    seg = jnp.concatenate([info[:, 1:2], info[:, 1:2]], axis=0)
    rel_at = pl.ds(pl.multiple_of((blocks - 1) * rows - owner * rows, 32), span)
    lane = lax.broadcasted_iota(jnp.int32, (2 * rows, HEAD_DIM), 1)
    for h in range(heads):
        own = slice(h * HEAD_DIM, (h + 1) * HEAD_DIM)
        raw = q_ref[piece, :, own]
        q_word = ((raw + bias_ref[0:1, own]).astype(BF16) * SCALE).astype(BF16)
        q_rel = ((raw + bias_ref[1:2, own]).astype(BF16) * SCALE).astype(BF16)
        same, differ = seg_columns((raw + bias_ref[2:3, own]) * SCALE, bias_ref[3:5, own])
        gap = differ - same
        base = same + gap * seg
        slope = gap * (1.0 - 2.0 * seg)
        base_high = base.astype(BF16).astype(F32)
        slope_high = slope.astype(BF16).astype(F32)
        extra = jnp.where(
            lane == 0,
            base_high,
            jnp.where(
                lane == 1,
                base - base_high,
                jnp.where(lane == 2, slope_high, jnp.where(lane == 3, slope - slope_high, 0.0)),
            ),
        ).astype(BF16)
        q_aug = jnp.concatenate([q_word, extra], axis=1)
        rel = dot_nt(q_rel, rel_ref[h, rel_at, :])
        shift = span - (rows - 1)
        rel = jnp.concatenate(
            [
                pltpu.roll(rel[:rows], shift, 1, stride=1, stride_axis=0)[:, :keys],
                pltpu.roll(rel[rows:], shift, 1, stride=1, stride_axis=0)[:, :keys],
            ],
            axis=0,
        )
        scores = dot_nt(q_aug, k_ref[h]) + rel + mask_ref[...]
        weight = jnp.exp(scores - jnp.max(scores, axis=1, keepdims=True))
        probs = (weight * (1.0 / jnp.sum(weight, axis=1, keepdims=True))).astype(BF16)
        prob_ref[h, 0] = probs
        attn_f = dot_nn(probs, v_ref[h])
        af_ref[0, :, own] = attn_f
        out_ref[piece, :, own] = attn_f.astype(BF16)

    for i in range(1, blocks):

        @pl.when(piece == i)
        def _(i=i):
            out_copy(i).start()

    @pl.when(step == blocks - 1)
    def _():
        got_ref[0] = out_ref[0]
        for i in range(1, blocks):
            out_copy(i).wait()
            got_ref[i] = got_buf[i]


def flip_eights(values):
    index = 7 - lax.broadcasted_iota(jnp.int32, (8, values.shape[1]), 0)
    return jnp.take_along_axis(values, index, axis=0)


def spread_rows(values, rows, keys):
    span = rows + keys
    padded = jnp.concatenate([values, jnp.zeros((rows, rows), F32)], axis=1)
    groups = []
    for a in range(rows // 8):
        group = flip_eights(padded[8 * a : 8 * a + 8])
        group = pltpu.roll(group, (rows - 8 - 8 * a) % span, 1, stride=1, stride_axis=0)
        groups.append(flip_eights(group))
    return jnp.concatenate(groups, axis=0)


def attn_bwd_kernel(heads, rows, mem_rows, blocks, place_ref, *refs):
    gb_refs = refs[:blocks]
    (
        wo_ref,
        prob_ref,
        af_ref,
        q_ref,
        k_ref,
        v_ref,
        rel_ref,
        bias_ref,
        embed_ref,
        query_seg_ref,
        grads_ref,
        rel_grad_ref,
        small_ref,
        ga_ref,
        kt_ref,
        vt_ref,
        rt_ref,
    ) = refs[blocks:]
    piece = pl.program_id(0)
    block_id = place_ref[0]
    mem_all = mem_rows * blocks
    keys = k_ref.shape[1]
    span = rows + keys

    @pl.when(piece == 0)
    def _():
        for i in range(blocks):
            ga_ref[i] = dot_nt(gb_refs[i][...], wo_ref[...]).astype(BF16)
        kt_ref[...] = jnp.zeros_like(kt_ref)
        vt_ref[...] = jnp.zeros_like(vt_ref)
        rt_ref[...] = jnp.zeros_like(rt_ref)
        small_ref[...] = jnp.zeros_like(small_ref)

    owner = block_id ^ piece
    tok_at = pl.ds(pl.multiple_of(owner * rows, 32), rows)
    rel_start = pl.multiple_of((blocks - 1) * rows - owner * rows, 128)
    rel_at = pl.ds(rel_start, span)
    seg = query_seg_ref[tok_at, :]
    seg = jnp.concatenate([seg, seg], axis=0)
    for h in range(heads):
        own = slice(h * HEAD_DIM, (h + 1) * HEAD_DIM)
        raw = q_ref[piece, :, own]
        q_word = (raw + bias_ref[0:1, own]).astype(BF16)
        q_rel = (raw + bias_ref[1:2, own]).astype(BF16)
        q_seg = raw + bias_ref[2:3, own]
        embed = embed_ref[:, own]
        ga = ga_ref[piece, :, own]
        probs = prob_ref[h, 0]
        ga_f = ga.astype(F32) * SCALE
        row_dot = jnp.sum(ga_f * af_ref[0, :, own], axis=1, keepdims=True)
        grad_prob = dot_nt(ga_f.astype(BF16), v_ref[h])
        grad_score = probs.astype(F32) * (grad_prob - row_dot)
        grad_low = grad_score.astype(BF16)
        wide_word = dot_nn(grad_low, k_ref[h])
        grad_word = wide_word[:, :HEAD_DIM]
        total = wide_word[:, HEAD_DIM : HEAD_DIM + 1]
        ones = wide_word[:, HEAD_DIM + 2 : HEAD_DIM + 3]
        differ = ones + seg * (total - 2.0 * ones)
        same = total - differ
        grad_seg = same * embed[0:1] + differ * embed[1:2]
        spread = jnp.concatenate(
            [
                spread_rows(grad_score[:rows], rows, keys),
                spread_rows(grad_score[rows:], rows, keys),
            ],
            axis=0,
        ).astype(BF16)
        grad_rel = dot_nn(spread, rel_ref[h, rel_at, :])
        kt_ref[h] += dot_tn(q_word, grad_low)
        vt_ref[h] += dot_tn(ga, probs)
        rt_ref[h, :, pl.ds(rel_start, span)] += dot_tn(q_rel, spread)
        grads_ref[piece, : 2 * rows, own] = (grad_word + grad_rel + grad_seg).astype(BF16)
        small_ref[:, own] += jnp.concatenate(
            [
                jnp.sum(grad_word, axis=0, keepdims=True),
                jnp.sum(grad_rel, axis=0, keepdims=True),
                jnp.sum(grad_seg, axis=0, keepdims=True),
                jnp.sum(same * q_seg, axis=0, keepdims=True),
                jnp.sum(differ * q_seg, axis=0, keepdims=True),
                jnp.zeros((3, HEAD_DIM), F32),
            ],
            axis=0,
        )

    @pl.when(piece == blocks - 1)
    def _():
        for h in range(heads):
            own = slice(h * HEAD_DIM, (h + 1) * HEAD_DIM)
            rel_grad_ref[:, own] = rt_ref[h].T.astype(BF16)
            for base, acc in ((2 * rows, kt_ref), (3 * rows + mem_rows, vt_ref)):
                full = acc[h].T.astype(BF16)
                for i in range(blocks):
                    home = i ^ block_id
                    grads_ref[home, base : base + mem_rows, own] = full[
                        i * mem_rows : (i + 1) * mem_rows
                    ]
                    grads_ref[home, base + mem_rows : base + mem_rows + rows, own] = full[
                        mem_all + i * rows : mem_all + (i + 1) * rows
                    ]


def whole(shape):
    return pl.BlockSpec(shape, lambda *_: (0,) * len(shape))


def local(
    h_in,
    g_in,
    memory,
    cot_h,
    cot_g,
    perm_order,
    target,
    segment,
    mem_flag,
    w_q,
    w_k,
    w_v,
    w_r,
    w_o,
    r_w_bias,
    r_r_bias,
    r_s_bias,
    seg_embed,
    ln1_gain,
    ln1_bias,
    w_1,
    b_1,
    w_2,
    b_2,
    ln2_gain,
    ln2_bias,
):
    _, rows, width = h_in.shape
    mem_rows = memory.shape[1]
    hidden = w_1.shape[1]
    blocks = lax.axis_size("blk")
    groups = lax.axis_size("dp")
    block_id = lax.axis_index("blk")
    group_id = lax.axis_index("dp")
    tok_all = rows * blocks
    mem_all = mem_rows * blocks
    keys = mem_all + tok_all
    dist_count = tok_all + keys
    heads = HEADS // blocks
    wide = heads * HEAD_DIM
    both = 2 * rows
    chunk = mem_rows + 2 * rows
    share = groups * blocks
    place = block_id.astype(jnp.int32).reshape(1)

    def gather(values):
        pieces = [values]
        for step in bits_of(blocks):
            pieces = pieces + [swap(one, "blk", step) for one in pieces]
        return pieces

    def in_order(pieces):
        stacked = jnp.stack(pieces)
        return jnp.stack(
            [lax.dynamic_index_in_dim(stacked, block_id ^ i, 0, keepdims=False) for i in range(blocks)]
        )

    def column_slice(weight, index):
        return lax.dynamic_slice_in_dim(weight, index * wide, wide, axis=1)

    order_own = jnp.where(target > 0, perm_order, -1)
    info_own = jnp.concatenate([order_own, segment, jnp.zeros((6, rows), jnp.int32)], axis=0)
    flags = jnp.broadcast_to(mem_flag.reshape(1, 1), (8, mem_all))
    bias_rows = jnp.concatenate(
        [r_w_bias[None], r_r_bias[None], r_s_bias[None], seg_embed, jnp.zeros((3, width), F32)]
    )
    coarse, fine = position_units(keys - 1, dist_count, width, 32)
    wo_pieces = [
        lax.dynamic_slice_in_dim(w_o, (block_id ^ i) * wide, wide, axis=0) for i in range(blocks)
    ]
    hbm = pl.BlockSpec(memory_space=pl.ANY)
    (
        probs, attn_f, q_raw, k_aug, v_all, rel_heads, got_out, attn_out, x_all, pos_table,
        query_info, biases,
    ) = pl.pallas_call(
        functools.partial(attn_fwd_kernel, heads, rows, mem_rows, blocks),
        name="attn_fwd",
        grid=(blocks,),
        in_specs=[hbm] * 4
        + [whole((8, mem_all))]
        + [whole((width, width))] * 4
        + [whole((8, width)), whole(coarse.shape), whole(fine.shape)],
        out_specs=[
            pl.BlockSpec((heads, 1, both, keys), lambda s: (0, blocks - 1 - s, 0, 0)),
            pl.BlockSpec((1, both, wide), lambda s: (blocks - 1 - s, 0, 0)),
            whole((blocks, both, wide)),
            whole((heads, keys, 2 * HEAD_DIM)),
            whole((heads, keys, HEAD_DIM)),
            whole((heads, dist_count, HEAD_DIM)),
            whole((blocks, both, wide)),
            whole((blocks, both, wide)),
            whole((blocks, chunk, width)),
            whole((dist_count, width)),
            whole((tok_all, 8)),
            whole((8, wide)),
        ],
        out_shape=[
            jax.ShapeDtypeStruct((heads, blocks, both, keys), BF16),
            jax.ShapeDtypeStruct((blocks, both, wide), F32),
            jax.ShapeDtypeStruct((blocks, both, wide), F32),
            jax.ShapeDtypeStruct((heads, keys, 2 * HEAD_DIM), BF16),
            jax.ShapeDtypeStruct((heads, keys, HEAD_DIM), BF16),
            jax.ShapeDtypeStruct((heads, dist_count, HEAD_DIM), BF16),
            jax.ShapeDtypeStruct((blocks, both, wide), BF16),
            jax.ShapeDtypeStruct((blocks, both, wide), BF16),
            jax.ShapeDtypeStruct((blocks, chunk, width), BF16),
            jax.ShapeDtypeStruct((dist_count, width), BF16),
            jax.ShapeDtypeStruct((tok_all, 8), F32),
            jax.ShapeDtypeStruct((8, wide), F32),
        ],
        scratch_shapes=[
            pltpu.VMEM((width, 3 * wide), BF16),
            pltpu.VMEM((width, wide), BF16),
            pltpu.VMEM((both, keys), F32),
            pltpu.VMEM((blocks, 8, rows), jnp.int32),
            pltpu.VMEM((blocks, chunk, width), BF16),
            pltpu.VMEM((blocks, both, wide), BF16),
            pltpu.VMEM((8, keys), jnp.int32),
            pltpu.VMEM((tok_all, 8), F32),
            pltpu.SemaphoreType.DMA((blocks, 3)),
            pltpu.SemaphoreType.DMA((blocks, 3)),
            pltpu.SemaphoreType.DMA((blocks,)),
            pltpu.SemaphoreType.DMA((blocks,)),
            pltpu.SemaphoreType.DMA((blocks,)),
            pltpu.SemaphoreType.DMA((blocks,)),
            pltpu.SemaphoreType.DMA((4,)),
        ],
        compiler_params=pltpu.CompilerParams(
            vmem_limit_bytes=60 << 20, collective_id=0, has_side_effects=True
        ),
    )(
        memory[0], h_in[0], g_in[0], info_own, flags, w_q, w_k, w_v, w_r, bias_rows, coarse, fine
    )
    x_pieces = [
        lax.dynamic_index_in_dim(x_all, block_id ^ i, 0, keepdims=False) for i in range(blocks)
    ]
    embeds = biases[3:5]
    query_seg = query_info[:, 1:2]
    vmem = pltpu.CompilerParams(vmem_limit_bytes=60 << 20)

    def exchange(pieces):
        return [pieces[0]] + [swap(pieces[i], "blk", i) for i in range(1, blocks)]

    branch_att = sum(dot_nn(got_out[i], wo_pieces[i]) for i in range(blocks))
    streams = jnp.concatenate([h_in[0], g_in[0]], axis=0)
    resid_one = branch_att + streams.astype(F32)
    out_one = layer_norm(resid_one, ln1_gain, ln1_bias)
    ffn_in = out_one.astype(BF16)
    ffn_pieces = gather(ffn_in)
    pre_act = dot_nn(ffn_in, w_1) + b_1
    activation = gelu_tanh(pre_act).astype(BF16)
    branch_ffn = dot_nn(activation, w_2) + b_2
    resid_two = branch_ffn + out_one
    out_two = layer_norm(resid_two, ln2_gain, ln2_bias)
    target_f = target[0].astype(F32)[:, None]
    stat_weight = jnp.concatenate([jnp.ones((rows, 1), F32), target_f], axis=0)

    def stats_of(values):
        weighted = jnp.sum(values * values, axis=1, keepdims=True) * stat_weight
        return jnp.sum(weighted[:rows]), jnp.sum(weighted[rows:])

    att_stat, ffn_stat, out_stat = stats_of(branch_att), stats_of(branch_ffn), stats_of(out_two)
    stat_terms = jnp.stack(
        [
            att_stat[0],
            ffn_stat[0],
            out_stat[0],
            att_stat[1],
            ffn_stat[1],
            out_stat[1],
            jnp.asarray(rows, F32),
            jnp.sum(target_f),
        ]
    )
    cot = jnp.concatenate([cot_h[0], cot_g[0]], axis=0).astype(F32)
    grad_resid_two, grad_ln2_gain, grad_ln2_bias = jax.vjp(
        layer_norm, resid_two, ln2_gain, ln2_bias
    )[1](cot)
    grad_ffn = grad_resid_two.astype(BF16)
    grad_ffn_pieces = gather(grad_ffn)
    grad_b_2 = jnp.sum(grad_ffn.astype(F32), axis=0)
    grad_act = dot_nt(grad_ffn, w_2)
    grad_pre = jax.vjp(gelu_tanh, pre_act)[1](grad_act)[0].astype(BF16)
    grad_b_1 = jnp.sum(grad_pre.astype(F32), axis=0)
    grad_out_one = grad_resid_two + dot_nt(grad_pre, w_1)
    grad_resid_one, grad_ln1_gain, grad_ln1_bias = jax.vjp(
        layer_norm, resid_one, ln1_gain, ln1_bias
    )[1](grad_out_one)
    grad_branch = grad_resid_one.astype(BF16)
    branch_pieces = gather(grad_branch)

    part = hidden // share
    w_1_own = lax.dynamic_index_in_dim(
        w_1.reshape(width, groups, blocks, part), block_id, 2, keepdims=False
    ).reshape(width, groups * part)
    b_1_own = lax.dynamic_index_in_dim(
        b_1.reshape(groups, blocks, part), block_id, 1, keepdims=False
    ).reshape(groups * part)
    w_2_own = lax.dynamic_index_in_dim(
        w_2.reshape(groups, blocks, part, width), block_id, 1, keepdims=False
    ).reshape(groups * part, width)
    ffn_all = jnp.concatenate(ffn_pieces, axis=0)
    grad_ffn_all = jnp.concatenate(grad_ffn_pieces, axis=0)
    pre_slice = dot_nn(ffn_all, w_1_own) + b_1_own
    act_slice = gelu_tanh(pre_slice).astype(BF16)
    grad_act_slice = dot_nt(grad_ffn_all, w_2_own)
    grad_pre_slice = jax.vjp(gelu_tanh, pre_slice)[1](grad_act_slice)[0].astype(BF16)
    grad_w_1 = dot_tn(ffn_all, grad_pre_slice)
    grad_w_2 = dot_tn(act_slice, grad_ffn_all)

    def reduce_groups(values, steps):
        tail = values.shape[1:]
        held = values
        done = 0
        names = list(bits_of(groups))
        left = [s for s in reversed(names)]
        for step in steps:
            at = left.index(step)
            shaped = held.reshape((1 << at, 2, -1) + tail)
            mine = (group_id // step) % 2
            keep = lax.dynamic_index_in_dim(shaped, mine, 1, keepdims=False)
            give = lax.dynamic_index_in_dim(shaped, 1 - mine, 1, keepdims=False).astype(BF16)
            got = swap(give, "dp", step)
            held = keep.astype(F32) + got.astype(F32)
            left.pop(at)
            done += 1
        return held.reshape(tail)

    steps = bits_of(groups)
    first_order = steps
    second_order = [steps[1], steps[0]] + steps[2:]
    w_2_sum = reduce_groups(grad_w_2.reshape(groups, part, width), second_order)
    w_1_sum = reduce_groups(
        grad_w_1.reshape(groups, width // groups, groups * part), first_order
    )
    grad_w_o = sum(dot_tn(attn_out[i], branch_pieces[i]) for i in range(blocks))
    w_o_sum = reduce_groups(grad_w_o.reshape(groups, wide // groups, width), second_order)
    w_o_flat = lax.ppermute(
        w_o_sum,
        ("dp", "blk"),
        [(d * blocks + k, groups * k + d) for d in range(groups) for k in range(blocks)],
    ).reshape(-1)

    grads, rel_grad, head_small = pl.pallas_call(
        functools.partial(attn_bwd_kernel, heads, rows, mem_rows, blocks),
        name="attn_bwd",
        grid_spec=pltpu.PrefetchScalarGridSpec(
            num_scalar_prefetch=1,
            grid=(blocks,),
            in_specs=[whole((both, width))] * blocks
            + [
                whole((wide, width)),
                pl.BlockSpec((heads, 1, both, keys), lambda p, _: (0, p, 0, 0)),
                pl.BlockSpec((1, both, wide), lambda p, _: (p, 0, 0)),
                whole((blocks, both, wide)),
                whole((heads, keys, 2 * HEAD_DIM)),
                whole((heads, keys, HEAD_DIM)),
                whole((heads, dist_count, HEAD_DIM)),
                whole((8, wide)),
                whole((2, wide)),
                whole((tok_all, 1)),
            ],
            out_specs=[
                whole((blocks, 4 * rows + 2 * mem_rows, wide)),
                whole((dist_count, wide)),
                whole((8, wide)),
            ],
            scratch_shapes=[
                pltpu.VMEM((blocks, both, wide), BF16),
                pltpu.VMEM((heads, HEAD_DIM, keys), F32),
                pltpu.VMEM((heads, HEAD_DIM, keys), F32),
                pltpu.VMEM((heads, HEAD_DIM, dist_count), F32),
            ],
        ),
        out_shape=[
            jax.ShapeDtypeStruct((blocks, 4 * rows + 2 * mem_rows, wide), BF16),
            jax.ShapeDtypeStruct((dist_count, wide), BF16),
            jax.ShapeDtypeStruct((8, wide), F32),
        ],
        compiler_params=vmem,
    )(
        place, *branch_pieces, wo_pieces[0], probs, attn_f, q_raw, k_aug, v_all, rel_heads,
        biases, embeds, query_seg,
    )

    got = exchange([grads[i] for i in range(blocks)])
    k_at, v_at = both, both + mem_rows + rows
    end = both + 2 * (mem_rows + rows)
    grad_streams = grad_resid_one
    grad_rows = 0.0
    for i in range(blocks):
        wq_i, wk_i, wv_i = (column_slice(w, block_id ^ i) for w in (w_q, w_k, w_v))
        grad_streams = grad_streams + dot_nt(got[i][:both], wq_i)
        grad_rows = (
            grad_rows + dot_nt(got[i][k_at:v_at], wk_i) + dot_nt(got[i][v_at:end], wv_i)
        )
    h_grad = grad_streams[:rows] + grad_rows[mem_rows:]
    g_grad = grad_streams[rows:]
    memory_grad = grad_rows[:mem_rows]

    grad_w_q = sum(dot_tn(x_pieces[i][mem_rows:], grads[i, :both]) for i in range(blocks))
    grad_w_k = sum(
        dot_tn(x_pieces[i][: mem_rows + rows], grads[i, k_at:v_at]) for i in range(blocks)
    )
    grad_w_v = sum(
        dot_tn(x_pieces[i][: mem_rows + rows], grads[i, v_at:end]) for i in range(blocks)
    )
    grad_w_r = dot_tn(pos_table, rel_grad)
    head_grads = jnp.stack([grad_w_q, grad_w_k, grad_w_v, grad_w_r], axis=1)
    head_grads = head_grads.reshape(groups, width // groups, 4, wide)
    head_sum = reduce_groups(head_grads, first_order)

    def to_rows(values):
        cut = values.astype(BF16).reshape((blocks, -1) + values.shape[1:])
        pieces = [
            lax.dynamic_index_in_dim(cut, block_id ^ i, 0, keepdims=False) for i in range(blocks)
        ]
        return in_order(exchange(pieces)).astype(F32)

    w_1_rows = to_rows(w_1_sum)
    w_1_flat = (
        w_1_rows.reshape(blocks, -1, groups, part).transpose(1, 2, 0, 3).reshape(-1)
    )
    head_rows = to_rows(head_sum)
    head_flat = head_rows.transpose(2, 1, 0, 3).reshape(4, -1)

    def sum_over(values, axis):
        for step in bits_of(lax.axis_size(axis)):
            values = values + swap(values, axis, step)
        return values

    early = [grad_ln1_gain, grad_ln1_bias, grad_b_1, grad_b_2, grad_ln2_gain, grad_ln2_bias]
    early_sum = sum_over(sum_over(jnp.concatenate(early + [stat_terms]), "blk"), "dp")
    ends = []
    at = 0
    for one in early:
        ends.append(early_sum[at : at + one.shape[0]])
        at += one.shape[0]
    totals = early_sum[at:]
    late = in_order(gather(sum_over(head_small, "dp")))
    late = late.transpose(1, 0, 2).reshape(8, blocks * wide)
    denoms = jnp.stack([totals[6], totals[6], totals[6], totals[7], totals[7], totals[7]])
    rms_stats = jnp.sqrt(totals[:6] / (denoms * width))
    return (
        out_two[None, :rows].astype(BF16),
        out_two[None, rows:].astype(BF16),
        h_grad[None],
        g_grad[None],
        memory_grad[None],
        head_flat[0],
        head_flat[1],
        head_flat[2],
        head_flat[3],
        w_o_flat,
        w_1_flat,
        w_2_sum.reshape(-1),
        late[0],
        late[1],
        late[2],
        late[3:5],
        ends[0],
        ends[1],
        ends[2],
        ends[3],
        ends[4],
        ends[5],
        rms_stats,
    )


def solution(mesh):
    rows = P("dp", "blk", None)
    ints = P("dp", "blk")
    flat = P(("dp", "blk"))
    return jax.shard_map(
        local,
        mesh=mesh,
        in_specs=(rows,) * 5 + (ints,) * 3 + (P("dp"),) + (P(),) * 17,
        out_specs=(rows,) * 5 + (flat,) * 7 + (P(),) * 11,
        check_vma=False,
    )
```

```python
import functools
import math

import jax
import jax.numpy as jnp
import numpy as np
from jax import lax
from jax.experimental import pallas as pl
from jax.experimental.pallas import tpu as pltpu
from jax.sharding import PartitionSpec as P

HEADS = 12
HEAD_DIM = 64
EPSILON = 1e-12
NEGATIVE = -1e30
SCALE = 1.0 / math.sqrt(HEAD_DIM)
F32 = jnp.float32
BF16 = jnp.bfloat16
MESH_IDS = pl.DeviceIdType.MESH


def position_units(top, dist_count, model_width, unit):
    freq = np.exp(np.arange(model_width // 2) * (-2.0 * math.log(10000.0) / model_width))
    coarse = (top - unit * np.arange(dist_count // unit))[:, None] * freq[None, :]
    fine = np.arange(unit)[:, None] * freq[None, :]
    return tuple(
        np.stack([np.sin(angle), np.cos(angle)]).astype(np.float32) for angle in (coarse, fine)
    )


def dot_nn(left, right):
    return lax.dot_general(left, right, (((1,), (0,)), ((), ())), preferred_element_type=F32)


def dot_nt(left, right):
    return lax.dot_general(left, right, (((1,), (1,)), ((), ())), preferred_element_type=F32)


def dot_tn(left, right):
    return lax.dot_general(left, right, (((0,), (0,)), ((), ())), preferred_element_type=F32)


def bits_of(count):
    return [1 << k for k in range(count.bit_length() - 1)]


def seg_columns(q_seg, embed):
    return (
        jnp.sum(q_seg * embed[0:1], axis=1, keepdims=True),
        jnp.sum(q_seg * embed[1:2], axis=1, keepdims=True),
    )


def flip(index, step):
    for bit in (1 << k for k in range(step.bit_length())):
        if step & bit:
            index = index + bit - 2 * bit * ((index // bit) % 2)
    return index


def mix(index, other, blocks):
    total = 0
    for bit in bits_of(blocks):
        left = (index // bit) % 2
        right = (other // bit) % 2
        total = total + bit * (left + right - 2 * left * right)
    return total


def row_of(ref):
    return jnp.concatenate([ref[j : j + 1, :] for j in range(ref.shape[0])], axis=1)


def put_row(ref, at, values):
    for j in range(values.shape[1] // 128):
        ref[at + j : at + j + 1, :] = values[:, 128 * j : 128 * (j + 1)]


def row_mean(values):
    return jnp.mean(values, axis=1, keepdims=True)


def norm_parts(values):
    center = values - row_mean(values)
    rate = lax.rsqrt(row_mean(center * center) + EPSILON)
    return center * rate, rate


def norm_back(unit, rate, scaled):
    return rate * (scaled - row_mean(scaled) - unit * row_mean(scaled * unit))


def gelu_pair(values):
    square = values * values
    inner = math.sqrt(2.0 / math.pi) * values * (1.0 + 0.044715 * square)
    bend = jnp.tanh(inner)
    half = 0.5 * (1.0 + bend)
    slope = half + values * (1.0 - bend * bend) * (
        0.5 * math.sqrt(2.0 / math.pi) * (1.0 + 3 * 0.044715 * square)
    )
    return values * half, slope


def column_sum(values):
    return jnp.sum(values, axis=0, keepdims=True)


def reversed_index(index, count):
    total = 0
    for bit in bits_of(count):
        total = total * 2 + (index // bit) % 2
    return total


def attn_fwd_kernel(
    heads,
    rows,
    mem_rows,
    blocks,
    mem_ref,
    h_ref,
    g_ref,
    perm_ref,
    target_ref,
    segment_ref,
    flag_ref,
    wq_ref,
    wk_ref,
    wv_ref,
    wr_ref,
    rw_ref,
    rr_ref,
    rs_ref,
    embed_ref,
    coarse_ref,
    fine_ref,
    prob_ref,
    af_ref,
    q_hbm,
    k_hbm,
    v_hbm,
    rel_hbm,
    got_ref,
    out_hbm,
    x_hbm,
    pos_hbm,
    col_ref,
    bias_ref,
    w_buf,
    wr_buf,
    mask_ref,
    info_buf,
    x_buf,
    got_buf,
    out_ref,
    q_ref,
    k_ref,
    v_ref,
    rel_ref,
    pos_ref,
    key_order_ref,
    x_send,
    x_recv,
    info_send,
    info_recv,
    out_send,
    out_recv,
    own_sem,
    keep_sem,
):
    step = pl.program_id(0)
    piece = blocks - 1 - step
    block_id = lax.axis_index("blk")
    group_id = lax.axis_index("dp")
    wide = heads * HEAD_DIM
    width = mem_ref.shape[1]
    mem_all = mem_rows * blocks
    keys = k_ref.shape[1]
    span = rows + keys
    steps = bits_of(blocks)
    sources = (mem_ref, h_ref, g_ref)
    infos = (perm_ref, target_ref, segment_ref)
    keeps = [
        pltpu.make_async_copy(src, dst, keep_sem.at[k])
        for k, (src, dst) in enumerate(
            (
                (pos_ref, pos_hbm),
                (rel_ref, rel_hbm),
                (x_buf, x_hbm),
                (q_ref, q_hbm),
                (k_ref, k_hbm),
                (v_ref, v_hbm),
                (out_ref, out_hbm),
            )
        )
    ]
    spots = (
        pl.ds(0, mem_rows),
        pl.ds(mem_rows, rows),
        pl.ds(mem_rows + rows, rows),
    )

    def device(i):
        return (group_id, flip(block_id, i))

    def x_copy(hop, part, come):
        where = x_buf.at[flip(block_id, come), spots[part]]
        return pltpu.make_async_remote_copy(
            src_ref=sources[part] if come == 0 else where,
            dst_ref=where,
            send_sem=x_send.at[come + hop, part],
            recv_sem=x_recv.at[come + hop, part],
            device_id=device(hop),
            device_id_type=MESH_IDS,
        )

    def info_copy(i, kind):
        return pltpu.make_async_remote_copy(
            src_ref=infos[kind],
            dst_ref=info_buf.at[block_id, kind],
            send_sem=info_send.at[i, kind],
            recv_sem=info_recv.at[i, kind],
            device_id=device(i),
            device_id_type=MESH_IDS,
        )

    def own_copy(part):
        return pltpu.make_async_copy(
            sources[part], x_buf.at[block_id, spots[part]], own_sem.at[part]
        )

    def out_copy(i):
        return pltpu.make_async_remote_copy(
            src_ref=out_ref.at[i],
            dst_ref=got_buf.at[i],
            send_sem=out_send.at[i],
            recv_sem=out_recv.at[i],
            device_id=device(i),
            device_id_type=MESH_IDS,
        )

    @pl.when(step == 0)
    def _():
        barrier = pltpu.get_barrier_semaphore()
        for i in range(1, blocks):
            pl.semaphore_signal(barrier, inc=1, device_id=device(i), device_id_type=MESH_IDS)
        pl.semaphore_wait(barrier, blocks - 1)
        for part in range(3):
            x_copy(steps[-1], part, 0).start()
        for hop in steps[:-1]:
            for part in range(3):
                x_copy(hop, part, 0).start()
        for i in range(1, blocks):
            for kind in range(3):
                info_copy(i, kind).start()
        own_infos = [
            pltpu.make_async_copy(infos[kind], info_buf.at[block_id, kind], own_sem.at[3 + kind])
            for kind in range(3)
        ]
        for one in own_infos:
            one.start()
        for part in range(3):
            own_copy(part).start()
        for block in range(blocks):

            @pl.when(block_id == block)
            def _(block=block):
                at = slice(block * wide, (block + 1) * wide)
                w_buf[:, :wide] = wq_ref[:, at]
                w_buf[:, wide : 2 * wide] = wk_ref[:, at]
                w_buf[:, 2 * wide :] = wv_ref[:, at]
                wr_buf[...] = wr_ref[:, at]
                for k, ref in enumerate((rw_ref, rr_ref, rs_ref)):
                    bias_ref[k : k + 1, :] = row_of(ref)[:, at]
                bias_ref[3:5, :] = embed_ref[:, at]

        dist_count = pos_ref.shape[0]
        half = width // 2
        fine_sin, fine_cos = fine_ref[0], fine_ref[1]
        unit = fine_ref.shape[1]

        def fill(a, carry):
            at = pl.ds(pl.multiple_of(a * unit, unit), unit)
            big_sin, big_cos = coarse_ref[0, pl.ds(a, 1), :], coarse_ref[1, pl.ds(a, 1), :]
            pos_ref[at, :half] = (big_sin * fine_cos - big_cos * fine_sin).astype(BF16)
            pos_ref[at, half:] = (big_cos * fine_cos + big_sin * fine_sin).astype(BF16)
            return carry

        lax.fori_loop(0, dist_count // unit, fill, 0)
        keeps[0].start()
        rel = dot_nn(pos_ref[...], wr_buf[...]).astype(BF16)
        for h in range(heads):
            rel_ref[h] = rel[:, h * HEAD_DIM : (h + 1) * HEAD_DIM]
        keeps[1].start()
        for one in own_infos:
            one.wait()
        for part in range(3):
            own_copy(part).wait()

        def project(i):
            owner = flip(block_id, i)
            mem_at = pl.ds(pl.multiple_of(owner * mem_rows, 32), mem_rows)
            tok_at = pl.ds(pl.multiple_of(mem_all + owner * rows, 32), rows)
            qkv = dot_nn(x_buf[owner], w_buf[...])
            q_ref[i] = qkv[mem_rows:, :wide]
            low = qkv[: mem_rows + rows, wide:].astype(BF16)
            for h in range(heads):
                k_part = low[:, h * HEAD_DIM : (h + 1) * HEAD_DIM]
                v_part = low[:, wide + h * HEAD_DIM : wide + (h + 1) * HEAD_DIM]
                k_ref[h, mem_at, :HEAD_DIM] = k_part[:mem_rows]
                k_ref[h, tok_at, :HEAD_DIM] = k_part[mem_rows:]
                v_ref[h, mem_at, :] = v_part[:mem_rows]
                v_ref[h, tok_at, :] = v_part[mem_rows:]

        project(0)
        have = [0]
        for at, hop in enumerate(steps):
            fresh = [i + hop for i in have]
            for come in fresh:
                for part in range(3):
                    x_copy(come, part, 0).wait_recv() if come in steps else x_copy(
                        hop, part, come - hop
                    ).wait_recv()
                    if hop == steps[-1] and come == hop:
                        for near in steps[:-1]:
                            x_copy(near, part, come).start()
                project(come)
            have = have + fresh
        keeps[2].start()
        keeps[3].start()
        for i in range(1, blocks):
            for kind in range(3):
                info_copy(i, kind).wait()
        for part in range(3):
            for hop in steps:
                x_copy(hop, part, 0).wait_send()
            for near in steps[:-1]:
                x_copy(near, part, steps[-1]).wait_send()

        key_order_ref[:, :mem_all] = jnp.full(
            (8, mem_all), jnp.where(flag_ref[0] > 0, -2.0, 1e9), F32
        )
        for block in range(blocks):
            at = slice(mem_all + block * rows, mem_all + (block + 1) * rows)
            order = jnp.where(info_buf[block, 1] > 0, info_buf[block, 0], -1).astype(F32)
            order = jnp.broadcast_to(order, (8, rows))
            key_order_ref[:, at] = order
            ids = jnp.broadcast_to(info_buf[block, 2].astype(F32), (8, rows))
            place = lax.broadcasted_iota(jnp.int32, (8, rows), 0)
            col_ref[pl.ds(block * rows, rows), :] = jnp.where(place == 0, order, ids).T
        lane = lax.broadcasted_iota(jnp.int32, (mem_all, HEAD_DIM), 1)
        mem_extra = jnp.where(lane < 2, 1.0, 0.0).astype(BF16)
        lane = lax.broadcasted_iota(jnp.int32, (keys - mem_all, HEAD_DIM), 1)
        tok_extra = jnp.where(
            lane < 2, 1.0, jnp.where(lane < 4, col_ref[:, 1:2], 0.0)
        ).astype(BF16)
        for h in range(heads):
            k_ref[h, :mem_all, HEAD_DIM:] = mem_extra
            k_ref[h, mem_all:, HEAD_DIM:] = tok_extra
        keeps[4].start()
        keeps[5].start()

    owner = mix(block_id, piece, blocks)
    tok_at = pl.ds(pl.multiple_of(owner * rows, 32), rows)
    info = col_ref[tok_at, :]
    visible = key_order_ref[0:1, :] <= info[:, 0:1]
    key_at = lax.broadcasted_iota(jnp.int32, (rows, keys), 1) - mem_all - owner * rows
    other = key_at != lax.broadcasted_iota(jnp.int32, (rows, keys), 0)
    mask_ref[:rows, :] = jnp.where(visible, 0.0, NEGATIVE)
    mask_ref[rows:, :] = jnp.where(visible & other, 0.0, NEGATIVE)
    seg = jnp.concatenate([info[:, 1:2], info[:, 1:2]], axis=0)
    rel_at = pl.ds(pl.multiple_of((blocks - 1) * rows - owner * rows, 32), span)
    lane = lax.broadcasted_iota(jnp.int32, (2 * rows, HEAD_DIM), 1)
    for h in range(heads):
        own = slice(h * HEAD_DIM, (h + 1) * HEAD_DIM)
        raw = q_ref[piece, :, own]
        q_word = ((raw + bias_ref[0:1, own]).astype(BF16) * SCALE).astype(BF16)
        q_rel = ((raw + bias_ref[1:2, own]).astype(BF16) * SCALE).astype(BF16)
        same, differ = seg_columns((raw + bias_ref[2:3, own]) * SCALE, bias_ref[3:5, own])
        gap = differ - same
        base = same + gap * seg
        slope = gap * (1.0 - 2.0 * seg)
        base_high = base.astype(BF16).astype(F32)
        slope_high = slope.astype(BF16).astype(F32)
        extra = jnp.where(
            lane == 0,
            base_high,
            jnp.where(
                lane == 1,
                base - base_high,
                jnp.where(lane == 2, slope_high, jnp.where(lane == 3, slope - slope_high, 0.0)),
            ),
        ).astype(BF16)
        q_aug = jnp.concatenate([q_word, extra], axis=1)
        rel = dot_nt(q_rel, rel_ref[h, rel_at, :])
        shift = span - (rows - 1)
        rel = jnp.concatenate(
            [
                pltpu.roll(rel[:rows], shift, 1, stride=1, stride_axis=0)[:, :keys],
                pltpu.roll(rel[rows:], shift, 1, stride=1, stride_axis=0)[:, :keys],
            ],
            axis=0,
        )
        scores = dot_nt(q_aug, k_ref[h]) + rel + mask_ref[...]
        weight = jnp.exp(scores - jnp.max(scores, axis=1, keepdims=True))
        probs = (weight * (1.0 / jnp.sum(weight, axis=1, keepdims=True))).astype(BF16)
        prob_ref[h, 0] = probs
        attn_f = dot_nn(probs, v_ref[h])
        af_ref[0, :, own] = attn_f
        out_ref[piece, :, own] = attn_f.astype(BF16)

    for i in range(1, blocks):

        @pl.when(piece == i)
        def _(i=i):
            out_copy(i).start()

    @pl.when(step == blocks - 1)
    def _():
        keeps[6].start()
        got_ref[0] = out_ref[0]
        for i in range(1, blocks):
            out_copy(i).wait()
            got_ref[i] = got_buf[i]
        for one in keeps:
            one.wait()


def flip_eights(values):
    index = 7 - lax.broadcasted_iota(jnp.int32, (8, values.shape[1]), 0)
    return jnp.take_along_axis(values, index, axis=0)


def spread_rows(values, rows, keys):
    span = rows + keys
    padded = jnp.concatenate([values, jnp.zeros((rows, rows), F32)], axis=1)
    groups = []
    for a in range(rows // 8):
        group = flip_eights(padded[8 * a : 8 * a + 8])
        group = pltpu.roll(group, (rows - 8 - 8 * a) % span, 1, stride=1, stride_axis=0)
        groups.append(flip_eights(group))
    return jnp.concatenate(groups, axis=0)


SMALL_ROWS = 64


def place_of(index, order):
    total = 0
    for bit in order:
        total = total * 2 + (index // bit) % 2
    return total


def main_kernel(
    groups,
    heads,
    mem_rows,
    orders,
    got_ref,
    h_ref,
    g_ref,
    cot_h_ref,
    cot_g_ref,
    target_ref,
    bias_ref,
    info_ref,
    wo_hbm,
    w1_hbm,
    w2_hbm,
    wq_hbm,
    wk_hbm,
    wv_hbm,
    prob_hbm,
    af_hbm,
    q_hbm,
    k_hbm,
    v_hbm,
    rel_hbm,
    out_hbm,
    x_hbm,
    pos_hbm,
    ln1_gain_ref,
    ln1_bias_ref,
    b1_ref,
    b2_ref,
    ln2_gain_ref,
    ln2_bias_ref,
    h_out_ref,
    g_out_ref,
    h_grad_ref,
    g_grad_ref,
    mem_grad_ref,
    head_out_ref,
    w1_out_ref,
    w2_out_ref,
    wo_out_ref,
    small_out_ref,
    late_out_ref,
    wo_ref,
    w1_ref,
    w2_ref,
    attn_ref,
    slope_ref,
    act_ref,
    gpre_ref,
    ffn_all,
    gf_all,
    gb_all,
    act_s_ref,
    gpre_s_ref,
    b1_s_ref,
    resid_grad_ref,
    prob_ref,
    af_ref,
    q_ref,
    k_ref,
    v_ref,
    rel_ref,
    out_ref,
    ga_ref,
    kv_acc,
    rel_acc,
    rel_low_ref,
    dq_ref,
    dkv_ref,
    pack_ref,
    pack_got,
    dq_all,
    dkv_all,
    small_ref,
    small_got,
    late_ref,
    late_got,
    late_all,
    *rest,
):
    jobs_count = len(orders)
    nb = len(orders[0])
    src_refs = rest[:jobs_count]
    recv_refs = [
        rest[jobs_count + k * nb : jobs_count + (k + 1) * nb] for k in range(jobs_count)
    ]
    (
        w1_cut,
        w1_got,
        head_cut,
        head_got,
        w2_cut,
        w2_got,
        wo_cut,
        wo_got,
        load_sem,
        late_load_sem,
        send_sem,
        recv_sem,
        job_send,
        job_recv,
        pack_send,
        pack_recv,
        small_send,
        small_recv,
        end_send,
        end_recv,
    ) = rest[jobs_count + jobs_count * nb :]
    block_id = lax.axis_index("blk")
    group_id = lax.axis_index("dp")
    both, width = attn_ref.shape
    rows = both // 2
    wide = heads * HEAD_DIM
    blocks = act_ref.shape[0]
    part = act_s_ref.shape[2]
    steps = bits_of(blocks)
    mem_all = mem_rows * blocks
    chunk = mem_rows + both
    pair = mem_rows + rows
    keys = k_ref.shape[1]
    span = rows + keys
    dist_count = rel_ref.shape[1]
    share = width // (groups * blocks)

    def device(i):
        return (group_id, flip(block_id, i))

    held = groups * block_id + group_id
    owner_id = (held // blocks, held % blocks)
    mine = blocks * group_id + block_id
    source_id = (mine % groups, mine // groups)
    moves = held != mine

    loads = [
        pltpu.make_async_copy(src, dst, load_sem.at[k])
        for k, (src, dst) in enumerate(
            (
                (wo_hbm, wo_ref),
                (w1_hbm, w1_ref),
                (w2_hbm, w2_ref),
                (out_hbm, out_ref),
                (af_hbm, af_ref),
                (q_hbm, q_ref),
                (k_hbm, k_ref),
                (v_hbm, v_ref),
                (rel_hbm, rel_ref),
                (prob_hbm, prob_ref),
            )
        )
    ]
    for one in loads[:3]:
        one.start()
    barrier = pltpu.get_barrier_semaphore()
    for i in range(1, blocks):
        pl.semaphore_signal(barrier, inc=1, device_id=device(i), device_id_type=MESH_IDS)
    for bit in orders[0]:
        pl.semaphore_signal(
            barrier, inc=1, device_id=(flip(group_id, bit), block_id), device_id_type=MESH_IDS
        )

    @pl.when(moves)
    def _():
        pl.semaphore_signal(barrier, inc=1, device_id=source_id, device_id_type=MESH_IDS)
        pl.semaphore_wait(barrier, blocks + nb)

    @pl.when(held == mine)
    def _():
        pl.semaphore_wait(barrier, blocks - 1 + nb)

    def remote(src, dst, send, recv, target):
        return pltpu.make_async_remote_copy(
            src_ref=src,
            dst_ref=dst,
            send_sem=send,
            recv_sem=recv,
            device_id=target,
            device_id_type=MESH_IDS,
        )

    def piece_copy(ref, which, hop, come):
        at = come + hop
        return remote(
            ref.at[come], ref.at[at], send_sem.at[which, at], recv_sem.at[which, at], device(hop)
        )

    def spread(ref, which):
        for hop in reversed(steps):
            piece_copy(ref, which, hop, 0).start()

    def near_ready(ref, which):
        for hop in steps[:-1]:
            piece_copy(ref, which, hop, 0).wait_recv()

    def relay(ref, which):
        far = steps[-1]
        piece_copy(ref, which, far, 0).wait_recv()
        for hop in steps[:-1]:
            piece_copy(ref, which, hop, far).start()

    def collect(ref, which):
        for hop in steps[:-1]:
            piece_copy(ref, which, hop, steps[-1]).wait_recv()

    def finish(ref, which):
        for hop in steps:
            piece_copy(ref, which, hop, 0).wait_send()
        for hop in steps[:-1]:
            piece_copy(ref, which, hop, steps[-1]).wait_send()

    def job_source(job, stage):
        return src_refs[job] if stage == 0 else recv_refs[job][stage - 1]

    def job_half(job, stage, own):
        half = groups >> (stage + 1)
        bit = (group_id // orders[job][stage]) % 2
        which = bit if own else 1 - bit
        return pl.ds(which * half, half)

    def job_copy(job, stage):
        return remote(
            job_source(job, stage).at[job_half(job, stage, False)],
            recv_refs[job][stage],
            job_send.at[job, stage],
            job_recv.at[job, stage],
            (flip(group_id, orders[job][stage]), block_id),
        )

    def job_start(job):
        job_copy(job, 0).start()

    def job_next(job, stage):
        job_copy(job, stage).wait_recv()
        keep = job_source(job, stage)[job_half(job, stage, True)]
        into = recv_refs[job][stage]
        total = keep.astype(F32) + into[...].astype(F32)
        if stage < nb - 1:
            into[...] = total.astype(BF16)
            job_copy(job, stage + 1).start()
            return None
        return total[0]

    def job_done(job):
        for stage in range(nb):
            job_copy(job, stage).wait_send()

    def cut_copy(cut, got, which, i):
        return remote(
            cut.at[i], got.at[i], end_send.at[which, i], end_recv.at[which, i], device(i)
        )

    def cut_start(cut, which, got, first, values):
        low = values.astype(BF16)
        for k in range(blocks):
            at = mix(block_id, k, blocks)
            cut[at, :, first : first + values.shape[1]] = low[k * share : (k + 1) * share]

    def cut_send(cut, got, which):
        for i in range(1, blocks):
            cut_copy(cut, got, which, i).start()

    def owner_copy(cut, got, which):
        return remote(cut, got, end_send.at[which, 0], end_recv.at[which, 0], owner_id)

    def owner_send(cut, got, which):
        @pl.when(moves)
        def _():
            owner_copy(cut, got, which).start()

        @pl.when(held == mine)
        def _():
            got[...] = cut[...]

    def owner_wait(cut, got, which):
        @pl.when(moves)
        def _():
            owner_copy(cut, got, which).wait()

    for block in range(blocks):

        @pl.when(block_id == block)
        def _(block=block):
            for i in range(blocks):
                at = (block ^ i) * wide
                attn_ref[:, at : at + wide] = got_ref[i]
            b1_s_ref[0:1, :] = row_of(b1_ref.at[pl.ds(block * part // 128, part // 128)])

    small_ref[0] = jnp.zeros(small_ref.shape[1:], F32)
    target = jnp.broadcast_to(target_ref[...].astype(F32), (8, rows)).T[:, 0:1]
    weight = jnp.concatenate([jnp.ones((rows, 1), F32), target], axis=0)

    def squares(values):
        weighted = jnp.sum(values * values, axis=1, keepdims=True) * weight
        return column_sum(weighted[:rows]), column_sum(weighted[rows:])

    loads[0].wait()
    branch = dot_nn(attn_ref[...], wo_ref[...])
    att_stat = squares(branch)
    streams = jnp.concatenate([h_ref[...], g_ref[...]], axis=0).astype(F32)
    unit_one, rate_one = norm_parts(branch + streams)
    gain_one = row_of(ln1_gain_ref)
    out_one = unit_one * gain_one + row_of(ln1_bias_ref)
    ffn_all[0] = out_one.astype(BF16)
    spread(ffn_all, 0)
    loads[1].wait()
    loads[2].wait()
    for one in loads[3:]:
        one.start()
    branch_ffn = row_of(b2_ref)
    for c in range(blocks):
        at = slice(c * part, (c + 1) * part)
        rows_at = b1_ref.at[pl.ds(c * part // 128, part // 128)]
        act, slope = gelu_pair(dot_nn(ffn_all[0], w1_ref[:, at]) + row_of(rows_at))
        slope_ref[:, at] = slope
        act_ref[c] = act.astype(BF16)
        branch_ffn = branch_ffn + dot_nn(act_ref[c], w2_ref[at, :])
    ffn_stat = squares(branch_ffn)
    unit_two, rate_two = norm_parts(branch_ffn + out_one)
    gain_two = row_of(ln2_gain_ref)
    out_two = unit_two * gain_two + row_of(ln2_bias_ref)
    out_stat = squares(out_two)
    h_out_ref[...] = out_two[:rows].astype(BF16)
    g_out_ref[...] = out_two[rows:].astype(BF16)
    cot = jnp.concatenate([cot_h_ref[...], cot_g_ref[...]], axis=0).astype(F32)
    grad_two = norm_back(unit_two, rate_two, cot * gain_two)
    grad_ffn = grad_two.astype(BF16)
    gf_all[0] = grad_ffn
    spread(gf_all, 1)
    relay(ffn_all, 0)
    tall = width // 128
    tall_part = part // 128
    stat_row = 5 * tall + blocks * tall_part
    early = small_ref.at[0]
    put_row(early, 0, column_sum(cot * unit_two))
    put_row(early, tall, column_sum(cot))
    put_row(early, 2 * tall, column_sum(grad_ffn.astype(F32)))
    grad_out_one = grad_two
    for c in range(blocks):
        at = slice(c * part, (c + 1) * part)
        grad_pre = (dot_nt(gf_all[0], w2_ref[at, :]) * slope_ref[:, at]).astype(BF16)
        gpre_ref[c] = grad_pre
        put_row(early, 5 * tall + c * tall_part, column_sum(grad_pre.astype(F32)))
        grad_out_one = grad_out_one + dot_nt(grad_pre, w1_ref[:, at])
    put_row(early, 3 * tall, column_sum(grad_out_one * unit_one))
    put_row(early, 4 * tall, column_sum(grad_out_one))
    grad_one = norm_back(unit_one, rate_one, grad_out_one * gain_one)
    resid_grad_ref[...] = grad_one
    gb_all[0] = grad_one.astype(BF16)
    spread(gb_all, 2)
    lane = lax.broadcasted_iota(jnp.int32, (1, 128), 1)
    stats = jnp.zeros((1, 128), F32)
    terms = [att_stat[0], ffn_stat[0], out_stat[0], att_stat[1], ffn_stat[1], out_stat[1]]
    terms += [jnp.full((1, 1), float(rows), F32), column_sum(target)]
    for k, term in enumerate(terms):
        stats = jnp.where(lane == k, term, stats)
    early[stat_row : stat_row + 1, :] = stats

    small_steps = [("blk", bit) for bit in steps] + [("dp", bit) for bit in bits_of(groups)]

    def small_copy(k):
        axis, bit = small_steps[k]
        target_id = device(bit) if axis == "blk" else (flip(group_id, bit), block_id)
        return remote(
            small_ref.at[k], small_got.at[k], small_send.at[k], small_recv.at[k], target_id
        )

    def small_next(k):
        small_copy(k).wait_recv()
        small_ref[k + 1] = small_ref[k] + small_got[k]
        if k + 1 < len(small_steps):
            small_copy(k + 1).start()

    small_copy(0).start()

    own_at = pl.ds(pl.multiple_of(block_id * part, 128), part)
    act_s_ref[0] = act_ref[block_id]
    gpre_s_ref[0] = gpre_ref[block_id]
    near_ready(ffn_all, 0)
    collect(ffn_all, 0)
    for i in range(1, blocks):
        act, slope = gelu_pair(dot_nn(ffn_all[i], w1_ref[:, own_at]) + b1_s_ref[0:1, :])
        act_s_ref[i] = act.astype(BF16)
        slope_ref[:, (i - 1) * part : i * part] = slope

    def slice_back(i):
        grad_pre = dot_nt(gf_all[i], w2_ref[own_at, :]) * slope_ref[:, (i - 1) * part : i * part]
        gpre_s_ref[i] = grad_pre.astype(BF16)

    near_ready(gf_all, 1)
    for i in steps[:-1]:
        slice_back(i)
    relay(gf_all, 1)
    slice_back(steps[-1])
    collect(gf_all, 1)
    for i in range(1, blocks):
        if i not in steps:
            slice_back(i)

    def flat(ref):
        return ref[...].reshape(blocks * both, ref.shape[2])

    def put_shares(first, count, values):
        tall_share = values.shape[0] // groups
        lanes_here = values.shape[1] // count
        low = values.astype(BF16)
        for k in range(count):
            for d in range(groups):
                src_refs[first + k][place_of(d, orders[first + k])] = low[
                    d * tall_share : (d + 1) * tall_share,
                    k * lanes_here : (k + 1) * lanes_here,
                ]
            job_start(first + k)

    put_shares(0, 2, dot_tn(flat(act_s_ref), flat(gf_all)))
    put_shares(2, 2, dot_tn(flat(ffn_all), flat(gpre_s_ref)))

    x_rows = blocks * chunk
    late_loads = [
        pltpu.make_async_copy(x_hbm.at[i], w2_ref.at[pl.ds(i * chunk, chunk)], late_load_sem.at[i])
        for i in range(blocks)
    ]
    late_loads.append(
        pltpu.make_async_copy(
            pos_hbm, w2_ref.at[pl.ds(x_rows, dist_count)], late_load_sem.at[blocks]
        )
    )
    for k, src in enumerate((wq_hbm, wk_hbm, wv_hbm)):
        late_loads.append(
            pltpu.make_async_copy(
                src, w1_ref.at[:, k * width : (k + 1) * width], late_load_sem.at[blocks + 1 + k]
            )
        )
    for one in late_loads:
        one.start()

    near_ready(gb_all, 2)
    relay(gb_all, 2)
    for one in loads[3:]:
        one.wait()
    wo_own = wo_ref[pl.ds(pl.multiple_of(block_id * wide, HEAD_DIM), wide), :]
    kv_acc[...] = jnp.zeros_like(kv_acc)
    rel_acc[...] = jnp.zeros_like(rel_acc)
    late_ref[0] = jnp.zeros(late_ref.shape[1:], F32)
    collect(gb_all, 2)
    for i in range(blocks):
        ga_ref[i] = dot_nt(gb_all[i], wo_own).astype(BF16)
    put_shares(4, 1, sum(dot_tn(out_ref[i], gb_all[i]) for i in range(blocks)))

    def pack_copy(h, i):
        return remote(
            pack_ref.at[h, i], pack_got.at[h, i], pack_send.at[h, i], pack_recv.at[h, i], device(i)
        )

    events = {}
    def after(at, *acts):
        events.setdefault(at, []).extend(acts)

    def end_w2(k):
        w2_cut[:, k * (width // 2) : (k + 1) * (width // 2)] = job_next(k, nb - 1).astype(BF16)

    def end_w1(k):
        cut_start(w1_cut, 0, w1_got, k * (part // 2), job_next(2 + k, nb - 1))

    def end_wo():
        wo_cut[...] = job_next(4, nb - 1).astype(BF16)

    small_at = [(0, 0), (0, 1), (0, 2), (0, 3), (1, 0)]
    for k in range(len(small_steps)):
        after(small_at[min(k, 4)], lambda k=k: small_next(k))
    middle = list(range(nb - 1))
    after((0, 1), lambda: job_next(0, 0))
    after((0, 3), lambda: [job_next(0, k) for k in middle[1:]])
    after((1, 0), lambda: job_next(1, 0))
    after((1, 2), lambda: end_w2(0))
    after((1, 2), lambda: [job_next(1, k) for k in middle[1:]])
    after((2, 0), lambda: end_w2(1), lambda: owner_send(w2_cut, w2_got, 2))
    after((2, 0), lambda: job_next(2, 0))
    after((2, 3), lambda: [job_next(2, k) for k in middle[1:]])

    for h in range(heads):
        own = slice(h * HEAD_DIM, (h + 1) * HEAD_DIM)

        def tile(piece, carry, h=h, own=own):
            for slot in range(blocks):
                if (h, slot) in events:

                    @pl.when(piece == slot)
                    def _(slot=slot):
                        for act in events[h, slot]:
                            act()

            owner = mix(block_id, piece, blocks)
            tok_at = pl.ds(pl.multiple_of(owner * rows, 32), rows)
            rel_start = pl.multiple_of((blocks - 1) * rows - owner * rows, 128)
            rel_at = pl.ds(rel_start, span)
            seg = info_ref[tok_at, 1:2]
            seg = jnp.concatenate([seg, seg], axis=0)
            raw = q_ref[piece, :, own]
            q_word = (raw + bias_ref[0:1, own]).astype(BF16)
            q_rel = (raw + bias_ref[1:2, own]).astype(BF16)
            q_seg = raw + bias_ref[2:3, own]
            embed = bias_ref[3:5, own]
            ga = ga_ref[piece, :, own]
            probs = prob_ref[h, piece]
            ga_f = ga.astype(F32) * SCALE
            row_dot = jnp.sum(ga_f * af_ref[piece, :, own], axis=1, keepdims=True)
            grad_prob = dot_nt(ga_f.astype(BF16), v_ref[h])
            grad_score = probs.astype(F32) * (grad_prob - row_dot)
            grad_low = grad_score.astype(BF16)
            wide_word = dot_nn(grad_low, k_ref[h])
            grad_word = wide_word[:, :HEAD_DIM]
            total = wide_word[:, HEAD_DIM : HEAD_DIM + 1]
            ones = wide_word[:, HEAD_DIM + 2 : HEAD_DIM + 3]
            differ = ones + seg * (total - 2.0 * ones)
            same = total - differ
            grad_seg = same * embed[0:1] + differ * embed[1:2]
            wind = jnp.concatenate(
                [
                    spread_rows(grad_score[:rows], rows, keys),
                    spread_rows(grad_score[rows:], rows, keys),
                ],
                axis=0,
            ).astype(BF16)
            grad_rel = dot_nn(wind, rel_ref[h, rel_at, :])
            kv_acc[h, :HEAD_DIM] += dot_tn(q_word, grad_low)
            kv_acc[h, HEAD_DIM:] += dot_tn(ga, probs)
            rel_acc[h, :, rel_at] += dot_tn(q_rel, wind)
            grad_q = (grad_word + grad_rel + grad_seg).astype(BF16)
            dq_ref[piece, :, own] = grad_q
            pack_ref[h, piece, :rows, :HEAD_DIM] = grad_q[:rows]
            pack_ref[h, piece, :rows, HEAD_DIM:] = grad_q[rows:]
            late_ref[0, :, own] += jnp.concatenate(
                [
                    column_sum(grad_word),
                    column_sum(grad_rel),
                    column_sum(grad_seg),
                    column_sum(same * q_seg),
                    column_sum(differ * q_seg),
                    jnp.zeros((3, HEAD_DIM), F32),
                ],
                axis=0,
            )
            return carry

        lax.fori_loop(0, blocks, tile, 0)
        full = kv_acc[h].T.astype(BF16)
        for k in range(blocks):
            at = mix(block_id, k, blocks)
            mem_part = full[k * mem_rows : (k + 1) * mem_rows]
            tok_part = full[mem_all + k * rows : mem_all + (k + 1) * rows]
            pack_ref[h, at, rows : rows + mem_rows, :] = mem_part
            pack_ref[h, at, rows + mem_rows :, :] = tok_part
            for base, lanes_at in ((0, slice(0, HEAD_DIM)), (wide, slice(HEAD_DIM, None))):
                to = slice(base + h * HEAD_DIM, base + (h + 1) * HEAD_DIM)
                dkv_ref[at, :mem_rows, to] = mem_part[:, lanes_at]
                dkv_ref[at, mem_rows:, to] = tok_part[:, lanes_at]
        for i in range(blocks - 1, 0, -1):
            pack_copy(h, i).start()
        rel_low_ref[:, own] = rel_acc[h].T.astype(BF16)

    def late_copy(k, i=0):
        bits = bits_of(groups)
        if k < nb:
            return remote(
                late_ref.at[k],
                late_got.at[k],
                small_send.at[8 + k],
                small_recv.at[8 + k],
                (flip(group_id, bits[k]), block_id),
            )
        return remote(
            late_ref.at[nb],
            late_all.at[i],
            small_send.at[8 + nb + i],
            small_recv.at[8 + nb + i],
            device(i),
        )

    def late_next(k):
        late_copy(k).wait_recv()
        late_ref[k + 1] = late_ref[k] + late_got[k]
        if k + 1 < nb:
            late_copy(k + 1).start()
        else:
            for i in range(1, blocks):
                late_copy(nb, i).start()

    late_copy(0).start()
    for one in late_loads:
        one.wait()

    def x_part(i, first, count):
        base = mix(block_id, i, blocks) * chunk + first
        return w2_ref[pl.ds(pl.multiple_of(base, 32), count), :]

    grad_wr = dot_tn(w2_ref[x_rows : x_rows + dist_count, :], rel_low_ref[...])
    grad_wq = sum(dot_tn(x_part(i, mem_rows, both), dq_ref[i]) for i in range(blocks))
    put_shares(5, 1, jnp.concatenate([grad_wr, grad_wq], axis=1))
    grad_wkv = sum(dot_tn(x_part(i, 0, pair), dkv_ref[i]) for i in range(blocks))
    put_shares(6, 1, grad_wkv)

    job_next(3, 0)
    end_w1(0)
    late_next(0)
    for k in middle[1:]:
        job_next(3, k)
    job_next(4, 0)

    for h in range(heads):
        for i in range(1, blocks):
            pack_copy(h, i).wait_recv()
    for block in range(blocks):

        @pl.when(block_id == block)
        def _(block=block):
            for h in range(heads):
                for i in range(blocks):
                    at = (block ^ i) * wide + h * HEAD_DIM
                    to = slice(at, at + HEAD_DIM)
                    piece = pack_ref[h, 0] if i == 0 else pack_got[h, i]
                    dq_all[:rows, to] = piece[:rows, :HEAD_DIM]
                    dq_all[rows:, to] = piece[:rows, HEAD_DIM:]
                    dkv_all[:, to] = piece[rows:, :HEAD_DIM]
                    dkv_all[:, width + at : width + at + HEAD_DIM] = piece[rows:, HEAD_DIM:]

    grad_rows = dot_nt(dkv_all[:, :width], w1_ref[:, width : 2 * width]) + dot_nt(
        dkv_all[:, width:], w1_ref[:, 2 * width : 3 * width]
    )
    grad_streams = resid_grad_ref[...] + dot_nt(dq_all[...], w1_ref[:, :width])
    h_grad_ref[...] = grad_streams[:rows] + grad_rows[mem_rows:]
    g_grad_ref[...] = grad_streams[rows:]
    mem_grad_ref[...] = grad_rows[:mem_rows]

    for k in middle[1:]:
        job_next(4, k)
    for k in range(1, nb):
        late_next(k)
    end_w1(1)
    cut_send(w1_cut, w1_got, 0)
    end_wo()
    owner_send(wo_cut, wo_got, 3)
    job_next(5, 0)
    for k in middle[1:]:
        job_next(5, k)
    job_next(6, 0)
    for k in middle[1:]:
        job_next(6, k)
    cut_start(head_cut, 1, head_got, 0, job_next(5, nb - 1))
    cut_start(head_cut, 1, head_got, 2 * wide, job_next(6, nb - 1))
    cut_send(head_cut, head_got, 1)
    owner_wait(w2_cut, w2_got, 2)
    owner_wait(wo_cut, wo_got, 3)
    w2_out_ref[...] = w2_got[...]
    wo_out_ref[...] = wo_got[...]
    w1_out_ref[0] = w1_cut[0]
    for i in range(1, blocks):
        cut_copy(w1_cut, w1_got, 0, i).wait()
        w1_out_ref[i] = w1_got[i]
    head_out_ref[0] = head_cut[0]
    for i in range(1, blocks):
        cut_copy(head_cut, head_got, 1, i).wait()
        head_out_ref[i] = head_got[i]

    small_out_ref[...] = small_ref[len(small_steps)]
    for i in range(1, blocks):
        late_copy(nb, i).wait()
        late_out_ref[i] = late_all[i]
    late_out_ref[0] = late_ref[nb]

    for k in range(len(small_steps)):
        small_copy(k).wait_send()
    for k in range(nb):
        late_copy(k).wait_send()
    for h in range(heads):
        for i in range(1, blocks):
            pack_copy(h, i).wait_send()
    for job in range(jobs_count):
        job_done(job)
    for which, ref in enumerate((ffn_all, gf_all, gb_all)):
        finish(ref, which)


def finish_kernel(
    heads,
    h_ref,
    g_ref,
    h_grad_ref,
    g_grad_ref,
    mem_grad_ref,
    head_ref,
    w1_ref,
    w2_ref,
    wo_ref,
    small_ref,
    late_ref,
    h_out_ref,
    g_out_ref,
    h_grad_out_ref,
    g_grad_out_ref,
    mem_grad_out_ref,
    wq_out_ref,
    wk_out_ref,
    wv_out_ref,
    wr_out_ref,
    wo_out_ref,
    w1_out_ref,
    w2_out_ref,
    rw_out_ref,
    rr_out_ref,
    rs_out_ref,
    embed_out_ref,
    ln1_gain_out_ref,
    ln1_bias_out_ref,
    b1_out_ref,
    b2_out_ref,
    ln2_gain_out_ref,
    ln2_bias_out_ref,
    rms_out_ref,
    rows_ref,
):
    block_id = lax.axis_index("blk")
    blocks, share, part = w1_ref.shape
    width = h_ref.shape[1]
    wide = heads * HEAD_DIM
    tall = width // 128
    tall_part = part // 128
    stat_row = 5 * tall + blocks * tall_part

    def put_lanes(out, values, stride, first):
        count = values.shape[0]
        for j in range(values.shape[1] // 128):
            out[pl.ds(first + j, count, stride=stride), :] = values[:, 128 * j : 128 * (j + 1)]

    h_out_ref[...] = h_ref[...]
    g_out_ref[...] = g_ref[...]
    h_grad_out_ref[...] = h_grad_ref[...]
    g_grad_out_ref[...] = g_grad_ref[...]
    mem_grad_out_ref[...] = mem_grad_ref[...]
    put_lanes(w2_out_ref, w2_ref[...].astype(F32), tall, 0)
    put_lanes(wo_out_ref, wo_ref[...].astype(F32), tall, 0)
    for i in range(blocks):
        first = mix(block_id, i, blocks) * tall_part
        put_lanes(w1_out_ref, w1_ref[i].astype(F32), blocks * tall_part, first)
    for block in range(blocks):

        @pl.when(block_id == block)
        def _(block=block):
            for i in range(blocks):
                at = slice((block ^ i) * wide, ((block ^ i) + 1) * wide)
                for k in range(4):
                    rows_ref[k, :share, at] = head_ref[i, :, k * wide : (k + 1) * wide].astype(F32)
                rows_ref[4, :8, at] = late_ref[i]

    for k, out in enumerate((wr_out_ref, wq_out_ref, wk_out_ref, wv_out_ref)):
        put_lanes(out, rows_ref[k, :share, :], tall, 0)
    put_row(rw_out_ref, 0, rows_ref[4, 0:1, :])
    put_row(rr_out_ref, 0, rows_ref[4, 1:2, :])
    put_row(rs_out_ref, 0, rows_ref[4, 2:3, :])
    embed_out_ref[...] = rows_ref[4, 3:5, :]
    ln2_gain_out_ref[...] = small_ref[:tall]
    ln2_bias_out_ref[...] = small_ref[tall : 2 * tall]
    b2_out_ref[...] = small_ref[2 * tall : 3 * tall]
    ln1_gain_out_ref[...] = small_ref[3 * tall : 4 * tall]
    ln1_bias_out_ref[...] = small_ref[4 * tall : 5 * tall]
    b1_out_ref[...] = small_ref[5 * tall : stat_row]
    stats = small_ref[stat_row : stat_row + 1]
    lane = lax.broadcasted_iota(jnp.int32, (1, 128), 1)
    counts = jnp.where(lane < 3, stats[:, 6:7], stats[:, 7:8]) * float(width)
    rms_out_ref[...] = jnp.sqrt(stats / counts)


def whole(shape):
    return pl.BlockSpec(shape, lambda *_: (0,) * len(shape))


def local(
    h_in,
    g_in,
    memory,
    cot_h,
    cot_g,
    perm_order,
    target,
    segment,
    mem_flag,
    w_q,
    w_k,
    w_v,
    w_r,
    w_o,
    r_w_bias,
    r_r_bias,
    r_s_bias,
    seg_embed,
    ln1_gain,
    ln1_bias,
    w_1,
    b_1,
    w_2,
    b_2,
    ln2_gain,
    ln2_bias,
):
    _, rows, width = h_in.shape
    mem_rows = memory.shape[1]
    hidden = w_1.shape[1]
    blocks = lax.axis_size("blk")
    groups = lax.axis_size("dp")
    tok_all = rows * blocks
    mem_all = mem_rows * blocks
    keys = mem_all + tok_all
    dist_count = tok_all + keys
    heads = HEADS // blocks
    wide = heads * HEAD_DIM
    both = 2 * rows
    chunk = mem_rows + both
    pair = mem_rows + rows
    part = hidden // blocks
    tall = width // 128
    share = width // (groups * blocks)
    nb = len(bits_of(groups))
    hbm = pl.BlockSpec(memory_space=pl.ANY)
    vmem = pl.BlockSpec(memory_space=pltpu.VMEM)
    shape = jax.ShapeDtypeStruct

    def lanes(values):
        return values.reshape(-1, 128)

    coarse, fine = position_units(keys - 1, dist_count, width, 32)
    (
        probs, attn_f, q_raw, k_aug, v_all, rel_heads, got_out, attn_out, x_all, pos_table,
        query_info, biases,
    ) = pl.pallas_call(
        functools.partial(attn_fwd_kernel, heads, rows, mem_rows, blocks),
        name="attn_fwd",
        grid=(blocks,),
        in_specs=[hbm] * 3
        + [whole((1, rows))] * 3
        + [pl.BlockSpec(memory_space=pltpu.SMEM)]
        + [whole((width, width))] * 4
        + [whole((tall, 128))] * 3
        + [whole((2, width)), whole(coarse.shape), whole(fine.shape)],
        out_specs=[
            pl.BlockSpec((heads, 1, both, keys), lambda s: (0, blocks - 1 - s, 0, 0)),
            pl.BlockSpec((1, both, wide), lambda s: (blocks - 1 - s, 0, 0)),
            hbm,
            hbm,
            hbm,
            hbm,
            whole((blocks, both, wide)),
            hbm,
            hbm,
            hbm,
            whole((tok_all, 8)),
            whole((8, wide)),
        ],
        out_shape=[
            shape((heads, blocks, both, keys), BF16),
            shape((blocks, both, wide), F32),
            shape((blocks, both, wide), F32),
            shape((heads, keys, 2 * HEAD_DIM), BF16),
            shape((heads, keys, HEAD_DIM), BF16),
            shape((heads, dist_count, HEAD_DIM), BF16),
            shape((blocks, both, wide), BF16),
            shape((blocks, both, wide), BF16),
            shape((blocks, chunk, width), BF16),
            shape((dist_count, width), BF16),
            shape((tok_all, 8), F32),
            shape((8, wide), F32),
        ],
        scratch_shapes=[
            pltpu.VMEM((width, 3 * wide), BF16),
            pltpu.VMEM((width, wide), BF16),
            pltpu.VMEM((both, keys), F32),
            pltpu.VMEM((blocks, 3, 1, rows), jnp.int32),
            pltpu.VMEM((blocks, chunk, width), BF16),
            pltpu.VMEM((blocks, both, wide), BF16),
            pltpu.VMEM((blocks, both, wide), BF16),
            pltpu.VMEM((blocks, both, wide), F32),
            pltpu.VMEM((heads, keys, 2 * HEAD_DIM), BF16),
            pltpu.VMEM((heads, keys, HEAD_DIM), BF16),
            pltpu.VMEM((heads, dist_count, HEAD_DIM), BF16),
            pltpu.VMEM((dist_count, width), BF16),
            pltpu.VMEM((8, keys), F32),
            pltpu.SemaphoreType.DMA((blocks, 3)),
            pltpu.SemaphoreType.DMA((blocks, 3)),
            pltpu.SemaphoreType.DMA((blocks, 3)),
            pltpu.SemaphoreType.DMA((blocks, 3)),
            pltpu.SemaphoreType.DMA((blocks,)),
            pltpu.SemaphoreType.DMA((blocks,)),
            pltpu.SemaphoreType.DMA((6,)),
            pltpu.SemaphoreType.DMA((7,)),
        ],
        compiler_params=pltpu.CompilerParams(
            vmem_limit_bytes=60 << 20, collective_id=0, has_side_effects=True
        ),
    )(
        memory[0], h_in[0], g_in[0], perm_order, target, segment, mem_flag, w_q, w_k, w_v, w_r,
        lanes(r_w_bias), lanes(r_r_bias), lanes(r_s_bias), seg_embed, coarse, fine,
    )

    near = tuple(bits_of(groups))
    orders = (near,) * 7
    job_shapes = (
        [(part // groups, width // 2)] * 2
        + [(width // groups, part // 2)] * 2
        + [(wide // groups, width)]
        + [(width // groups, 2 * wide)] * 2
    )
    sources = [pltpu.VMEM((groups,) + one, BF16) for one in job_shapes]
    receivers = [
        pltpu.VMEM((groups >> (k + 1),) + one, BF16) for one in job_shapes for k in range(nb)
    ]
    bits = len(bits_of(blocks)) + nb
    square = width * width // (groups * blocks * 128)
    oblong = width * hidden // (groups * blocks * 128)
    grads_shape = [
        shape((rows, width), BF16),
        shape((rows, width), BF16),
        shape((rows, width), F32),
        shape((rows, width), F32),
        shape((mem_rows, width), F32),
    ]
    parts = pl.pallas_call(
        functools.partial(main_kernel, groups, heads, mem_rows, orders),
        name="main",
        in_specs=[vmem] * 8 + [hbm] * 15 + [vmem] * 6,
        out_specs=[vmem] * 11,
        out_shape=grads_shape
        + [
            shape((blocks, share, 4 * wide), BF16),
            shape((blocks, share, part), BF16),
            shape((part // groups, width), BF16),
            shape((wide // groups, width), BF16),
            shape((SMALL_ROWS, 128), F32),
            shape((blocks, 8, wide), F32),
        ],
        scratch_shapes=[
            pltpu.VMEM((width, width), BF16),
            pltpu.VMEM((width, hidden), BF16),
            pltpu.VMEM((hidden, width), BF16),
            pltpu.VMEM((both, width), BF16),
            pltpu.VMEM((both, hidden), F32),
            pltpu.VMEM((blocks, both, part), BF16),
            pltpu.VMEM((blocks, both, part), BF16),
            pltpu.VMEM((blocks, both, width), BF16),
            pltpu.VMEM((blocks, both, width), BF16),
            pltpu.VMEM((blocks, both, width), BF16),
            pltpu.VMEM((blocks, both, part), BF16),
            pltpu.VMEM((blocks, both, part), BF16),
            pltpu.VMEM((8, part), F32),
            pltpu.VMEM((both, width), F32),
            pltpu.VMEM((heads, blocks, both, keys), BF16),
            pltpu.VMEM((blocks, both, wide), F32),
            pltpu.VMEM((blocks, both, wide), F32),
            pltpu.VMEM((heads, keys, 2 * HEAD_DIM), BF16),
            pltpu.VMEM((heads, keys, HEAD_DIM), BF16),
            pltpu.VMEM((heads, dist_count, HEAD_DIM), BF16),
            pltpu.VMEM((blocks, both, wide), BF16),
            pltpu.VMEM((blocks, both, wide), BF16),
            pltpu.VMEM((heads, 2 * HEAD_DIM, keys), F32),
            pltpu.VMEM((heads, HEAD_DIM, dist_count), F32),
            pltpu.VMEM((dist_count, wide), BF16),
            pltpu.VMEM((blocks, both, wide), BF16),
            pltpu.VMEM((blocks, pair, 2 * wide), BF16),
            pltpu.VMEM((heads, blocks, rows + pair, 2 * HEAD_DIM), BF16),
            pltpu.VMEM((heads, blocks, rows + pair, 2 * HEAD_DIM), BF16),
            pltpu.VMEM((both, width), BF16),
            pltpu.VMEM((pair, 2 * width), BF16),
            pltpu.VMEM((bits + 1, SMALL_ROWS, 128), F32),
            pltpu.VMEM((bits, SMALL_ROWS, 128), F32),
            pltpu.VMEM((nb + 1, 8, wide), F32),
            pltpu.VMEM((nb, 8, wide), F32),
            pltpu.VMEM((blocks, 8, wide), F32),
        ]
        + sources
        + receivers
        + [
            pltpu.VMEM((blocks, share, part), BF16),
            pltpu.VMEM((blocks, share, part), BF16),
            pltpu.VMEM((blocks, share, 4 * wide), BF16),
            pltpu.VMEM((blocks, share, 4 * wide), BF16),
            pltpu.VMEM((part // groups, width), BF16),
            pltpu.VMEM((part // groups, width), BF16),
            pltpu.VMEM((wide // groups, width), BF16),
            pltpu.VMEM((wide // groups, width), BF16),
            pltpu.SemaphoreType.DMA((10,)),
            pltpu.SemaphoreType.DMA((blocks + 4,)),
            pltpu.SemaphoreType.DMA((3, blocks)),
            pltpu.SemaphoreType.DMA((3, blocks)),
            pltpu.SemaphoreType.DMA((len(job_shapes), nb)),
            pltpu.SemaphoreType.DMA((len(job_shapes), nb)),
            pltpu.SemaphoreType.DMA((heads, blocks)),
            pltpu.SemaphoreType.DMA((heads, blocks)),
            pltpu.SemaphoreType.DMA((8 + nb + blocks,)),
            pltpu.SemaphoreType.DMA((8 + nb + blocks,)),
            pltpu.SemaphoreType.DMA((4, blocks)),
            pltpu.SemaphoreType.DMA((4, blocks)),
        ],
        compiler_params=pltpu.CompilerParams(
            vmem_limit_bytes=67043328, collective_id=1, has_side_effects=True
        ),
    )(
        got_out, h_in[0], g_in[0], cot_h[0], cot_g[0], target, biases, query_info,
        w_o, w_1, w_2, w_q, w_k, w_v, probs, attn_f, q_raw, k_aug, v_all, rel_heads, attn_out,
        x_all, pos_table,
        lanes(ln1_gain), lanes(ln1_bias), lanes(b_1), lanes(b_2), lanes(ln2_gain), lanes(ln2_bias),
    )
    outs = pl.pallas_call(
        functools.partial(finish_kernel, heads),
        name="finish",
        in_specs=[vmem] * 11,
        out_specs=[vmem] * 23,
        out_shape=grads_shape
        + [shape((square, 128), F32)] * 5
        + [shape((oblong, 128), F32)] * 2
        + [shape((tall, 128), F32)] * 3
        + [shape((2, width), F32)]
        + [shape((tall, 128), F32)] * 2
        + [shape((hidden // 128, 128), F32)]
        + [shape((tall, 128), F32)] * 3
        + [shape((1, 128), F32)],
        scratch_shapes=[pltpu.VMEM((5, max(8, share), width), F32)],
        compiler_params=pltpu.CompilerParams(vmem_limit_bytes=60 << 20),
    )(*parts)
    outs = list(outs)
    for k in range(5):
        outs[k] = outs[k][None]
    for k in list(range(5, 15)) + list(range(16, 22)):
        outs[k] = outs[k].reshape(-1)
    outs[22] = outs[22][0, :6]
    return tuple(outs)


def solution(mesh):
    rows = P("dp", "blk", None)
    ints = P("dp", "blk")
    flat = P(("dp", "blk"))
    return jax.shard_map(
        local,
        mesh=mesh,
        in_specs=(rows,) * 5 + (ints,) * 3 + (P("dp"),) + (P(),) * 17,
        out_specs=(rows,) * 5 + (flat,) * 7 + (P(),) * 11,
        check_vma=False,
    )
```

```python
import functools
import math

import jax
import jax.numpy as jnp
import numpy as np
from jax import lax
from jax.experimental import pallas as pl
from jax.experimental.pallas import tpu as pltpu
from jax.sharding import PartitionSpec as P

HEADS = 12
HEAD_DIM = 64
EPSILON = 1e-12
NEGATIVE = -1e30
SCALE = 1.0 / math.sqrt(HEAD_DIM)
F32 = jnp.float32
BF16 = jnp.bfloat16
MESH_IDS = pl.DeviceIdType.MESH


def position_units(top, dist_count, model_width, unit):
    freq = np.exp(np.arange(model_width // 2) * (-2.0 * math.log(10000.0) / model_width))
    coarse = (top - unit * np.arange(dist_count // unit))[:, None] * freq[None, :]
    fine = np.arange(unit)[:, None] * freq[None, :]
    return tuple(
        np.stack([np.sin(angle), np.cos(angle)]).astype(np.float32) for angle in (coarse, fine)
    )


def dot_nn(left, right):
    return lax.dot_general(left, right, (((1,), (0,)), ((), ())), preferred_element_type=F32)


def dot_nt(left, right):
    return lax.dot_general(left, right, (((1,), (1,)), ((), ())), preferred_element_type=F32)


def dot_tn(left, right):
    return lax.dot_general(left, right, (((0,), (0,)), ((), ())), preferred_element_type=F32)


def bits_of(count):
    return [1 << k for k in range(count.bit_length() - 1)]


def seg_columns(q_seg, embed):
    return (
        jnp.sum(q_seg * embed[0:1], axis=1, keepdims=True),
        jnp.sum(q_seg * embed[1:2], axis=1, keepdims=True),
    )


def flip(index, step):
    for bit in (1 << k for k in range(step.bit_length())):
        if step & bit:
            index = index + bit - 2 * bit * ((index // bit) % 2)
    return index


def mix(index, other, blocks):
    total = 0
    for bit in bits_of(blocks):
        left = (index // bit) % 2
        right = (other // bit) % 2
        total = total + bit * (left + right - 2 * left * right)
    return total


def row_of(ref):
    return jnp.concatenate([ref[j : j + 1, :] for j in range(ref.shape[0])], axis=1)


def put_row(ref, at, values):
    for j in range(values.shape[1] // 128):
        ref[at + j : at + j + 1, :] = values[:, 128 * j : 128 * (j + 1)]


def row_mean(values):
    return jnp.mean(values, axis=1, keepdims=True)


def norm_parts(values):
    center = values - row_mean(values)
    rate = lax.rsqrt(row_mean(center * center) + EPSILON)
    return center * rate, rate


def norm_back(unit, rate, scaled):
    return rate * (scaled - row_mean(scaled) - unit * row_mean(scaled * unit))


def gelu_pair(values):
    square = values * values
    inner = math.sqrt(2.0 / math.pi) * values * (1.0 + 0.044715 * square)
    bend = jnp.tanh(inner)
    half = 0.5 * (1.0 + bend)
    slope = half + values * (1.0 - bend * bend) * (
        0.5 * math.sqrt(2.0 / math.pi) * (1.0 + 3 * 0.044715 * square)
    )
    return values * half, slope


def column_sum(values):
    return jnp.sum(values, axis=0, keepdims=True)


def reversed_index(index, count):
    total = 0
    for bit in bits_of(count):
        total = total * 2 + (index // bit) % 2
    return total


def attn_fwd_kernel(
    heads,
    rows,
    mem_rows,
    blocks,
    mem_ref,
    h_ref,
    g_ref,
    perm_ref,
    target_ref,
    segment_ref,
    flag_ref,
    wq_ref,
    wk_ref,
    wv_ref,
    wr_ref,
    rw_ref,
    rr_ref,
    rs_ref,
    embed_ref,
    coarse_ref,
    fine_ref,
    prob_ref,
    af_ref,
    q_hbm,
    k_hbm,
    v_hbm,
    rel_hbm,
    got_ref,
    out_hbm,
    x_hbm,
    pos_hbm,
    col_ref,
    bias_ref,
    w_buf,
    wr_buf,
    mask_ref,
    info_buf,
    x_buf,
    got_buf,
    out_ref,
    q_ref,
    k_ref,
    v_ref,
    rel_ref,
    pos_ref,
    key_order_ref,
    x_send,
    x_recv,
    info_send,
    info_recv,
    out_send,
    out_recv,
    own_sem,
    keep_sem,
):
    step = pl.program_id(0)
    piece = blocks - 1 - step
    block_id = lax.axis_index("blk")
    group_id = lax.axis_index("dp")
    wide = heads * HEAD_DIM
    width = mem_ref.shape[1]
    mem_all = mem_rows * blocks
    keys = k_ref.shape[1]
    span = rows + keys
    steps = bits_of(blocks)
    sources = (mem_ref, h_ref, g_ref)
    infos = (perm_ref, target_ref, segment_ref)
    keeps = [
        pltpu.make_async_copy(src, dst, keep_sem.at[k])
        for k, (src, dst) in enumerate(
            (
                (pos_ref, pos_hbm),
                (rel_ref, rel_hbm),
                (x_buf, x_hbm),
                (q_ref, q_hbm),
                (k_ref, k_hbm),
                (v_ref, v_hbm),
                (out_ref, out_hbm),
            )
        )
    ]
    spots = (
        pl.ds(0, mem_rows),
        pl.ds(mem_rows, rows),
        pl.ds(mem_rows + rows, rows),
    )

    def device(i):
        return (group_id, flip(block_id, i))

    def x_copy(hop, part, come):
        where = x_buf.at[flip(block_id, come), spots[part]]
        return pltpu.make_async_remote_copy(
            src_ref=sources[part] if come == 0 else where,
            dst_ref=where,
            send_sem=x_send.at[come + hop, part],
            recv_sem=x_recv.at[come + hop, part],
            device_id=device(hop),
            device_id_type=MESH_IDS,
        )

    def info_copy(i, kind):
        return pltpu.make_async_remote_copy(
            src_ref=infos[kind],
            dst_ref=info_buf.at[block_id, kind],
            send_sem=info_send.at[i, kind],
            recv_sem=info_recv.at[i, kind],
            device_id=device(i),
            device_id_type=MESH_IDS,
        )

    def own_copy(part):
        return pltpu.make_async_copy(
            sources[part], x_buf.at[block_id, spots[part]], own_sem.at[part]
        )

    def out_copy(i):
        return pltpu.make_async_remote_copy(
            src_ref=out_ref.at[i],
            dst_ref=got_buf.at[i],
            send_sem=out_send.at[i],
            recv_sem=out_recv.at[i],
            device_id=device(i),
            device_id_type=MESH_IDS,
        )

    @pl.when(step == 0)
    def _():
        barrier = pltpu.get_barrier_semaphore()
        for i in range(1, blocks):
            pl.semaphore_signal(barrier, inc=1, device_id=device(i), device_id_type=MESH_IDS)
        pl.semaphore_wait(barrier, blocks - 1)
        for part in range(3):
            x_copy(steps[-1], part, 0).start()
        for hop in steps[:-1]:
            for part in range(3):
                x_copy(hop, part, 0).start()
        for i in range(1, blocks):
            for kind in range(3):
                info_copy(i, kind).start()
        own_infos = [
            pltpu.make_async_copy(infos[kind], info_buf.at[block_id, kind], own_sem.at[3 + kind])
            for kind in range(3)
        ]
        for one in own_infos:
            one.start()
        for part in range(3):
            own_copy(part).start()
        for block in range(blocks):

            @pl.when(block_id == block)
            def _(block=block):
                at = slice(block * wide, (block + 1) * wide)
                w_buf[:, :wide] = wq_ref[:, at]
                w_buf[:, wide : 2 * wide] = wk_ref[:, at]
                w_buf[:, 2 * wide :] = wv_ref[:, at]
                wr_buf[...] = wr_ref[:, at]
                for k, ref in enumerate((rw_ref, rr_ref, rs_ref)):
                    bias_ref[k : k + 1, :] = row_of(ref)[:, at]
                bias_ref[3:5, :] = embed_ref[:, at]

        dist_count = pos_ref.shape[0]
        half = width // 2
        fine_sin, fine_cos = fine_ref[0], fine_ref[1]
        unit = fine_ref.shape[1]

        def fill(a, carry):
            at = pl.ds(pl.multiple_of(a * unit, unit), unit)
            big_sin, big_cos = coarse_ref[0, pl.ds(a, 1), :], coarse_ref[1, pl.ds(a, 1), :]
            pos_ref[at, :half] = (big_sin * fine_cos - big_cos * fine_sin).astype(BF16)
            pos_ref[at, half:] = (big_cos * fine_cos + big_sin * fine_sin).astype(BF16)
            return carry

        lax.fori_loop(0, dist_count // unit, fill, 0)
        keeps[0].start()
        rel = dot_nn(pos_ref[...], wr_buf[...]).astype(BF16)
        for h in range(heads):
            rel_ref[h] = rel[:, h * HEAD_DIM : (h + 1) * HEAD_DIM]
        keeps[1].start()
        for one in own_infos:
            one.wait()
        for part in range(3):
            own_copy(part).wait()

        def project(i):
            owner = flip(block_id, i)
            mem_at = pl.ds(pl.multiple_of(owner * mem_rows, 32), mem_rows)
            tok_at = pl.ds(pl.multiple_of(mem_all + owner * rows, 32), rows)
            qkv = dot_nn(x_buf[owner], w_buf[...])
            q_ref[i] = qkv[mem_rows:, :wide]
            low = qkv[: mem_rows + rows, wide:].astype(BF16)
            for h in range(heads):
                k_part = low[:, h * HEAD_DIM : (h + 1) * HEAD_DIM]
                v_part = low[:, wide + h * HEAD_DIM : wide + (h + 1) * HEAD_DIM]
                k_ref[h, mem_at, :HEAD_DIM] = k_part[:mem_rows]
                k_ref[h, tok_at, :HEAD_DIM] = k_part[mem_rows:]
                v_ref[h, mem_at, :] = v_part[:mem_rows]
                v_ref[h, tok_at, :] = v_part[mem_rows:]

        project(0)
        have = [0]
        for at, hop in enumerate(steps):
            fresh = [i + hop for i in have]
            for come in fresh:
                for part in range(3):
                    x_copy(come, part, 0).wait_recv() if come in steps else x_copy(
                        hop, part, come - hop
                    ).wait_recv()
                    if hop == steps[-1] and come == hop:
                        for near in steps[:-1]:
                            x_copy(near, part, come).start()
                project(come)
            have = have + fresh
        keeps[2].start()
        keeps[3].start()
        for i in range(1, blocks):
            for kind in range(3):
                info_copy(i, kind).wait()
        for part in range(3):
            for hop in steps:
                x_copy(hop, part, 0).wait_send()
            for near in steps[:-1]:
                x_copy(near, part, steps[-1]).wait_send()

        key_order_ref[:, :mem_all] = jnp.full(
            (8, mem_all), jnp.where(flag_ref[0] > 0, -2.0, 1e9), F32
        )
        for block in range(blocks):
            at = slice(mem_all + block * rows, mem_all + (block + 1) * rows)
            order = jnp.where(info_buf[block, 1] > 0, info_buf[block, 0], -1).astype(F32)
            order = jnp.broadcast_to(order, (8, rows))
            key_order_ref[:, at] = order
            ids = jnp.broadcast_to(info_buf[block, 2].astype(F32), (8, rows))
            place = lax.broadcasted_iota(jnp.int32, (8, rows), 0)
            col_ref[pl.ds(block * rows, rows), :] = jnp.where(place == 0, order, ids).T
        lane = lax.broadcasted_iota(jnp.int32, (mem_all, HEAD_DIM), 1)
        mem_extra = jnp.where(lane < 2, 1.0, 0.0).astype(BF16)
        lane = lax.broadcasted_iota(jnp.int32, (keys - mem_all, HEAD_DIM), 1)
        tok_extra = jnp.where(
            lane < 2, 1.0, jnp.where(lane < 4, col_ref[:, 1:2], 0.0)
        ).astype(BF16)
        for h in range(heads):
            k_ref[h, :mem_all, HEAD_DIM:] = mem_extra
            k_ref[h, mem_all:, HEAD_DIM:] = tok_extra
        keeps[4].start()
        keeps[5].start()

    owner = mix(block_id, piece, blocks)
    tok_at = pl.ds(pl.multiple_of(owner * rows, 32), rows)
    info = col_ref[tok_at, :]
    visible = key_order_ref[0:1, :] <= info[:, 0:1]
    key_at = lax.broadcasted_iota(jnp.int32, (rows, keys), 1) - mem_all - owner * rows
    other = key_at != lax.broadcasted_iota(jnp.int32, (rows, keys), 0)
    mask_ref[:rows, :] = jnp.where(visible, 0.0, NEGATIVE)
    mask_ref[rows:, :] = jnp.where(visible & other, 0.0, NEGATIVE)
    seg = jnp.concatenate([info[:, 1:2], info[:, 1:2]], axis=0)
    rel_at = pl.ds(pl.multiple_of((blocks - 1) * rows - owner * rows, 32), span)
    lane = lax.broadcasted_iota(jnp.int32, (2 * rows, HEAD_DIM), 1)
    for h in range(heads):
        own = slice(h * HEAD_DIM, (h + 1) * HEAD_DIM)
        raw = q_ref[piece, :, own]
        q_word = ((raw + bias_ref[0:1, own]).astype(BF16) * SCALE).astype(BF16)
        q_rel = ((raw + bias_ref[1:2, own]).astype(BF16) * SCALE).astype(BF16)
        same, differ = seg_columns((raw + bias_ref[2:3, own]) * SCALE, bias_ref[3:5, own])
        gap = differ - same
        base = same + gap * seg
        slope = gap * (1.0 - 2.0 * seg)
        base_high = base.astype(BF16).astype(F32)
        slope_high = slope.astype(BF16).astype(F32)
        extra = jnp.where(
            lane == 0,
            base_high,
            jnp.where(
                lane == 1,
                base - base_high,
                jnp.where(lane == 2, slope_high, jnp.where(lane == 3, slope - slope_high, 0.0)),
            ),
        ).astype(BF16)
        q_aug = jnp.concatenate([q_word, extra], axis=1)
        rel = dot_nt(q_rel, rel_ref[h, rel_at, :])
        shift = span - (rows - 1)
        rel = jnp.concatenate(
            [
                pltpu.roll(rel[:rows], shift, 1, stride=1, stride_axis=0)[:, :keys],
                pltpu.roll(rel[rows:], shift, 1, stride=1, stride_axis=0)[:, :keys],
            ],
            axis=0,
        )
        scores = dot_nt(q_aug, k_ref[h]) + rel + mask_ref[...]
        weight = jnp.exp(scores - jnp.max(scores, axis=1, keepdims=True))
        probs = (weight * (1.0 / jnp.sum(weight, axis=1, keepdims=True))).astype(BF16)
        prob_ref[h, 0] = probs
        attn_f = dot_nn(probs, v_ref[h])
        af_ref[0, :, own] = attn_f
        out_ref[piece, :, own] = attn_f.astype(BF16)

    for i in range(1, blocks):

        @pl.when(piece == i)
        def _(i=i):
            out_copy(i).start()

    @pl.when(step == blocks - 1)
    def _():
        keeps[6].start()
        got_ref[0] = out_ref[0]
        for i in range(1, blocks):
            out_copy(i).wait()
            got_ref[i] = got_buf[i]
        for one in keeps:
            one.wait()


def flip_eights(values):
    index = 7 - lax.broadcasted_iota(jnp.int32, (8, values.shape[1]), 0)
    return jnp.take_along_axis(values, index, axis=0)


def spread_rows(values, rows, keys):
    span = rows + keys
    padded = jnp.concatenate([values, jnp.zeros((rows, rows), F32)], axis=1)
    groups = []
    for a in range(rows // 8):
        group = flip_eights(padded[8 * a : 8 * a + 8])
        group = pltpu.roll(group, (rows - 8 - 8 * a) % span, 1, stride=1, stride_axis=0)
        groups.append(flip_eights(group))
    return jnp.concatenate(groups, axis=0)


SMALL_ROWS = 64


def place_of(index, order):
    total = 0
    for bit in order:
        total = total * 2 + (index // bit) % 2
    return total


def main_kernel(
    groups,
    heads,
    mem_rows,
    orders,
    plan,
    got_ref,
    h_ref,
    g_ref,
    cot_h_ref,
    cot_g_ref,
    target_ref,
    bias_ref,
    info_ref,
    wo_hbm,
    w1_hbm,
    w2_hbm,
    wq_hbm,
    wk_hbm,
    wv_hbm,
    prob_hbm,
    af_hbm,
    q_hbm,
    k_hbm,
    v_hbm,
    rel_hbm,
    out_hbm,
    x_hbm,
    pos_hbm,
    ln1_gain_ref,
    ln1_bias_ref,
    b1_ref,
    b2_ref,
    ln2_gain_ref,
    ln2_bias_ref,
    h_out_ref,
    g_out_ref,
    h_grad_ref,
    g_grad_ref,
    mem_grad_ref,
    head_out_ref,
    w1_out_ref,
    w2_out_ref,
    wo_out_ref,
    small_out_ref,
    late_out_ref,
    wo_ref,
    w1_ref,
    w2_ref,
    attn_ref,
    slope_ref,
    act_ref,
    gpre_ref,
    ffn_all,
    gf_all,
    gb_all,
    b1_s_ref,
    resid_grad_ref,
    prob_ref,
    af_ref,
    q_ref,
    k_ref,
    v_ref,
    rel_ref,
    out_ref,
    ga_ref,
    kv_acc,
    rel_acc,
    dq_ref,
    pack_ref,
    pack_got,
    dq_all,
    dkv_all,
    small_ref,
    small_got,
    late_ref,
    late_got,
    late_all,
    *rest,
):
    jobs_count = len(orders)
    nb = len(orders[0])
    src_refs = rest[:jobs_count]
    recv_refs = [
        rest[jobs_count + k * nb : jobs_count + (k + 1) * nb] for k in range(jobs_count)
    ]
    (
        w1_cut,
        w1_got,
        head_cut,
        head_got,
        w2_cut,
        w2_got,
        wo_cut,
        wo_got,
        load_sem,
        late_load_sem,
        send_sem,
        recv_sem,
        job_send,
        job_recv,
        pack_send,
        pack_recv,
        small_send,
        small_recv,
        end_send,
        end_recv,
    ) = rest[jobs_count + jobs_count * nb :]
    block_id = lax.axis_index("blk")
    group_id = lax.axis_index("dp")
    both, width = attn_ref.shape
    rows = both // 2
    wide = heads * HEAD_DIM
    blocks = act_ref.shape[0]
    part = act_ref.shape[2]
    steps = bits_of(blocks)
    mem_all = mem_rows * blocks
    chunk = mem_rows + both
    pair = mem_rows + rows
    keys = k_ref.shape[1]
    span = rows + keys
    dist_count = rel_ref.shape[1]
    share = width // (groups * blocks)

    def device(i):
        return (group_id, flip(block_id, i))

    held = groups * block_id + group_id
    owner_id = (held // blocks, held % blocks)
    mine = blocks * group_id + block_id
    source_id = (mine % groups, mine // groups)
    moves = held != mine

    loads = [
        pltpu.make_async_copy(src, dst, load_sem.at[k])
        for k, (src, dst) in enumerate(
            (
                (wo_hbm, wo_ref),
                (w1_hbm, w1_ref),
                (w2_hbm, w2_ref),
                (out_hbm, out_ref),
                (af_hbm, af_ref),
                (q_hbm, q_ref),
                (k_hbm, k_ref),
                (v_hbm, v_ref),
                (rel_hbm, rel_ref),
            )
        )
    ]
    prob_loads = [
        pltpu.make_async_copy(prob_hbm.at[h], prob_ref.at[h % 2], load_sem.at[len(loads) + h])
        for h in range(heads)
    ]
    for one in loads[:3]:
        one.start()
    barrier = pltpu.get_barrier_semaphore()
    for i in range(1, blocks):
        pl.semaphore_signal(barrier, inc=1, device_id=device(i), device_id_type=MESH_IDS)
    for bit in orders[0]:
        pl.semaphore_signal(
            barrier, inc=1, device_id=(flip(group_id, bit), block_id), device_id_type=MESH_IDS
        )

    @pl.when(moves)
    def _():
        pl.semaphore_signal(barrier, inc=1, device_id=source_id, device_id_type=MESH_IDS)
        pl.semaphore_wait(barrier, blocks + nb)

    @pl.when(held == mine)
    def _():
        pl.semaphore_wait(barrier, blocks - 1 + nb)

    def remote(src, dst, send, recv, target):
        return pltpu.make_async_remote_copy(
            src_ref=src,
            dst_ref=dst,
            send_sem=send,
            recv_sem=recv,
            device_id=target,
            device_id_type=MESH_IDS,
        )

    def piece_copy(ref, which, hop, come):
        at = come + hop
        return remote(
            ref.at[come], ref.at[at], send_sem.at[which, at], recv_sem.at[which, at], device(hop)
        )

    def spread(ref, which):
        for hop in reversed(steps):
            piece_copy(ref, which, hop, 0).start()

    def near_ready(ref, which):
        for hop in steps[:-1]:
            piece_copy(ref, which, hop, 0).wait_recv()

    def relay(ref, which):
        far = steps[-1]
        piece_copy(ref, which, far, 0).wait_recv()
        for hop in steps[:-1]:
            piece_copy(ref, which, hop, far).start()

    def collect(ref, which):
        for hop in steps[:-1]:
            piece_copy(ref, which, hop, steps[-1]).wait_recv()

    def finish(ref, which):
        for hop in steps:
            piece_copy(ref, which, hop, 0).wait_send()
        for hop in steps[:-1]:
            piece_copy(ref, which, hop, steps[-1]).wait_send()

    def job_source(job, stage):
        return src_refs[job] if stage == 0 else recv_refs[job][stage - 1]

    def job_half(job, stage, own):
        half = groups >> (stage + 1)
        bit = (group_id // orders[job][stage]) % 2
        which = bit if own else 1 - bit
        return pl.ds(which * half, half)

    def job_copy(job, stage):
        return remote(
            job_source(job, stage).at[job_half(job, stage, False)],
            recv_refs[job][stage],
            job_send.at[job, stage],
            job_recv.at[job, stage],
            (flip(group_id, orders[job][stage]), block_id),
        )

    def job_start(job):
        job_copy(job, 0).start()

    def job_next(job, stage):
        job_copy(job, stage).wait_recv()
        keep = job_source(job, stage)[job_half(job, stage, True)]
        into = recv_refs[job][stage]
        total = keep.astype(F32) + into[...].astype(F32)
        if stage < nb - 1:
            into[...] = total.astype(BF16)
            job_copy(job, stage + 1).start()
            return None
        return total[0]

    def job_done(job):
        for stage in range(nb):
            job_copy(job, stage).wait_send()

    def cut_copy(cut, got, which, i):
        return remote(
            cut.at[i], got.at[i], end_send.at[which, i], end_recv.at[which, i], device(i)
        )

    def cut_start(cut, first, values):
        low = values.astype(BF16)
        for k in range(blocks):
            at = mix(block_id, k, blocks)
            cut[at, :, first : first + values.shape[1]] = low[k * share : (k + 1) * share]

    def cut_send(cut, got, which):
        for i in range(1, blocks):
            cut_copy(cut, got, which, i).start()

    def owner_copy(cut, got, which):
        return remote(cut, got, end_send.at[which, 0], end_recv.at[which, 0], owner_id)

    def owner_send(cut, got, which):
        @pl.when(moves)
        def _():
            owner_copy(cut, got, which).start()

        @pl.when(held == mine)
        def _():
            got[...] = cut[...]

    def owner_wait(cut, got, which):
        @pl.when(moves)
        def _():
            owner_copy(cut, got, which).wait()

    for block in range(blocks):

        @pl.when(block_id == block)
        def _(block=block):
            for i in range(blocks):
                at = (block ^ i) * wide
                attn_ref[:, at : at + wide] = got_ref[i]
            b1_s_ref[0:1, :] = row_of(b1_ref.at[pl.ds(block * part // 128, part // 128)])

    small_ref[0] = jnp.zeros(small_ref.shape[1:], F32)
    target = jnp.broadcast_to(target_ref[...].astype(F32), (8, rows)).T[:, 0:1]
    weight = jnp.concatenate([jnp.ones((rows, 1), F32), target], axis=0)

    def squares(values):
        weighted = jnp.sum(values * values, axis=1, keepdims=True) * weight
        return column_sum(weighted[:rows]), column_sum(weighted[rows:])

    loads[0].wait()
    branch = dot_nn(attn_ref[...], wo_ref[...])
    att_stat = squares(branch)
    streams = jnp.concatenate([h_ref[...], g_ref[...]], axis=0).astype(F32)
    unit_one, rate_one = norm_parts(branch + streams)
    gain_one = row_of(ln1_gain_ref)
    out_one = unit_one * gain_one + row_of(ln1_bias_ref)
    ffn_all[0] = out_one.astype(BF16)
    spread(ffn_all, 0)
    loads[1].wait()
    loads[2].wait()
    for one in loads[3:] + prob_loads[:2]:
        one.start()
    branch_ffn = row_of(b2_ref)
    for c in range(blocks):
        at = slice(c * part, (c + 1) * part)
        rows_at = b1_ref.at[pl.ds(c * part // 128, part // 128)]
        act, slope = gelu_pair(dot_nn(ffn_all[0], w1_ref[:, at]) + row_of(rows_at))
        slope_ref[:, at] = slope
        act_ref[c] = act.astype(BF16)
        branch_ffn = branch_ffn + dot_nn(act_ref[c], w2_ref[at, :])
    ffn_stat = squares(branch_ffn)
    unit_two, rate_two = norm_parts(branch_ffn + out_one)
    gain_two = row_of(ln2_gain_ref)
    out_two = unit_two * gain_two + row_of(ln2_bias_ref)
    out_stat = squares(out_two)
    h_out_ref[...] = out_two[:rows].astype(BF16)
    g_out_ref[...] = out_two[rows:].astype(BF16)
    cot = jnp.concatenate([cot_h_ref[...], cot_g_ref[...]], axis=0).astype(F32)
    grad_two = norm_back(unit_two, rate_two, cot * gain_two)
    grad_ffn = grad_two.astype(BF16)
    gf_all[0] = grad_ffn
    spread(gf_all, 1)
    relay(ffn_all, 0)
    tall = width // 128
    tall_part = part // 128
    stat_row = 5 * tall + blocks * tall_part
    early = small_ref.at[0]
    put_row(early, 0, column_sum(cot * unit_two))
    put_row(early, tall, column_sum(cot))
    put_row(early, 2 * tall, column_sum(grad_ffn.astype(F32)))
    grad_out_one = grad_two
    for c in range(blocks):
        at = slice(c * part, (c + 1) * part)
        grad_pre = (dot_nt(gf_all[0], w2_ref[at, :]) * slope_ref[:, at]).astype(BF16)
        gpre_ref[c] = grad_pre
        put_row(early, 5 * tall + c * tall_part, column_sum(grad_pre.astype(F32)))
        grad_out_one = grad_out_one + dot_nt(grad_pre, w1_ref[:, at])
    put_row(early, 3 * tall, column_sum(grad_out_one * unit_one))
    put_row(early, 4 * tall, column_sum(grad_out_one))
    grad_one = norm_back(unit_one, rate_one, grad_out_one * gain_one)
    resid_grad_ref[...] = grad_one
    gb_all[0] = grad_one.astype(BF16)
    spread(gb_all, 2)
    lane = lax.broadcasted_iota(jnp.int32, (1, 128), 1)
    stats = jnp.zeros((1, 128), F32)
    terms = [att_stat[0], ffn_stat[0], out_stat[0], att_stat[1], ffn_stat[1], out_stat[1]]
    terms += [jnp.full((1, 1), float(rows), F32), column_sum(target)]
    for k, term in enumerate(terms):
        stats = jnp.where(lane == k, term, stats)
    early[stat_row : stat_row + 1, :] = stats

    small_steps = [("blk", bit) for bit in steps] + [("dp", bit) for bit in bits_of(groups)]

    def small_copy(k):
        axis, bit = small_steps[k]
        target_id = device(bit) if axis == "blk" else (flip(group_id, bit), block_id)
        return remote(
            small_ref.at[k], small_got.at[k], small_send.at[k], small_recv.at[k], target_id
        )

    def small_next(k):
        small_copy(k).wait_recv()
        small_ref[k + 1] = small_ref[k] + small_got[k]
        if k + 1 < len(small_steps):
            small_copy(k + 1).start()

    small_copy(0).start()

    def late_copy(k, i=0):
        bits = bits_of(groups)
        if k < nb:
            return remote(
                late_ref.at[k],
                late_got.at[k],
                small_send.at[8 + k],
                small_recv.at[8 + k],
                (flip(group_id, bits[k]), block_id),
            )
        return remote(
            late_ref.at[nb],
            late_all.at[i],
            small_send.at[8 + nb + i],
            small_recv.at[8 + nb + i],
            device(i),
        )

    def late_next(k):
        late_copy(k).wait_recv()
        late_ref[k + 1] = late_ref[k] + late_got[k]
        if k + 1 < nb:
            late_copy(k + 1).start()
        else:
            for i in range(1, blocks):
                late_copy(nb, i).start()

    x_rows = blocks * chunk

    def x_part(i, first, count):
        base = mix(block_id, i, blocks) * chunk + first
        return w2_ref[pl.ds(pl.multiple_of(base, 32), count), :]

    done = set()

    def job_event(job, stage):
        value = job_next(job, stage)
        if stage < nb - 1:
            return
        done.add(job)
        if job < 2:
            w2_cut[:, job * (width // 2) : (job + 1) * (width // 2)] = value.astype(BF16)
            if {0, 1} <= done:
                owner_send(w2_cut, w2_got, 2)
        elif job < 4:
            cut_start(w1_cut, (job - 2) * (part // 2), value)
            if {2, 3} <= done:
                cut_send(w1_cut, w1_got, 0)
        elif job == 4:
            wo_cut[...] = value.astype(BF16)
            owner_send(wo_cut, wo_got, 3)
        else:
            cut_start(head_cut.at[job - 5], 0, value)
            cut_send(head_cut.at[job - 5], head_got.at[job - 5], 4 + job - 5)

    def happen(spot):
        for kind, first, *more in plan.get(spot, ()):
            if kind == "job":
                job_event(first, *more)
            elif kind == "small":
                small_next(first)
            else:
                late_next(first)

    own_at = pl.ds(pl.multiple_of(block_id * part, 128), part)
    act_ref[0] = act_ref[block_id]
    gpre_ref[0] = gpre_ref[block_id]
    near_ready(ffn_all, 0)
    collect(ffn_all, 0)
    for i in range(1, blocks):
        act, slope = gelu_pair(dot_nn(ffn_all[i], w1_ref[:, own_at]) + b1_s_ref[0:1, :])
        act_ref[i] = act.astype(BF16)
        slope_ref[:, (i - 1) * part : i * part] = slope

    def slice_back(i):
        grad_pre = dot_nt(gf_all[i], w2_ref[own_at, :]) * slope_ref[:, (i - 1) * part : i * part]
        gpre_ref[i] = grad_pre.astype(BF16)

    near_ready(gf_all, 1)
    for i in steps[:-1]:
        slice_back(i)
    relay(gf_all, 1)
    slice_back(steps[-1])
    collect(gf_all, 1)
    for i in range(1, blocks):
        if i not in steps:
            slice_back(i)

    def flat(ref):
        return ref[...].reshape(blocks * both, ref.shape[2])

    def put_shares(first, count, values):
        tall_share = values.shape[0] // groups
        lanes_here = values.shape[1] // count
        low = values.astype(BF16)
        for k in range(count):
            for d in range(groups):
                src_refs[first + k][place_of(d, orders[first + k])] = low[
                    d * tall_share : (d + 1) * tall_share,
                    k * lanes_here : (k + 1) * lanes_here,
                ]
            job_start(first + k)

    put_shares(0, 2, dot_tn(flat(act_ref), flat(gf_all)))
    put_shares(2, 2, dot_tn(flat(ffn_all), flat(gpre_ref)))
    happen("ffn")

    late_loads = [
        pltpu.make_async_copy(x_hbm.at[i], w2_ref.at[pl.ds(i * chunk, chunk)], late_load_sem.at[i])
        for i in range(blocks)
    ]
    late_loads.append(
        pltpu.make_async_copy(
            pos_hbm, w2_ref.at[pl.ds(x_rows, dist_count)], late_load_sem.at[blocks]
        )
    )
    for k, src in enumerate((wq_hbm, wk_hbm, wv_hbm)):
        late_loads.append(
            pltpu.make_async_copy(
                src, w1_ref.at[:, k * width : (k + 1) * width], late_load_sem.at[blocks + 1 + k]
            )
        )
    for one in late_loads:
        one.start()

    near_ready(gb_all, 2)
    relay(gb_all, 2)
    for one in loads[3:]:
        one.wait()
    wo_own = wo_ref[pl.ds(pl.multiple_of(block_id * wide, HEAD_DIM), wide), :]
    kv_acc[...] = jnp.zeros_like(kv_acc)
    rel_acc[...] = jnp.zeros_like(rel_acc)
    late_ref[0] = jnp.zeros(late_ref.shape[1:], F32)
    collect(gb_all, 2)
    for i in range(blocks):
        ga_ref[i] = dot_nt(gb_all[i], wo_own).astype(BF16)
    put_shares(4, 1, sum(dot_tn(out_ref[i], gb_all[i]) for i in range(blocks)))
    happen("pre")

    def pack_copy(h, i):
        return remote(
            pack_ref.at[h, i], pack_got.at[h, i], pack_send.at[h, i], pack_recv.at[h, i], device(i)
        )


    for h in range(heads):
        own = slice(h * HEAD_DIM, (h + 1) * HEAD_DIM)

        def tile(piece, carry, h=h, own=own):
            for slot in range(blocks):
                if plan.get((h, slot)):

                    @pl.when(piece == slot)
                    def _(slot=slot):
                        happen((h, slot))

            owner = mix(block_id, piece, blocks)
            tok_at = pl.ds(pl.multiple_of(owner * rows, 32), rows)
            rel_start = pl.multiple_of((blocks - 1) * rows - owner * rows, 128)
            rel_at = pl.ds(rel_start, span)
            seg = info_ref[tok_at, 1:2]
            seg = jnp.concatenate([seg, seg], axis=0)
            raw = q_ref[piece, :, own]
            q_word = (raw + bias_ref[0:1, own]).astype(BF16)
            q_rel = (raw + bias_ref[1:2, own]).astype(BF16)
            q_seg = raw + bias_ref[2:3, own]
            embed = bias_ref[3:5, own]
            ga = ga_ref[piece, :, own]
            probs = prob_ref[h % 2, piece]
            ga_f = ga.astype(F32) * SCALE
            row_dot = jnp.sum(ga_f * af_ref[piece, :, own], axis=1, keepdims=True)
            grad_prob = dot_nt(ga_f.astype(BF16), v_ref[h])
            grad_score = probs.astype(F32) * (grad_prob - row_dot)
            grad_low = grad_score.astype(BF16)
            wide_word = dot_nn(grad_low, k_ref[h])
            grad_word = wide_word[:, :HEAD_DIM]
            total = wide_word[:, HEAD_DIM : HEAD_DIM + 1]
            ones = wide_word[:, HEAD_DIM + 2 : HEAD_DIM + 3]
            differ = ones + seg * (total - 2.0 * ones)
            same = total - differ
            grad_seg = same * embed[0:1] + differ * embed[1:2]
            wind = jnp.concatenate(
                [
                    spread_rows(grad_score[:rows], rows, keys),
                    spread_rows(grad_score[rows:], rows, keys),
                ],
                axis=0,
            ).astype(BF16)
            grad_rel = dot_nn(wind, rel_ref[h, rel_at, :])
            kv_acc[h, :HEAD_DIM] += dot_tn(q_word, grad_low)
            kv_acc[h, HEAD_DIM:] += dot_tn(ga, probs)
            rel_acc[h, :, rel_at] += dot_tn(q_rel, wind)
            grad_q = (grad_word + grad_rel + grad_seg).astype(BF16)
            dq_ref[piece, :, own] = grad_q
            pack_ref[h, piece, :rows, :HEAD_DIM] = grad_q[:rows]
            pack_ref[h, piece, :rows, HEAD_DIM:] = grad_q[rows:]
            late_ref[0, :, own] += jnp.concatenate(
                [
                    column_sum(grad_word),
                    column_sum(grad_rel),
                    column_sum(grad_seg),
                    column_sum(same * q_seg),
                    column_sum(differ * q_seg),
                    jnp.zeros((3, HEAD_DIM), F32),
                ],
                axis=0,
            )
            return carry

        prob_loads[h].wait()
        lax.fori_loop(0, blocks, tile, 0)
        if h + 2 < heads:
            prob_loads[h + 2].start()
        full = kv_acc[h].T.astype(BF16)
        for k in range(blocks):
            at = mix(block_id, k, blocks)
            mem_part = full[k * mem_rows : (k + 1) * mem_rows]
            tok_part = full[mem_all + k * rows : mem_all + (k + 1) * rows]
            pack_ref[h, at, rows : rows + mem_rows, :] = mem_part
            pack_ref[h, at, rows + mem_rows :, :] = tok_part
        for i in range(blocks - 1, 0, -1):
            pack_copy(h, i).start()
        if h == heads - 1:
            late_copy(0).start()
        happen(("packed", h))
        if h == 0:
            for one in late_loads:
                one.wait()
        grad_wr = dot_tn(w2_ref[x_rows : x_rows + dist_count, :], rel_acc[h].T.astype(BF16))
        grad_wq = sum(dot_tn(x_part(i, mem_rows, both), dq_ref[i, :, own]) for i in range(blocks))
        grad_wkv = sum(
            dot_tn(x_part(i, 0, pair), pack_ref[h, i, rows:, :]) for i in range(blocks)
        )
        put_shares(5 + h, 1, jnp.concatenate([grad_wr, grad_wq, grad_wkv], axis=1))
        happen(("head", h))

    happen("tail")

    for h in range(heads - 1):
        for i in range(1, blocks):
            pack_copy(h, i).wait_recv()
    happen("pack")
    for i in range(1, blocks):
        pack_copy(heads - 1, i).wait_recv()
    for block in range(blocks):

        @pl.when(block_id == block)
        def _(block=block):
            for h in range(heads):
                for i in range(blocks):
                    at = (block ^ i) * wide + h * HEAD_DIM
                    to = slice(at, at + HEAD_DIM)
                    piece = pack_ref[h, 0] if i == 0 else pack_got[h, i]
                    dq_all[:rows, to] = piece[:rows, :HEAD_DIM]
                    dq_all[rows:, to] = piece[:rows, HEAD_DIM:]
                    dkv_all[:, to] = piece[rows:, :HEAD_DIM]
                    dkv_all[:, width + at : width + at + HEAD_DIM] = piece[rows:, HEAD_DIM:]

    grad_rows = dot_nt(dkv_all[:, :width], w1_ref[:, width : 2 * width]) + dot_nt(
        dkv_all[:, width:], w1_ref[:, 2 * width : 3 * width]
    )
    grad_streams = resid_grad_ref[...] + dot_nt(dq_all[...], w1_ref[:, :width])
    h_grad_ref[...] = grad_streams[:rows] + grad_rows[mem_rows:]
    g_grad_ref[...] = grad_streams[rows:]
    mem_grad_ref[...] = grad_rows[:mem_rows]

    happen("end")
    owner_wait(w2_cut, w2_got, 2)
    owner_wait(wo_cut, wo_got, 3)
    w2_out_ref[...] = w2_got[...]
    wo_out_ref[...] = wo_got[...]
    w1_out_ref[0] = w1_cut[0]
    for i in range(1, blocks):
        cut_copy(w1_cut, w1_got, 0, i).wait()
        w1_out_ref[i] = w1_got[i]
    for h in range(heads):
        head_out_ref[h, 0] = head_cut[h, 0]
        for i in range(1, blocks):
            cut_copy(head_cut.at[h], head_got.at[h], 4 + h, i).wait()
            head_out_ref[h, i] = head_got[h, i]

    small_out_ref[...] = small_ref[len(small_steps)]
    for i in range(1, blocks):
        late_copy(nb, i).wait()
        late_out_ref[i] = late_all[i]
    late_out_ref[0] = late_ref[nb]

    for k in range(len(small_steps)):
        small_copy(k).wait_send()
    for k in range(nb):
        late_copy(k).wait_send()
    for h in range(heads):
        for i in range(1, blocks):
            pack_copy(h, i).wait_send()
    for job in range(jobs_count):
        job_done(job)
    for which, ref in enumerate((ffn_all, gf_all, gb_all)):
        finish(ref, which)


def finish_kernel(
    heads,
    h_ref,
    g_ref,
    h_grad_ref,
    g_grad_ref,
    mem_grad_ref,
    head_ref,
    w1_ref,
    w2_ref,
    wo_ref,
    small_ref,
    late_ref,
    h_out_ref,
    g_out_ref,
    h_grad_out_ref,
    g_grad_out_ref,
    mem_grad_out_ref,
    wq_out_ref,
    wk_out_ref,
    wv_out_ref,
    wr_out_ref,
    wo_out_ref,
    w1_out_ref,
    w2_out_ref,
    rw_out_ref,
    rr_out_ref,
    rs_out_ref,
    embed_out_ref,
    ln1_gain_out_ref,
    ln1_bias_out_ref,
    b1_out_ref,
    b2_out_ref,
    ln2_gain_out_ref,
    ln2_bias_out_ref,
    rms_out_ref,
    rows_ref,
):
    block_id = lax.axis_index("blk")
    blocks, share, part = w1_ref.shape
    width = h_ref.shape[1]
    wide = heads * HEAD_DIM
    tall = width // 128
    tall_part = part // 128
    stat_row = 5 * tall + blocks * tall_part

    def put_lanes(out, values, stride, first):
        count = values.shape[0]
        for j in range(values.shape[1] // 128):
            out[pl.ds(first + j, count, stride=stride), :] = values[:, 128 * j : 128 * (j + 1)]

    h_out_ref[...] = h_ref[...]
    g_out_ref[...] = g_ref[...]
    h_grad_out_ref[...] = h_grad_ref[...]
    g_grad_out_ref[...] = g_grad_ref[...]
    mem_grad_out_ref[...] = mem_grad_ref[...]
    put_lanes(w2_out_ref, w2_ref[...].astype(F32), tall, 0)
    put_lanes(wo_out_ref, wo_ref[...].astype(F32), tall, 0)
    for i in range(blocks):
        first = mix(block_id, i, blocks) * tall_part
        put_lanes(w1_out_ref, w1_ref[i].astype(F32), blocks * tall_part, first)
    for block in range(blocks):

        @pl.when(block_id == block)
        def _(block=block):
            for i in range(blocks):
                at = slice((block ^ i) * wide, ((block ^ i) + 1) * wide)
                for h in range(heads):
                    first = (block ^ i) * wide + h * HEAD_DIM
                    for k in range(4):
                        rows_ref[k, :share, first : first + HEAD_DIM] = head_ref[
                            h, i, :, k * HEAD_DIM : (k + 1) * HEAD_DIM
                        ].astype(F32)
                rows_ref[4, :8, at] = late_ref[i]

    for k, out in enumerate((wr_out_ref, wq_out_ref, wk_out_ref, wv_out_ref)):
        put_lanes(out, rows_ref[k, :share, :], tall, 0)
    put_row(rw_out_ref, 0, rows_ref[4, 0:1, :])
    put_row(rr_out_ref, 0, rows_ref[4, 1:2, :])
    put_row(rs_out_ref, 0, rows_ref[4, 2:3, :])
    embed_out_ref[...] = rows_ref[4, 3:5, :]
    ln2_gain_out_ref[...] = small_ref[:tall]
    ln2_bias_out_ref[...] = small_ref[tall : 2 * tall]
    b2_out_ref[...] = small_ref[2 * tall : 3 * tall]
    ln1_gain_out_ref[...] = small_ref[3 * tall : 4 * tall]
    ln1_bias_out_ref[...] = small_ref[4 * tall : 5 * tall]
    b1_out_ref[...] = small_ref[5 * tall : stat_row]
    stats = small_ref[stat_row : stat_row + 1]
    lane = lax.broadcasted_iota(jnp.int32, (1, 128), 1)
    counts = jnp.where(lane < 3, stats[:, 6:7], stats[:, 7:8]) * float(width)
    rms_out_ref[...] = jnp.sqrt(stats / counts)


def exchange_plan(groups, blocks, heads):
    near = tuple(bits_of(groups))
    jobs = 5 + heads
    smalls = len(near) + len(bits_of(blocks))
    if (groups, blocks, heads) == (8, 4, 3):
        orders = (
            (1, 2, 4),
            (1, 2, 4),
            (2, 4, 1),
            (2, 4, 1),
            (1, 2, 4),
            (2, 4, 1),
            (1, 2, 4),
            (1, 2, 4),
        )
        plan = {
            "ffn": [("small", 0)],
            "pre": [("small", 1), ("job", 0, 0)],
            (0, 2): [("job", 2, 0), ("small", 2)],
            ("packed", 0): [("job", 1, 0), ("small", 3)],
            ("head", 0): [("job", 3, 0), ("job", 4, 0), ("small", 4)],
            (1, 1): [("job", 0, 1)],
            ("head", 1): [("job", 1, 1), ("job", 2, 1)],
            (2, 2): [("job", 5, 0)],
            ("head", 2): [("job", 6, 0), ("job", 4, 1), ("job", 2, 2), ("late", 0), ("job", 3, 1)],
            "end": [("late", 1), ("job", 0, 2), ("job", 1, 2), ("job", 7, 0), ("job", 3, 2), ("late", 2), ("job", 6, 1), ("job", 5, 1), ("job", 4, 2), ("job", 7, 1), ("job", 5, 2), ("job", 6, 2), ("job", 7, 2)],
        }
        return orders, plan
    plan = {"end": [("job", job, stage) for stage in range(len(near)) for job in range(jobs)]}
    plan["end"] += [("small", k) for k in range(smalls)] + [("late", k) for k in range(len(near))]
    return (near,) * jobs, plan


def whole(shape):
    return pl.BlockSpec(shape, lambda *_: (0,) * len(shape))


def local(
    h_in,
    g_in,
    memory,
    cot_h,
    cot_g,
    perm_order,
    target,
    segment,
    mem_flag,
    w_q,
    w_k,
    w_v,
    w_r,
    w_o,
    r_w_bias,
    r_r_bias,
    r_s_bias,
    seg_embed,
    ln1_gain,
    ln1_bias,
    w_1,
    b_1,
    w_2,
    b_2,
    ln2_gain,
    ln2_bias,
):
    _, rows, width = h_in.shape
    mem_rows = memory.shape[1]
    hidden = w_1.shape[1]
    blocks = lax.axis_size("blk")
    groups = lax.axis_size("dp")
    tok_all = rows * blocks
    mem_all = mem_rows * blocks
    keys = mem_all + tok_all
    dist_count = tok_all + keys
    heads = HEADS // blocks
    wide = heads * HEAD_DIM
    both = 2 * rows
    chunk = mem_rows + both
    pair = mem_rows + rows
    part = hidden // blocks
    tall = width // 128
    share = width // (groups * blocks)
    nb = len(bits_of(groups))
    hbm = pl.BlockSpec(memory_space=pltpu.HBM)
    vmem = pl.BlockSpec(memory_space=pltpu.VMEM)
    shape = jax.ShapeDtypeStruct

    def lanes(values):
        return values.reshape(-1, 128)

    coarse, fine = position_units(keys - 1, dist_count, width, 32)
    (
        probs, attn_f, q_raw, k_aug, v_all, rel_heads, got_out, attn_out, x_all, pos_table,
        query_info, biases,
    ) = pl.pallas_call(
        functools.partial(attn_fwd_kernel, heads, rows, mem_rows, blocks),
        name="attn_fwd",
        grid=(blocks,),
        in_specs=[hbm] * 3
        + [whole((1, rows))] * 3
        + [pl.BlockSpec(memory_space=pltpu.SMEM)]
        + [whole((width, width))] * 4
        + [whole((tall, 128))] * 3
        + [whole((2, width)), whole(coarse.shape), whole(fine.shape)],
        out_specs=[
            pl.BlockSpec((heads, 1, both, keys), lambda s: (0, blocks - 1 - s, 0, 0)),
            pl.BlockSpec((1, both, wide), lambda s: (blocks - 1 - s, 0, 0)),
            hbm,
            hbm,
            hbm,
            hbm,
            whole((blocks, both, wide)),
            hbm,
            hbm,
            hbm,
            whole((tok_all, 8)),
            whole((8, wide)),
        ],
        out_shape=[
            shape((heads, blocks, both, keys), BF16),
            shape((blocks, both, wide), F32),
            shape((blocks, both, wide), F32),
            shape((heads, keys, 2 * HEAD_DIM), BF16),
            shape((heads, keys, HEAD_DIM), BF16),
            shape((heads, dist_count, HEAD_DIM), BF16),
            shape((blocks, both, wide), BF16),
            shape((blocks, both, wide), BF16),
            shape((blocks, chunk, width), BF16),
            shape((dist_count, width), BF16),
            shape((tok_all, 8), F32),
            shape((8, wide), F32),
        ],
        scratch_shapes=[
            pltpu.VMEM((width, 3 * wide), BF16),
            pltpu.VMEM((width, wide), BF16),
            pltpu.VMEM((both, keys), F32),
            pltpu.VMEM((blocks, 3, 1, rows), jnp.int32),
            pltpu.VMEM((blocks, chunk, width), BF16),
            pltpu.VMEM((blocks, both, wide), BF16),
            pltpu.VMEM((blocks, both, wide), BF16),
            pltpu.VMEM((blocks, both, wide), F32),
            pltpu.VMEM((heads, keys, 2 * HEAD_DIM), BF16),
            pltpu.VMEM((heads, keys, HEAD_DIM), BF16),
            pltpu.VMEM((heads, dist_count, HEAD_DIM), BF16),
            pltpu.VMEM((dist_count, width), BF16),
            pltpu.VMEM((8, keys), F32),
            pltpu.SemaphoreType.DMA((blocks, 3)),
            pltpu.SemaphoreType.DMA((blocks, 3)),
            pltpu.SemaphoreType.DMA((blocks, 3)),
            pltpu.SemaphoreType.DMA((blocks, 3)),
            pltpu.SemaphoreType.DMA((blocks,)),
            pltpu.SemaphoreType.DMA((blocks,)),
            pltpu.SemaphoreType.DMA((6,)),
            pltpu.SemaphoreType.DMA((7,)),
        ],
        compiler_params=pltpu.CompilerParams(
            vmem_limit_bytes=60 << 20, collective_id=0, has_side_effects=True
        ),
    )(
        memory[0], h_in[0], g_in[0], perm_order, target, segment, mem_flag, w_q, w_k, w_v, w_r,
        lanes(r_w_bias), lanes(r_r_bias), lanes(r_s_bias), seg_embed, coarse, fine,
    )

    near = tuple(bits_of(groups))
    orders, plan = exchange_plan(groups, blocks, heads)
    job_shapes = (
        [(part // groups, width // 2)] * 2
        + [(width // groups, part // 2)] * 2
        + [(wide // groups, width)]
        + [(width // groups, 4 * HEAD_DIM)] * heads
    )
    sources = [pltpu.VMEM((groups,) + one, BF16) for one in job_shapes]
    receivers = [
        pltpu.VMEM((groups >> (k + 1),) + one, BF16) for one in job_shapes for k in range(nb)
    ]
    bits = len(bits_of(blocks)) + nb
    square = width * width // (groups * blocks * 128)
    oblong = width * hidden // (groups * blocks * 128)
    grads_shape = [
        shape((rows, width), BF16),
        shape((rows, width), BF16),
        shape((rows, width), F32),
        shape((rows, width), F32),
        shape((mem_rows, width), F32),
    ]
    parts = pl.pallas_call(
        functools.partial(main_kernel, groups, heads, mem_rows, orders, plan),
        name="main",
        in_specs=[vmem] * 8 + [hbm] * 15 + [vmem] * 6,
        out_specs=[vmem] * 11,
        out_shape=grads_shape
        + [
            shape((heads, blocks, share, 4 * HEAD_DIM), BF16),
            shape((blocks, share, part), BF16),
            shape((part // groups, width), BF16),
            shape((wide // groups, width), BF16),
            shape((SMALL_ROWS, 128), F32),
            shape((blocks, 8, wide), F32),
        ],
        scratch_shapes=[
            pltpu.VMEM((width, width), BF16),
            pltpu.VMEM((width, hidden), BF16),
            pltpu.VMEM((hidden, width), BF16),
            pltpu.VMEM((both, width), BF16),
            pltpu.VMEM((both, hidden), F32),
            pltpu.VMEM((blocks, both, part), BF16),
            pltpu.VMEM((blocks, both, part), BF16),
            pltpu.VMEM((blocks, both, width), BF16),
            pltpu.VMEM((blocks, both, width), BF16),
            pltpu.VMEM((blocks, both, width), BF16),
            pltpu.VMEM((8, part), F32),
            pltpu.VMEM((both, width), F32),
            pltpu.VMEM((2, blocks, both, keys), BF16),
            pltpu.VMEM((blocks, both, wide), F32),
            pltpu.VMEM((blocks, both, wide), F32),
            pltpu.VMEM((heads, keys, 2 * HEAD_DIM), BF16),
            pltpu.VMEM((heads, keys, HEAD_DIM), BF16),
            pltpu.VMEM((heads, dist_count, HEAD_DIM), BF16),
            pltpu.VMEM((blocks, both, wide), BF16),
            pltpu.VMEM((blocks, both, wide), BF16),
            pltpu.VMEM((heads, 2 * HEAD_DIM, keys), F32),
            pltpu.VMEM((heads, HEAD_DIM, dist_count), F32),
            pltpu.VMEM((blocks, both, wide), BF16),
            pltpu.VMEM((heads, blocks, rows + pair, 2 * HEAD_DIM), BF16),
            pltpu.VMEM((heads, blocks, rows + pair, 2 * HEAD_DIM), BF16),
            pltpu.VMEM((both, width), BF16),
            pltpu.VMEM((pair, 2 * width), BF16),
            pltpu.VMEM((bits + 1, SMALL_ROWS, 128), F32),
            pltpu.VMEM((bits, SMALL_ROWS, 128), F32),
            pltpu.VMEM((nb + 1, 8, wide), F32),
            pltpu.VMEM((nb, 8, wide), F32),
            pltpu.VMEM((blocks, 8, wide), F32),
        ]
        + sources
        + receivers
        + [
            pltpu.VMEM((blocks, share, part), BF16),
            pltpu.VMEM((blocks, share, part), BF16),
            pltpu.VMEM((heads, blocks, share, 4 * HEAD_DIM), BF16),
            pltpu.VMEM((heads, blocks, share, 4 * HEAD_DIM), BF16),
            pltpu.VMEM((part // groups, width), BF16),
            pltpu.VMEM((part // groups, width), BF16),
            pltpu.VMEM((wide // groups, width), BF16),
            pltpu.VMEM((wide // groups, width), BF16),
            pltpu.SemaphoreType.DMA((9 + heads,)),
            pltpu.SemaphoreType.DMA((blocks + 4,)),
            pltpu.SemaphoreType.DMA((3, blocks)),
            pltpu.SemaphoreType.DMA((3, blocks)),
            pltpu.SemaphoreType.DMA((len(job_shapes), nb)),
            pltpu.SemaphoreType.DMA((len(job_shapes), nb)),
            pltpu.SemaphoreType.DMA((heads, blocks)),
            pltpu.SemaphoreType.DMA((heads, blocks)),
            pltpu.SemaphoreType.DMA((8 + nb + blocks,)),
            pltpu.SemaphoreType.DMA((8 + nb + blocks,)),
            pltpu.SemaphoreType.DMA((4 + heads, blocks)),
            pltpu.SemaphoreType.DMA((4 + heads, blocks)),
        ],
        compiler_params=pltpu.CompilerParams(
            vmem_limit_bytes=60 << 20, collective_id=1, has_side_effects=True
        ),
    )(
        got_out, h_in[0], g_in[0], cot_h[0], cot_g[0], target, biases, query_info,
        w_o, w_1, w_2, w_q, w_k, w_v, probs, attn_f, q_raw, k_aug, v_all, rel_heads, attn_out,
        x_all, pos_table,
        lanes(ln1_gain), lanes(ln1_bias), lanes(b_1), lanes(b_2), lanes(ln2_gain), lanes(ln2_bias),
    )
    outs = pl.pallas_call(
        functools.partial(finish_kernel, heads),
        name="finish",
        in_specs=[vmem] * 11,
        out_specs=[vmem] * 23,
        out_shape=grads_shape
        + [shape((square, 128), F32)] * 5
        + [shape((oblong, 128), F32)] * 2
        + [shape((tall, 128), F32)] * 3
        + [shape((2, width), F32)]
        + [shape((tall, 128), F32)] * 2
        + [shape((hidden // 128, 128), F32)]
        + [shape((tall, 128), F32)] * 3
        + [shape((1, 128), F32)],
        scratch_shapes=[pltpu.VMEM((5, max(8, share), width), F32)],
        compiler_params=pltpu.CompilerParams(vmem_limit_bytes=60 << 20),
    )(*parts)
    outs = list(outs)
    for k in range(5):
        outs[k] = outs[k][None]
    for k in list(range(5, 15)) + list(range(16, 22)):
        outs[k] = outs[k].reshape(-1)
    outs[22] = outs[22][0, :6]
    return tuple(outs)


def solution(mesh):
    rows = P("dp", "blk", None)
    ints = P("dp", "blk")
    flat = P(("dp", "blk"))
    return jax.shard_map(
        local,
        mesh=mesh,
        in_specs=(rows,) * 5 + (ints,) * 3 + (P("dp"),) + (P(),) * 17,
        out_specs=(rows,) * 5 + (flat,) * 7 + (P(),) * 11,
        check_vma=False,
    )
```

```python
import functools
import math

import jax
import jax.numpy as jnp
import numpy as np
from jax import lax
from jax.experimental import pallas as pl
from jax.experimental.pallas import tpu as pltpu
from jax.sharding import PartitionSpec as P

HEADS = 12
HEAD_DIM = 64
EPSILON = 1e-12
NEGATIVE = -1e30
SCALE = 1.0 / math.sqrt(HEAD_DIM)
F32 = jnp.float32
BF16 = jnp.bfloat16
MESH_IDS = pl.DeviceIdType.MESH


def position_units(top, dist_count, model_width, unit):
    freq = np.exp(np.arange(model_width // 2) * (-2.0 * math.log(10000.0) / model_width))
    coarse = (top - unit * np.arange(dist_count // unit))[:, None] * freq[None, :]
    fine = np.arange(unit)[:, None] * freq[None, :]
    return tuple(
        np.stack([np.sin(angle), np.cos(angle)]).astype(np.float32) for angle in (coarse, fine)
    )


def dot_nn(left, right):
    return lax.dot_general(left, right, (((1,), (0,)), ((), ())), preferred_element_type=F32)


def dot_nt(left, right):
    return lax.dot_general(left, right, (((1,), (1,)), ((), ())), preferred_element_type=F32)


def dot_tn(left, right):
    return lax.dot_general(left, right, (((0,), (0,)), ((), ())), preferred_element_type=F32)


def bits_of(count):
    return [1 << k for k in range(count.bit_length() - 1)]


def seg_columns(q_seg, embed):
    return (
        jnp.sum(q_seg * embed[0:1], axis=1, keepdims=True),
        jnp.sum(q_seg * embed[1:2], axis=1, keepdims=True),
    )


def flip(index, step):
    for bit in (1 << k for k in range(step.bit_length())):
        if step & bit:
            index = index + bit - 2 * bit * ((index // bit) % 2)
    return index


def mix(index, other, blocks):
    total = 0
    for bit in bits_of(blocks):
        left = (index // bit) % 2
        right = (other // bit) % 2
        total = total + bit * (left + right - 2 * left * right)
    return total


def row_of(ref):
    return jnp.concatenate([ref[j : j + 1, :] for j in range(ref.shape[0])], axis=1)


def put_row(ref, at, values):
    for j in range(values.shape[1] // 128):
        ref[at + j : at + j + 1, :] = values[:, 128 * j : 128 * (j + 1)]


def row_mean(values):
    return jnp.mean(values, axis=1, keepdims=True)


def norm_parts(values):
    center = values - row_mean(values)
    rate = lax.rsqrt(row_mean(center * center) + EPSILON)
    return center * rate, rate


def norm_back(unit, rate, scaled):
    return rate * (scaled - row_mean(scaled) - unit * row_mean(scaled * unit))


def gelu_pair(values):
    square = values * values
    inner = math.sqrt(2.0 / math.pi) * values * (1.0 + 0.044715 * square)
    bend = jnp.tanh(inner)
    half = 0.5 * (1.0 + bend)
    slope = half + values * (1.0 - bend * bend) * (
        0.5 * math.sqrt(2.0 / math.pi) * (1.0 + 3 * 0.044715 * square)
    )
    return values * half, slope


def column_sum(values):
    return jnp.sum(values, axis=0, keepdims=True)


def reversed_index(index, count):
    total = 0
    for bit in bits_of(count):
        total = total * 2 + (index // bit) % 2
    return total


def attn_fwd_kernel(
    heads,
    rows,
    mem_rows,
    blocks,
    mem_ref,
    h_ref,
    g_ref,
    perm_ref,
    target_ref,
    segment_ref,
    flag_ref,
    wq_hbm,
    wk_hbm,
    wv_hbm,
    wr_hbm,
    rw_ref,
    rr_ref,
    rs_ref,
    embed_ref,
    coarse_ref,
    fine_ref,
    prob_ref,
    af_ref,
    q_hbm,
    k_hbm,
    v_hbm,
    rel_hbm,
    got_ref,
    out_hbm,
    pack_hbm,
    x_hbm,
    pos_hbm,
    col_ref,
    bias_ref,
    w_buf,
    wr_buf,
    mask_ref,
    info_buf,
    x_buf,
    got_buf,
    out_ref,
    pack_ref,
    q_ref,
    k_ref,
    v_ref,
    rel_ref,
    pos_ref,
    key_order_ref,
    x_send,
    x_recv,
    info_send,
    info_recv,
    out_send,
    out_recv,
    own_sem,
    keep_sem,
    full_ref,
    full_sem,
):
    step = pl.program_id(0)
    piece = blocks - 1 - step
    block_id = lax.axis_index("blk")
    group_id = lax.axis_index("dp")
    wide = heads * HEAD_DIM
    width = mem_ref.shape[1]
    mem_all = mem_rows * blocks
    keys = k_ref.shape[1]
    span = rows + keys
    steps = bits_of(blocks)
    sources = (mem_ref, h_ref, g_ref)
    infos = (perm_ref, target_ref, segment_ref)
    keeps = [
        pltpu.make_async_copy(src, dst, keep_sem.at[k])
        for k, (src, dst) in enumerate(
            (
                (pos_ref, pos_hbm),
                (rel_ref, rel_hbm),
                (x_buf, x_hbm),
                (q_ref, q_hbm),
                (k_ref, k_hbm),
                (v_ref, v_hbm),
                (out_ref, out_hbm),
                (pack_ref, pack_hbm),
            )
        )
    ]
    sizes = (mem_rows, rows, rows)
    firsts = (0, mem_all, keys)

    def spot(part, owner):
        first = firsts[part] + owner * sizes[part]
        return pl.ds(pl.multiple_of(first, 32), sizes[part])

    def device(i):
        return (group_id, flip(block_id, i))

    def x_copy(hop, part, come):
        where = x_buf.at[spot(part, flip(block_id, come))]
        return pltpu.make_async_remote_copy(
            src_ref=sources[part] if come == 0 else where,
            dst_ref=where,
            send_sem=x_send.at[come + hop, part],
            recv_sem=x_recv.at[come + hop, part],
            device_id=device(hop),
            device_id_type=MESH_IDS,
        )

    def info_copy(i, kind):
        return pltpu.make_async_remote_copy(
            src_ref=infos[kind],
            dst_ref=info_buf.at[block_id, kind],
            send_sem=info_send.at[i, kind],
            recv_sem=info_recv.at[i, kind],
            device_id=device(i),
            device_id_type=MESH_IDS,
        )

    def own_copy(part):
        return pltpu.make_async_copy(
            sources[part], x_buf.at[spot(part, block_id)], own_sem.at[part]
        )

    def out_copy(i):
        return pltpu.make_async_remote_copy(
            src_ref=pack_ref.at[i],
            dst_ref=got_buf.at[i],
            send_sem=out_send.at[i],
            recv_sem=out_recv.at[i],
            device_id=device(i),
            device_id_type=MESH_IDS,
        )

    @pl.when(step == 0)
    def _():
        weights = [
            pltpu.make_async_copy(src, full_ref.at[k], full_sem.at[k])
            for k, src in enumerate((wr_hbm, wq_hbm, wk_hbm, wv_hbm))
        ]
        for one in weights:
            one.start()
        barrier = pltpu.get_barrier_semaphore()
        for i in range(1, blocks):
            pl.semaphore_signal(barrier, inc=1, device_id=device(i), device_id_type=MESH_IDS)
        pl.semaphore_wait(barrier, blocks - 1)
        for part in range(3):
            x_copy(steps[-1], part, 0).start()
        for hop in steps[:-1]:
            for part in range(3):
                x_copy(hop, part, 0).start()
        for i in range(1, blocks):
            for kind in range(3):
                info_copy(i, kind).start()
        own_infos = [
            pltpu.make_async_copy(infos[kind], info_buf.at[block_id, kind], own_sem.at[3 + kind])
            for kind in range(3)
        ]
        for one in own_infos:
            one.start()
        for part in range(3):
            own_copy(part).start()
        for one in weights:
            one.wait()
        for block in range(blocks):

            @pl.when(block_id == block)
            def _(block=block):
                at = slice(block * wide, (block + 1) * wide)
                for k in range(3):
                    w_buf[:, k * wide : (k + 1) * wide] = full_ref[k + 1, :, at]
                wr_buf[...] = full_ref[0, :, at]
                for k, ref in enumerate((rw_ref, rr_ref, rs_ref)):
                    bias_ref[k : k + 1, :] = row_of(ref)[:, at]
                bias_ref[3:5, :] = embed_ref[:, at]

        dist_count = pos_ref.shape[0]
        half = width // 2
        fine_sin, fine_cos = fine_ref[0], fine_ref[1]
        unit = fine_ref.shape[1]

        def fill(a, carry):
            at = pl.ds(pl.multiple_of(a * unit, unit), unit)
            big_sin, big_cos = coarse_ref[0, pl.ds(a, 1), :], coarse_ref[1, pl.ds(a, 1), :]
            pos_ref[at, :half] = (big_sin * fine_cos - big_cos * fine_sin).astype(BF16)
            pos_ref[at, half:] = (big_cos * fine_cos + big_sin * fine_sin).astype(BF16)
            return carry

        lax.fori_loop(0, dist_count // unit, fill, 0)
        keeps[0].start()
        rel = dot_nn(pos_ref[...], wr_buf[...]).astype(BF16)
        for h in range(heads):
            rel_ref[h] = rel[:, h * HEAD_DIM : (h + 1) * HEAD_DIM]
        keeps[1].start()
        for one in own_infos:
            one.wait()
        for part in range(3):
            own_copy(part).wait()

        def project(i, carry):
            for hop in steps[:-1]:

                @pl.when(i == hop)
                def _(hop=hop):
                    for part in range(3):
                        x_copy(hop, part, 0).wait_recv()

            @pl.when(i == steps[-1])
            def _():
                for part in range(3):
                    x_copy(steps[-1], part, 0).wait_recv()
                    for near in steps[:-1]:
                        x_copy(near, part, steps[-1]).start()

            for near in steps[:-1]:

                @pl.when(i == steps[-1] + near)
                def _(near=near):
                    for part in range(3):
                        x_copy(near, part, steps[-1]).wait_recv()

            owner = mix(block_id, i, blocks)
            x_own = jnp.concatenate([x_buf[spot(part, owner), :] for part in range(3)], axis=0)
            qkv = dot_nn(x_own, w_buf[...])
            q_ref[i] = qkv[mem_rows:, :wide]
            low = qkv[: mem_rows + rows, wide:].astype(BF16)
            for h in range(heads):
                k_part = low[:, h * HEAD_DIM : (h + 1) * HEAD_DIM]
                v_part = low[:, wide + h * HEAD_DIM : wide + (h + 1) * HEAD_DIM]
                k_ref[h, spot(0, owner), :HEAD_DIM] = k_part[:mem_rows]
                k_ref[h, spot(1, owner), :HEAD_DIM] = k_part[mem_rows:]
                v_ref[h, spot(0, owner), :] = v_part[:mem_rows]
                v_ref[h, spot(1, owner), :] = v_part[mem_rows:]
            return carry

        lax.fori_loop(0, blocks, project, 0)
        keeps[2].start()
        keeps[3].start()
        for i in range(1, blocks):
            for kind in range(3):
                info_copy(i, kind).wait()
        for part in range(3):
            for hop in steps:
                x_copy(hop, part, 0).wait_send()
            for near in steps[:-1]:
                x_copy(near, part, steps[-1]).wait_send()

        key_order_ref[:, :mem_all] = jnp.full(
            (8, mem_all), jnp.where(flag_ref[0] > 0, -2.0, 1e9), F32
        )
        for block in range(blocks):
            at = slice(mem_all + block * rows, mem_all + (block + 1) * rows)
            order = jnp.where(info_buf[block, 1] > 0, info_buf[block, 0], -1).astype(F32)
            order = jnp.broadcast_to(order, (8, rows))
            key_order_ref[:, at] = order
            ids = jnp.broadcast_to(info_buf[block, 2].astype(F32), (8, rows))
            place = lax.broadcasted_iota(jnp.int32, (8, rows), 0)
            col_ref[pl.ds(block * rows, rows), :] = jnp.where(place == 0, order, ids).T
        lane = lax.broadcasted_iota(jnp.int32, (mem_all, HEAD_DIM), 1)
        mem_extra = jnp.where(lane < 2, 1.0, 0.0).astype(BF16)
        lane = lax.broadcasted_iota(jnp.int32, (keys - mem_all, HEAD_DIM), 1)
        tok_extra = jnp.where(
            lane < 2, 1.0, jnp.where(lane < 4, col_ref[:, 1:2], 0.0)
        ).astype(BF16)
        for h in range(heads):
            k_ref[h, :mem_all, HEAD_DIM:] = mem_extra
            k_ref[h, mem_all:, HEAD_DIM:] = tok_extra
        keeps[4].start()
        keeps[5].start()

    owner = mix(block_id, piece, blocks)
    tok_at = pl.ds(pl.multiple_of(owner * rows, 32), rows)
    info = col_ref[tok_at, :]
    visible = key_order_ref[0:1, :] <= info[:, 0:1]
    key_at = lax.broadcasted_iota(jnp.int32, (rows, keys), 1) - mem_all - owner * rows
    other = key_at != lax.broadcasted_iota(jnp.int32, (rows, keys), 0)
    mask_ref[:rows, :] = jnp.where(visible, 0.0, NEGATIVE)
    mask_ref[rows:, :] = jnp.where(visible & other, 0.0, NEGATIVE)
    seg = jnp.concatenate([info[:, 1:2], info[:, 1:2]], axis=0)
    rel_at = pl.ds(pl.multiple_of((blocks - 1) * rows - owner * rows, 32), span)
    lane = lax.broadcasted_iota(jnp.int32, (2 * rows, HEAD_DIM), 1)
    for h in range(heads):
        own = slice(h * HEAD_DIM, (h + 1) * HEAD_DIM)
        raw = q_ref[piece, :, own]
        q_word = ((raw + bias_ref[0:1, own]).astype(BF16) * SCALE).astype(BF16)
        q_rel = ((raw + bias_ref[1:2, own]).astype(BF16) * SCALE).astype(BF16)
        same, differ = seg_columns((raw + bias_ref[2:3, own]) * SCALE, bias_ref[3:5, own])
        gap = differ - same
        base = same + gap * seg
        slope = gap * (1.0 - 2.0 * seg)
        base_high = base.astype(BF16).astype(F32)
        slope_high = slope.astype(BF16).astype(F32)
        extra = jnp.where(
            lane == 0,
            base_high,
            jnp.where(
                lane == 1,
                base - base_high,
                jnp.where(lane == 2, slope_high, jnp.where(lane == 3, slope - slope_high, 0.0)),
            ),
        ).astype(BF16)
        q_aug = jnp.concatenate([q_word, extra], axis=1)
        rel = dot_nt(q_rel, rel_ref[h, rel_at, :])
        shift = span - (rows - 1)
        rel = jnp.concatenate(
            [
                pltpu.roll(rel[:rows], shift, 1, stride=1, stride_axis=0)[:, :keys],
                pltpu.roll(rel[rows:], shift, 1, stride=1, stride_axis=0)[:, :keys],
            ],
            axis=0,
        )
        scores = dot_nt(q_aug, k_ref[h]) + rel + mask_ref[...]
        weight = jnp.exp(scores - jnp.max(scores, axis=1, keepdims=True))
        probs = (weight * (1.0 / jnp.sum(weight, axis=1, keepdims=True))).astype(BF16)
        prob_ref[h, 0] = probs
        attn_f = dot_nn(probs, v_ref[h])
        af_ref[0, :, own] = attn_f
        low = attn_f.astype(BF16)
        out_ref[piece, :, own] = low
        pack_ref[piece, :, own] = low[:rows]
        pack_ref[piece, :, wide + h * HEAD_DIM : wide + (h + 1) * HEAD_DIM] = low[rows:]

    for i in range(1, blocks):

        @pl.when(piece == i)
        def _(i=i):
            out_copy(i).start()

    @pl.when(step == blocks - 1)
    def _():
        keeps[6].start()
        keeps[7].start()
        got_ref[0] = pack_ref[0]
        for i in range(1, blocks):
            out_copy(i).wait()
            got_ref[i] = got_buf[i]
        for one in keeps:
            one.wait()


def flip_eights(values):
    index = 7 - lax.broadcasted_iota(jnp.int32, (8, values.shape[1]), 0)
    return jnp.take_along_axis(values, index, axis=0)


def spread_rows(values, rows, keys):
    span = rows + keys
    padded = jnp.concatenate([values, jnp.zeros((rows, rows), F32)], axis=1)
    groups = []
    for a in range(rows // 8):
        group = flip_eights(padded[8 * a : 8 * a + 8])
        group = pltpu.roll(group, (rows - 8 - 8 * a) % span, 1, stride=1, stride_axis=0)
        groups.append(flip_eights(group))
    return jnp.concatenate(groups, axis=0)


SMALL_ROWS = 64


def place_of(index, order):
    total = 0
    for bit in order:
        total = total * 2 + (index // bit) % 2
    return total


def main_kernel(
    groups,
    heads,
    mem_rows,
    orders,
    plan,
    got_ref,
    h_hbm,
    g_hbm,
    cot_h_hbm,
    cot_g_hbm,
    target_ref,
    bias_ref,
    info_ref,
    wo_hbm,
    w1_hbm,
    w2_hbm,
    wq_hbm,
    wk_hbm,
    wv_hbm,
    prob_hbm,
    af_hbm,
    q_hbm,
    k_hbm,
    v_hbm,
    rel_hbm,
    out_hbm,
    pack_hbm,
    x_hbm,
    pos_hbm,
    ln1_gain_ref,
    ln1_bias_ref,
    b1_ref,
    b2_ref,
    ln2_gain_ref,
    ln2_bias_ref,
    h_out_ref,
    g_out_ref,
    h_grad_ref,
    g_grad_ref,
    mem_grad_ref,
    head_out_ref,
    w1_out_ref,
    w2_out_ref,
    wo_out_ref,
    small_out_ref,
    late_out_ref,
    wo_ref,
    w1_ref,
    w2_ref,
    attn_ref,
    slope_ref,
    act_ref,
    gpre_ref,
    ffn_all,
    gf_all,
    gb_all,
    b1_row_ref,
    acc_ref,
    streams_ref,
    cot_ref,
    resid_grad_ref,
    prob_ref,
    af_ref,
    q_ref,
    k_ref,
    v_ref,
    rel_ref,
    out_ref,
    own_ref,
    far_ref,
    ga_send_ref,
    ga_ref,
    kv_acc,
    rel_acc,
    turned_ref,
    pack_ref,
    pack_got,
    dq_all,
    dkv_all,
    small_ref,
    small_got,
    late_ref,
    late_got,
    late_all,
    *rest,
):
    jobs_count = len(orders)
    nb = len(orders[0])
    src_refs = rest[:jobs_count]
    recv_refs = [
        rest[jobs_count + k * nb : jobs_count + (k + 1) * nb] for k in range(jobs_count)
    ]
    (
        w1_cut,
        w1_got,
        head_cut,
        head_got,
        w2_cut,
        w2_got,
        wo_cut,
        wo_got,
        load_sem,
        late_load_sem,
        send_sem,
        recv_sem,
        job_send,
        job_recv,
        pack_send,
        pack_recv,
        small_send,
        small_recv,
        end_send,
        end_recv,
        far_send,
        far_recv,
        ga_sem_send,
        ga_sem_recv,
        weight_sem,
        entry_sem,
    ) = rest[jobs_count + jobs_count * nb :]
    block_id = lax.axis_index("blk")
    group_id = lax.axis_index("dp")
    both, width = attn_ref.shape
    rows = both // 2
    wide = heads * HEAD_DIM
    blocks = act_ref.shape[0]
    part = act_ref.shape[2]
    steps = bits_of(blocks)
    mem_all = mem_rows * blocks
    pair = mem_rows + rows
    keys = k_ref.shape[1]
    span = rows + keys
    dist_count = rel_ref.shape[1]
    share = width // (groups * blocks)

    def device(i):
        return (group_id, flip(block_id, i))

    held = groups * block_id + group_id
    owner_id = (held // blocks, held % blocks)
    mine = blocks * group_id + block_id
    source_id = (mine % groups, mine // groups)
    moves = held != mine

    loads = [
        pltpu.make_async_copy(src, dst, load_sem.at[k])
        for k, (src, dst) in enumerate(
            (
                (wo_hbm, wo_ref),
                (out_hbm, out_ref),
                (af_hbm, af_ref),
                (q_hbm, q_ref),
                (k_hbm, k_ref),
                (v_hbm, v_ref),
                (rel_hbm, rel_ref),
                (pack_hbm, own_ref),
            )
        )
    ]
    prob_loads = [
        pltpu.make_async_copy(prob_hbm.at[h], prob_ref.at[h % 2], load_sem.at[len(loads) + h])
        for h in range(heads)
    ]
    row_loads = [
        pltpu.make_async_copy(
            x_hbm.at[pl.ds(pl.multiple_of(first + flip(block_id, i) * rows, 32), rows)],
            ffn_all.at[i, pl.ds(to, rows)],
            load_sem.at[len(loads) + heads + 2 * i + k],
        )
        for i in range(1, blocks)
        for k, (first, to) in enumerate(((mem_all, 0), (keys, rows)))
    ]
    def columns(c):
        return pl.ds(pl.multiple_of(c * part, 128), part)

    def weight_loads(c):
        return (
            pltpu.make_async_copy(
                w1_hbm.at[:, columns(c)], w1_ref.at[:, columns(c)], weight_sem.at[0, c]
            ),
            pltpu.make_async_copy(w2_hbm.at[columns(c)], w2_ref.at[columns(c)], weight_sem.at[1, c]),
        )

    loads[0].start()
    entry_loads = [
        pltpu.make_async_copy(src, dst.at[pl.ds(first, rows)], entry_sem.at[k])
        for k, (src, dst, first) in enumerate(
            (
                (h_hbm, streams_ref, 0),
                (g_hbm, streams_ref, rows),
                (cot_h_hbm, cot_ref, 0),
                (cot_g_hbm, cot_ref, rows),
            )
        )
    ]
    for one in entry_loads:
        one.start()
    for c in range(blocks):
        for one in weight_loads(c):
            one.start()
    for one in loads[7:] + row_loads:
        one.start()
    barrier = pltpu.get_barrier_semaphore()
    for i in range(1, blocks):
        pl.semaphore_signal(barrier, inc=1, device_id=device(i), device_id_type=MESH_IDS)
    for bit in orders[0]:
        pl.semaphore_signal(
            barrier, inc=1, device_id=(flip(group_id, bit), block_id), device_id_type=MESH_IDS
        )

    @pl.when(moves)
    def _():
        pl.semaphore_signal(barrier, inc=1, device_id=source_id, device_id_type=MESH_IDS)
        pl.semaphore_wait(barrier, blocks + nb)

    @pl.when(held == mine)
    def _():
        pl.semaphore_wait(barrier, blocks - 1 + nb)

    def remote(src, dst, send, recv, target):
        return pltpu.make_async_remote_copy(
            src_ref=src,
            dst_ref=dst,
            send_sem=send,
            recv_sem=recv,
            device_id=target,
            device_id_type=MESH_IDS,
        )

    def piece_copy(ref, which, hop, come):
        at = come + hop
        return remote(
            ref.at[come], ref.at[at], send_sem.at[which, at], recv_sem.at[which, at], device(hop)
        )

    def far_copy(i, q):
        if i == steps[-1] + 1:
            src = got_ref.at[steps[-1]] if q == 1 else far_ref.at[1, (q ^ 1) - 1]
            target = device(1)
        else:
            src = pack_hbm.at[q ^ i]
            target = device(i)
        return remote(
            src, far_ref.at[i - 1, q - 1], far_send.at[i, q], far_recv.at[i, q], target
        )

    for q in range(1, blocks):
        far_copy(2, q).start()
    for q in range(1, blocks):
        far_copy(1, q).start()
    far_copy(3, 1).start()

    def spread(ref, which):
        for hop in reversed(steps):
            piece_copy(ref, which, hop, 0).start()

    def near_ready(ref, which):
        for hop in steps[:-1]:
            piece_copy(ref, which, hop, 0).wait_recv()

    def relay(ref, which):
        far = steps[-1]
        piece_copy(ref, which, far, 0).wait_recv()
        for hop in steps[:-1]:
            piece_copy(ref, which, hop, far).start()

    def collect(ref, which):
        for hop in steps[:-1]:
            piece_copy(ref, which, hop, steps[-1]).wait_recv()

    def finish(ref, which):
        for hop in steps:
            piece_copy(ref, which, hop, 0).wait_send()
        for hop in steps[:-1]:
            piece_copy(ref, which, hop, steps[-1]).wait_send()

    def job_source(job, stage):
        return src_refs[job] if stage == 0 else recv_refs[job][stage - 1]

    def job_half(job, stage, own):
        half = groups >> (stage + 1)
        bit = (group_id // orders[job][stage]) % 2
        which = bit if own else 1 - bit
        return pl.ds(which * half, half)

    def job_copy(job, stage):
        return remote(
            job_source(job, stage).at[job_half(job, stage, False)],
            recv_refs[job][stage],
            job_send.at[job, stage],
            job_recv.at[job, stage],
            (flip(group_id, orders[job][stage]), block_id),
        )

    def job_start(job):
        job_copy(job, 0).start()

    def job_next(job, stage):
        job_copy(job, stage).wait_recv()
        keep = job_source(job, stage)[job_half(job, stage, True)]
        into = recv_refs[job][stage]
        total = keep.astype(F32) + into[...].astype(F32)
        if stage < nb - 1:
            into[...] = total.astype(BF16)
            job_copy(job, stage + 1).start()
            return None
        return total[0]

    def job_done(job):
        for stage in range(nb):
            job_copy(job, stage).wait_send()

    def cut_copy(cut, got, which, i):
        return remote(
            cut.at[i], got.at[i], end_send.at[which, i], end_recv.at[which, i], device(i)
        )

    def cut_start(cut, first, values):
        low = values.astype(BF16)
        for k in range(blocks):
            at = mix(block_id, k, blocks)
            cut[at, :, first : first + values.shape[1]] = low[k * share : (k + 1) * share]

    def cut_send(cut, got, which):
        for i in range(1, blocks):
            cut_copy(cut, got, which, i).start()

    def owner_copy(cut, got, which):
        return remote(cut, got, end_send.at[which, 0], end_recv.at[which, 0], owner_id)

    def owner_send(cut, got, which):
        @pl.when(moves)
        def _():
            owner_copy(cut, got, which).start()

        @pl.when(held == mine)
        def _():
            got[...] = cut[...]

    def owner_wait(cut, got, which):
        @pl.when(moves)
        def _():
            owner_copy(cut, got, which).wait()

    def assemble(pieces):
        for block in range(blocks):

            @pl.when(block_id == block)
            def _(block=block):
                for i in range(blocks):
                    at = slice((block ^ i) * wide, ((block ^ i) + 1) * wide)
                    piece = pieces(i)
                    attn_ref[:rows, at] = piece[:, :wide]
                    attn_ref[rows:, at] = piece[:, wide:]

    assemble(lambda i: got_ref[i])
    small_ref[0] = jnp.zeros(small_ref.shape[1:], F32)
    b1_row_ref[0:1, :] = row_of(b1_ref)
    target = jnp.broadcast_to(target_ref[...].astype(F32), (8, rows)).T[:, 0:1]
    weight = jnp.concatenate([jnp.ones((rows, 1), F32), target], axis=0)

    def squares(values):
        weighted = jnp.sum(values * values, axis=1, keepdims=True) * weight
        return column_sum(weighted[:rows]), column_sum(weighted[rows:])

    loads[0].wait()
    branch = dot_nn(attn_ref[...], wo_ref[...])
    att_stat = squares(branch)
    for one in entry_loads:
        one.wait()
    streams = streams_ref[...].astype(F32)
    unit_one, rate_one = norm_parts(branch + streams)
    gain_one = row_of(ln1_gain_ref)
    out_one = unit_one * gain_one + row_of(ln1_bias_ref)
    ffn_all[0] = out_one.astype(BF16)
    for one in loads[1:7] + prob_loads[:2]:
        one.start()
    acc_ref[...] = jnp.broadcast_to(row_of(b2_ref), acc_ref.shape)

    def ffn_part(c, carry):
        for one in weight_loads(c):
            one.wait()
        at = columns(c)
        act, slope = gelu_pair(dot_nn(ffn_all[0], w1_ref[:, at]) + b1_row_ref[0:1, at])
        slope_ref[:, at] = slope
        act = act.astype(BF16)
        act_ref[c] = act
        acc_ref[...] += dot_nn(act, w2_ref[at, :])
        return carry

    lax.fori_loop(0, blocks, ffn_part, 0)
    branch_ffn = acc_ref[...]
    ffn_stat = squares(branch_ffn)
    unit_two, rate_two = norm_parts(branch_ffn + out_one)
    gain_two = row_of(ln2_gain_ref)
    out_two = unit_two * gain_two + row_of(ln2_bias_ref)
    out_stat = squares(out_two)
    h_out_ref[...] = out_two[:rows].astype(BF16)
    g_out_ref[...] = out_two[rows:].astype(BF16)
    cot = cot_ref[...].astype(F32)
    grad_two = norm_back(unit_two, rate_two, cot * gain_two)
    grad_ffn = grad_two.astype(BF16)
    gf_all[0] = grad_ffn
    spread(gf_all, 1)
    for q in (2, 3):
        far_copy(2, q).wait_recv()
        far_copy(3, q ^ 1).start()
    tall = width // 128
    tall_part = part // 128
    stat_row = 5 * tall + blocks * tall_part
    early = small_ref.at[0]
    put_row(early, 0, column_sum(cot * unit_two))
    put_row(early, tall, column_sum(cot))
    put_row(early, 2 * tall, column_sum(grad_ffn.astype(F32)))
    acc_ref[...] = grad_two

    def ffn_back(c, carry):
        at = columns(c)
        grad_pre = (dot_nt(gf_all[0], w2_ref[at, :]) * slope_ref[:, at]).astype(BF16)
        gpre_ref[c] = grad_pre
        b1_row_ref[1:2, at] = column_sum(grad_pre.astype(F32))
        acc_ref[...] += dot_nt(grad_pre, w1_ref[:, at])
        return carry

    lax.fori_loop(0, blocks, ffn_back, 0)
    grad_out_one = acc_ref[...]
    put_row(early, 5 * tall, b1_row_ref[1:2, :])
    put_row(early, 3 * tall, column_sum(grad_out_one * unit_one))
    put_row(early, 4 * tall, column_sum(grad_out_one))
    grad_one = norm_back(unit_one, rate_one, grad_out_one * gain_one)
    resid_grad_ref[...] = grad_one
    grad_branch = grad_one.astype(BF16)
    gb_all[0] = grad_branch
    grad_attn = dot_nt(grad_branch, wo_ref[...]).astype(BF16)
    for block in range(blocks):

        @pl.when(block_id == block)
        def _(block=block):
            for i in range(blocks):
                at = slice((block ^ i) * wide, ((block ^ i) + 1) * wide)
                ga_send_ref[i, :, :wide] = grad_attn[:rows, at]
                ga_send_ref[i, :, wide:] = grad_attn[rows:, at]

    def ga_copy(i):
        return remote(
            ga_send_ref.at[i], ga_ref.at[i], ga_sem_send.at[i], ga_sem_recv.at[i], device(i)
        )

    for i in range(blocks - 1, 0, -1):
        ga_copy(i).start()
    spread(gb_all, 2)
    ga_ref[0] = ga_send_ref[0]
    lane = lax.broadcasted_iota(jnp.int32, (1, 128), 1)
    stats = jnp.zeros((1, 128), F32)
    terms = [att_stat[0], ffn_stat[0], out_stat[0], att_stat[1], ffn_stat[1], out_stat[1]]
    terms += [jnp.full((1, 1), float(rows), F32), column_sum(target)]
    for k, term in enumerate(terms):
        stats = jnp.where(lane == k, term, stats)
    early[stat_row : stat_row + 1, :] = stats

    small_steps = [("blk", bit) for bit in steps] + [("dp", bit) for bit in bits_of(groups)]

    def small_copy(k):
        axis, bit = small_steps[k]
        target_id = device(bit) if axis == "blk" else (flip(group_id, bit), block_id)
        return remote(
            small_ref.at[k], small_got.at[k], small_send.at[k], small_recv.at[k], target_id
        )

    def small_next(k):
        small_copy(k).wait_recv()
        small_ref[k + 1] = small_ref[k] + small_got[k]
        if k + 1 < len(small_steps):
            small_copy(k + 1).start()

    small_copy(0).start()

    def late_copy(k, i=0):
        bits = bits_of(groups)
        if k < nb:
            return remote(
                late_ref.at[k],
                late_got.at[k],
                small_send.at[8 + k],
                small_recv.at[8 + k],
                (flip(group_id, bits[k]), block_id),
            )
        return remote(
            late_ref.at[nb],
            late_all.at[i],
            small_send.at[8 + nb + i],
            small_recv.at[8 + nb + i],
            device(i),
        )

    def late_next(k):
        late_copy(k).wait_recv()
        late_ref[k + 1] = late_ref[k] + late_got[k]
        if k + 1 < nb:
            late_copy(k + 1).start()
        else:
            for i in range(1, blocks):
                late_copy(nb, i).start()

    x_rows = keys + rows * blocks

    done = set()

    def job_event(job, stage):
        value = job_next(job, stage)
        if stage < nb - 1:
            return
        done.add(job)
        if job < 2:
            w2_cut[:, job * (width // 2) : (job + 1) * (width // 2)] = value.astype(BF16)
            if {0, 1} <= done:
                owner_send(w2_cut, w2_got, 2)
        elif job < 4:
            cut_start(w1_cut, (job - 2) * (part // 2), value)
            if {2, 3} <= done:
                cut_send(w1_cut, w1_got, 0)
        elif job == 4:
            wo_cut[...] = value.astype(BF16)
            owner_send(wo_cut, wo_got, 3)
        else:
            cut_start(head_cut.at[job - 5], 0, value)
            cut_send(head_cut.at[job - 5], head_got.at[job - 5], 4 + job - 5)

    def happen(spot):
        for kind, first, *more in plan.get(spot, ()):
            if kind == "job":
                job_event(first, *more)
            elif kind == "small":
                small_next(first)
            else:
                late_next(first)

    own_at = columns(block_id)
    act_ref[0] = act_ref[block_id]
    gpre_ref[0] = gpre_ref[block_id]
    loads[7].wait()
    for one in row_loads:
        one.wait()
    far_copy(2, 1).wait_recv()
    for q in range(1, blocks):
        far_copy(1, q).wait_recv()
        far_copy(3, q).wait_recv()

    def slice_front(i, carry):
        assemble(lambda k: own_ref[i] if k == 0 else far_ref[k - 1, i - 1])
        other = dot_nn(attn_ref[...], wo_ref[...]) + ffn_all[i].astype(F32)
        other = norm_parts(other)[0] * row_of(ln1_gain_ref) + row_of(ln1_bias_ref)
        ffn_all[i] = other.astype(BF16)
        act, slope = gelu_pair(dot_nn(ffn_all[i], w1_ref[:, own_at]) + b1_row_ref[0:1, own_at])
        act_ref[i] = act.astype(BF16)
        slope_ref[:, columns(i)] = slope
        return carry

    lax.fori_loop(1, blocks, slice_front, 0)

    def slice_back(i, carry):
        @pl.when(i == 1)
        def _():
            near_ready(gf_all, 1)

        @pl.when(i == steps[-1])
        def _():
            relay(gf_all, 1)

        @pl.when(i == steps[-1] + 1)
        def _():
            collect(gf_all, 1)

        grad_pre = dot_nt(gf_all[i], w2_ref[own_at, :]) * slope_ref[:, columns(i)]
        gpre_ref[i] = grad_pre.astype(BF16)
        return carry

    lax.fori_loop(1, blocks, slice_back, 0)

    def flat(ref):
        return ref[...].reshape(blocks * both, ref.shape[2])

    def put_shares(first, count, values):
        tall_share = values.shape[0] // groups
        lanes_here = values.shape[1] // count
        low = values.astype(BF16)
        for k in range(count):
            for d in range(groups):
                src_refs[first + k][place_of(d, orders[first + k])] = low[
                    d * tall_share : (d + 1) * tall_share,
                    k * lanes_here : (k + 1) * lanes_here,
                ]
            job_start(first + k)

    put_shares(0, 2, dot_tn(flat(act_ref), flat(gf_all)))
    put_shares(2, 2, dot_tn(flat(ffn_all), flat(gpre_ref)))
    happen("ffn")

    x_loads = [
        pltpu.make_async_copy(
            src, w2_ref.at[pl.ds(first, src.shape[0])], late_load_sem.at[k]
        )
        for k, (src, first) in enumerate(((x_hbm, 0), (pos_hbm, x_rows)))
    ]
    for one in x_loads:
        one.start()

    def turn(c, carry):
        at = pl.ds(pl.multiple_of(c * 128, 128), 128)
        w1_ref[:, at] = w2_ref[at, :].T
        return carry

    x_loads[0].wait()
    lax.fori_loop(0, x_rows // 128, turn, 0)
    x_loads[1].wait()
    lax.fori_loop(x_rows // 128, (x_rows + dist_count) // 128, turn, 0)
    late_loads = [
        pltpu.make_async_copy(
            src, w2_ref.at[pl.ds(k * width, width)], late_load_sem.at[2 + k]
        )
        for k, src in enumerate((wq_hbm, wk_hbm, wv_hbm))
    ]
    for one in late_loads:
        one.start()
    for one in loads[1:7]:
        one.wait()
    kv_acc[...] = jnp.zeros_like(kv_acc)
    rel_acc[...] = jnp.zeros_like(rel_acc)
    late_ref[0] = jnp.zeros(late_ref.shape[1:], F32)
    for i in range(1, blocks):
        ga_copy(i).wait_recv()
    turned_ref[...] = jnp.zeros_like(turned_ref)
    happen("pre")

    def pack_copy(h, i):
        return remote(
            pack_ref.at[h, i], pack_got.at[h, i], pack_send.at[h, i], pack_recv.at[h, i], device(i)
        )


    for h in range(heads):
        own = slice(h * HEAD_DIM, (h + 1) * HEAD_DIM)

        def tile(piece, carry, h=h, own=own):
            for slot in range(blocks):
                if plan.get((h, slot)):

                    @pl.when(piece == slot)
                    def _(slot=slot):
                        happen((h, slot))

            owner = mix(block_id, piece, blocks)
            tok_at = pl.ds(pl.multiple_of(owner * rows, 32), rows)
            rel_start = pl.multiple_of((blocks - 1) * rows - owner * rows, 128)
            rel_at = pl.ds(rel_start, span)
            seg = info_ref[tok_at, 1:2]
            seg = jnp.concatenate([seg, seg], axis=0)
            raw = q_ref[piece, :, own]
            q_word = (raw + bias_ref[0:1, own]).astype(BF16)
            q_rel = (raw + bias_ref[1:2, own]).astype(BF16)
            q_seg = raw + bias_ref[2:3, own]
            embed = bias_ref[3:5, own]
            other = slice(wide + h * HEAD_DIM, wide + (h + 1) * HEAD_DIM)
            ga = jnp.concatenate([ga_ref[piece, :, own], ga_ref[piece, :, other]], axis=0)
            probs = prob_ref[h % 2, piece]
            ga_f = ga.astype(F32) * SCALE
            row_dot = jnp.sum(ga_f * af_ref[piece, :, own], axis=1, keepdims=True)
            grad_prob = dot_nt(ga_f.astype(BF16), v_ref[h])
            grad_score = probs.astype(F32) * (grad_prob - row_dot)
            grad_low = grad_score.astype(BF16)
            wide_word = dot_nn(grad_low, k_ref[h])
            grad_word = wide_word[:, :HEAD_DIM]
            total = wide_word[:, HEAD_DIM : HEAD_DIM + 1]
            ones = wide_word[:, HEAD_DIM + 2 : HEAD_DIM + 3]
            differ = ones + seg * (total - 2.0 * ones)
            same = total - differ
            grad_seg = same * embed[0:1] + differ * embed[1:2]
            wind = jnp.concatenate(
                [
                    spread_rows(grad_score[:rows], rows, keys),
                    spread_rows(grad_score[rows:], rows, keys),
                ],
                axis=0,
            ).astype(BF16)
            grad_rel = dot_nn(wind, rel_ref[h, rel_at, :])
            kv_acc[h, :HEAD_DIM] += dot_tn(q_word, grad_low)
            kv_acc[h, HEAD_DIM:] += dot_tn(ga, probs)
            rel_acc[h, :, rel_at] += dot_tn(q_rel, wind)
            grad_q = (grad_word + grad_rel + grad_seg).astype(BF16)
            for first, part_q in ((mem_all, grad_q[:rows]), (keys, grad_q[rows:])):
                at = pl.ds(pl.multiple_of(first + owner * rows, 32), rows)
                turned_ref[at, 2 * HEAD_DIM :] = part_q
            pack_ref[h, piece, :rows, :HEAD_DIM] = grad_q[:rows]
            pack_ref[h, piece, :rows, HEAD_DIM:] = grad_q[rows:]
            late_ref[0, :, own] += jnp.concatenate(
                [
                    column_sum(grad_word),
                    column_sum(grad_rel),
                    column_sum(grad_seg),
                    column_sum(same * q_seg),
                    column_sum(differ * q_seg),
                    jnp.zeros((3, HEAD_DIM), F32),
                ],
                axis=0,
            )
            return carry

        prob_loads[h].wait()
        lax.fori_loop(0, blocks, tile, 0)
        if h + 2 < heads:
            prob_loads[h + 2].start()
        if h == 0:
            near_ready(gb_all, 2)
            relay(gb_all, 2)
        if h == 1:
            collect(gb_all, 2)
            put_shares(4, 1, dot_tn(flat(out_ref), flat(gb_all)))
        full = kv_acc[h].T.astype(BF16)
        turned_ref[:keys, : 2 * HEAD_DIM] = full
        for k in range(blocks):
            at = mix(block_id, k, blocks)
            mem_part = full[k * mem_rows : (k + 1) * mem_rows]
            tok_part = full[mem_all + k * rows : mem_all + (k + 1) * rows]
            pack_ref[h, at, rows : rows + mem_rows, :] = mem_part
            pack_ref[h, at, rows + mem_rows :, :] = tok_part
        for i in range(blocks - 1, 0, -1):
            pack_copy(h, i).start()
        if h == heads - 1:
            late_copy(0).start()
        happen(("packed", h))
        grad_wr = dot_nn(
            w1_ref[:, x_rows : x_rows + dist_count], rel_acc[h].T.astype(BF16)
        )
        grad_kvq = dot_nn(w1_ref[:, :x_rows], turned_ref[...])
        put_shares(5 + h, 1, jnp.concatenate([grad_kvq, grad_wr], axis=1))
        happen(("head", h))

    happen("tail")

    for h in range(heads - 1):
        for i in range(1, blocks):
            pack_copy(h, i).wait_recv()
    happen("pack")
    for one in late_loads:
        one.wait()
    for i in range(1, blocks):
        pack_copy(heads - 1, i).wait_recv()
    for block in range(blocks):

        @pl.when(block_id == block)
        def _(block=block):
            for h in range(heads):
                for i in range(blocks):
                    at = (block ^ i) * wide + h * HEAD_DIM
                    to = slice(at, at + HEAD_DIM)
                    piece = pack_ref[h, 0] if i == 0 else pack_got[h, i]
                    dq_all[:rows, to] = piece[:rows, :HEAD_DIM]
                    dq_all[rows:, to] = piece[:rows, HEAD_DIM:]
                    dkv_all[:, to] = piece[rows:, :HEAD_DIM]
                    dkv_all[:, width + at : width + at + HEAD_DIM] = piece[rows:, HEAD_DIM:]

    grad_rows = dot_nt(dkv_all[:, :width], w2_ref[width : 2 * width, :]) + dot_nt(
        dkv_all[:, width:], w2_ref[2 * width : 3 * width, :]
    )
    grad_streams = resid_grad_ref[...] + dot_nt(dq_all[...], w2_ref[:width, :])
    h_grad_ref[...] = grad_streams[:rows] + grad_rows[mem_rows:]
    g_grad_ref[...] = grad_streams[rows:]
    mem_grad_ref[...] = grad_rows[:mem_rows]

    happen("end")
    owner_wait(w2_cut, w2_got, 2)
    owner_wait(wo_cut, wo_got, 3)
    w2_out_ref[...] = w2_got[...]
    wo_out_ref[...] = wo_got[...]
    w1_out_ref[0] = w1_cut[0]
    for i in range(1, blocks):
        cut_copy(w1_cut, w1_got, 0, i).wait()
        w1_out_ref[i] = w1_got[i]
    for h in range(heads):
        head_out_ref[h, 0] = head_cut[h, 0]
        for i in range(1, blocks):
            cut_copy(head_cut.at[h], head_got.at[h], 4 + h, i).wait()
            head_out_ref[h, i] = head_got[h, i]

    small_out_ref[...] = small_ref[len(small_steps)]
    for i in range(1, blocks):
        late_copy(nb, i).wait()
        late_out_ref[i] = late_all[i]
    late_out_ref[0] = late_ref[nb]

    for k in range(len(small_steps)):
        small_copy(k).wait_send()
    for k in range(nb):
        late_copy(k).wait_send()
    for h in range(heads):
        for i in range(1, blocks):
            pack_copy(h, i).wait_send()
    for job in range(jobs_count):
        job_done(job)
    for i in range(1, blocks):
        ga_copy(i).wait_send()
        for q in range(1, blocks):
            far_copy(i, q).wait_send()
    finish(gf_all, 1)
    finish(gb_all, 2)


def finish_kernel(
    heads,
    h_ref,
    g_ref,
    h_grad_ref,
    g_grad_ref,
    mem_grad_ref,
    head_ref,
    w1_ref,
    w2_ref,
    wo_ref,
    small_ref,
    late_ref,
    h_out_ref,
    g_out_ref,
    h_grad_out_ref,
    g_grad_out_ref,
    mem_grad_out_ref,
    wq_out_ref,
    wk_out_ref,
    wv_out_ref,
    wr_out_ref,
    wo_out_ref,
    w1_out_ref,
    w2_out_ref,
    rw_out_ref,
    rr_out_ref,
    rs_out_ref,
    embed_out_ref,
    ln1_gain_out_ref,
    ln1_bias_out_ref,
    b1_out_ref,
    b2_out_ref,
    ln2_gain_out_ref,
    ln2_bias_out_ref,
    rms_out_ref,
    rows_ref,
):
    block_id = lax.axis_index("blk")
    blocks, share, part = w1_ref.shape
    width = h_ref.shape[1]
    wide = heads * HEAD_DIM
    tall = width // 128
    tall_part = part // 128
    stat_row = 5 * tall + blocks * tall_part

    def put_lanes(out, values, stride, first):
        count = values.shape[0]
        for j in range(values.shape[1] // 128):
            out[pl.ds(first + j, count, stride=stride), :] = values[:, 128 * j : 128 * (j + 1)]

    h_out_ref[...] = h_ref[...]
    g_out_ref[...] = g_ref[...]
    h_grad_out_ref[...] = h_grad_ref[...]
    g_grad_out_ref[...] = g_grad_ref[...]
    mem_grad_out_ref[...] = mem_grad_ref[...]
    put_lanes(w2_out_ref, w2_ref[...].astype(F32), tall, 0)
    put_lanes(wo_out_ref, wo_ref[...].astype(F32), tall, 0)
    for i in range(blocks):
        first = mix(block_id, i, blocks) * tall_part
        put_lanes(w1_out_ref, w1_ref[i].astype(F32), blocks * tall_part, first)
    for block in range(blocks):

        @pl.when(block_id == block)
        def _(block=block):
            for i in range(blocks):
                at = slice((block ^ i) * wide, ((block ^ i) + 1) * wide)
                for h in range(heads):
                    first = (block ^ i) * wide + h * HEAD_DIM
                    for k in range(4):
                        rows_ref[k, :share, first : first + HEAD_DIM] = head_ref[
                            h, i, :, k * HEAD_DIM : (k + 1) * HEAD_DIM
                        ].astype(F32)
                rows_ref[4, :8, at] = late_ref[i]

    for k, out in enumerate((wk_out_ref, wv_out_ref, wq_out_ref, wr_out_ref)):
        put_lanes(out, rows_ref[k, :share, :], tall, 0)
    put_row(rw_out_ref, 0, rows_ref[4, 0:1, :])
    put_row(rr_out_ref, 0, rows_ref[4, 1:2, :])
    put_row(rs_out_ref, 0, rows_ref[4, 2:3, :])
    embed_out_ref[...] = rows_ref[4, 3:5, :]
    ln2_gain_out_ref[...] = small_ref[:tall]
    ln2_bias_out_ref[...] = small_ref[tall : 2 * tall]
    b2_out_ref[...] = small_ref[2 * tall : 3 * tall]
    ln1_gain_out_ref[...] = small_ref[3 * tall : 4 * tall]
    ln1_bias_out_ref[...] = small_ref[4 * tall : 5 * tall]
    b1_out_ref[...] = small_ref[5 * tall : stat_row]
    stats = small_ref[stat_row : stat_row + 1]
    lane = lax.broadcasted_iota(jnp.int32, (1, 128), 1)
    counts = jnp.where(lane < 3, stats[:, 6:7], stats[:, 7:8]) * float(width)
    rms_out_ref[...] = jnp.sqrt(stats / counts)[0, :6]


def exchange_plan(groups, blocks, heads):
    near = tuple(bits_of(groups))
    jobs = 5 + heads
    smalls = len(near) + len(bits_of(blocks))
    if (groups, blocks, heads) == (8, 4, 3):
        orders = (
            (1, 2, 4),
            (2, 4, 1),
            (2, 4, 1),
            (1, 2, 4),
            (1, 2, 4),
            (2, 4, 1),
            (1, 2, 4),
            (1, 2, 4),
        )
        plan = {
            "ffn": [("small", 0)],
            "pre": [("small", 1)],
            (0, 2): [("job", 0, 0), ("job", 1, 0)],
            (0, 3): [("small", 2)],
            ("head", 0): [("small", 3), ("job", 2, 0), ("job", 3, 0)],
            (1, 2): [("job", 0, 1)],
            (1, 3): [("small", 4)],
            ("head", 1): [("job", 1, 1)],
            (2, 1): [("job", 5, 0)],
            (2, 3): [("job", 4, 0)],
            ("head", 2): [("job", 3, 1), ("job", 2, 1), ("job", 6, 0)],
            "end": [("job", 1, 2), ("late", 0), ("job", 0, 2), ("job", 4, 1), ("job", 5, 1), ("job", 7, 0), ("job", 2, 2), ("job", 6, 1), ("job", 3, 2), ("late", 1), ("job", 5, 2), ("job", 4, 2), ("late", 2), ("job", 7, 1), ("job", 6, 2), ("job", 7, 2)],
        }
        return orders, plan
    plan = {"end": [("job", job, stage) for stage in range(len(near)) for job in range(jobs)]}
    plan["end"] += [("small", k) for k in range(smalls)] + [("late", k) for k in range(len(near))]
    return (near,) * jobs, plan


def whole(shape):
    return pl.BlockSpec(shape, lambda *_: (0,) * len(shape))


def local(
    h_in,
    g_in,
    memory,
    cot_h,
    cot_g,
    perm_order,
    target,
    segment,
    mem_flag,
    w_q,
    w_k,
    w_v,
    w_r,
    w_o,
    r_w_bias,
    r_r_bias,
    r_s_bias,
    seg_embed,
    ln1_gain,
    ln1_bias,
    w_1,
    b_1,
    w_2,
    b_2,
    ln2_gain,
    ln2_bias,
):
    _, rows, width = h_in.shape
    mem_rows = memory.shape[1]
    hidden = w_1.shape[1]
    blocks = lax.axis_size("blk")
    groups = lax.axis_size("dp")
    tok_all = rows * blocks
    mem_all = mem_rows * blocks
    keys = mem_all + tok_all
    dist_count = tok_all + keys
    heads = HEADS // blocks
    wide = heads * HEAD_DIM
    both = 2 * rows
    pair = mem_rows + rows
    part = hidden // blocks
    tall = width // 128
    share = width // (groups * blocks)
    nb = len(bits_of(groups))
    hbm = pl.BlockSpec(memory_space=pltpu.HBM)
    vmem = pl.BlockSpec(memory_space=pltpu.VMEM)
    shape = jax.ShapeDtypeStruct

    def lanes(values):
        return values.reshape(-1, 128)

    coarse, fine = position_units(keys - 1, dist_count, width, 32)
    (
        probs, attn_f, q_raw, k_aug, v_all, rel_heads, got_out, attn_out, pack_out, x_all, pos_table,
        query_info, biases,
    ) = pl.pallas_call(
        functools.partial(attn_fwd_kernel, heads, rows, mem_rows, blocks),
        name="attn_fwd",
        grid=(blocks,),
        in_specs=[hbm] * 3
        + [whole((1, rows))] * 3
        + [pl.BlockSpec(memory_space=pltpu.SMEM)]
        + [hbm] * 4
        + [whole((tall, 128))] * 3
        + [whole((2, width)), whole(coarse.shape), whole(fine.shape)],
        out_specs=[
            pl.BlockSpec((heads, 1, both, keys), lambda s: (0, blocks - 1 - s, 0, 0)),
            pl.BlockSpec((1, both, wide), lambda s: (blocks - 1 - s, 0, 0)),
            hbm,
            hbm,
            hbm,
            hbm,
            whole((blocks, rows, 2 * wide)),
            hbm,
            hbm,
            hbm,
            hbm,
            whole((tok_all, 8)),
            whole((8, wide)),
        ],
        out_shape=[
            shape((heads, blocks, both, keys), BF16),
            shape((blocks, both, wide), F32),
            shape((blocks, both, wide), F32),
            shape((heads, keys, 2 * HEAD_DIM), BF16),
            shape((heads, keys, HEAD_DIM), BF16),
            shape((heads, dist_count, HEAD_DIM), BF16),
            shape((blocks, rows, 2 * wide), BF16),
            shape((blocks, both, wide), BF16),
            shape((blocks, rows, 2 * wide), BF16),
            shape((keys + tok_all, width), BF16),
            shape((dist_count, width), BF16),
            shape((tok_all, 8), F32),
            shape((8, wide), F32),
        ],
        scratch_shapes=[
            pltpu.VMEM((width, 3 * wide), BF16),
            pltpu.VMEM((width, wide), BF16),
            pltpu.VMEM((both, keys), F32),
            pltpu.VMEM((blocks, 3, 1, rows), jnp.int32),
            pltpu.VMEM((keys + tok_all, width), BF16),
            pltpu.VMEM((blocks, rows, 2 * wide), BF16),
            pltpu.VMEM((blocks, both, wide), BF16),
            pltpu.VMEM((blocks, rows, 2 * wide), BF16),
            pltpu.VMEM((blocks, both, wide), F32),
            pltpu.VMEM((heads, keys, 2 * HEAD_DIM), BF16),
            pltpu.VMEM((heads, keys, HEAD_DIM), BF16),
            pltpu.VMEM((heads, dist_count, HEAD_DIM), BF16),
            pltpu.VMEM((dist_count, width), BF16),
            pltpu.VMEM((8, keys), F32),
            pltpu.SemaphoreType.DMA((blocks, 3)),
            pltpu.SemaphoreType.DMA((blocks, 3)),
            pltpu.SemaphoreType.DMA((blocks, 3)),
            pltpu.SemaphoreType.DMA((blocks, 3)),
            pltpu.SemaphoreType.DMA((blocks,)),
            pltpu.SemaphoreType.DMA((blocks,)),
            pltpu.SemaphoreType.DMA((6,)),
            pltpu.SemaphoreType.DMA((8,)),
            pltpu.VMEM((4, width, width), BF16),
            pltpu.SemaphoreType.DMA((4,)),
        ],
        compiler_params=pltpu.CompilerParams(
            vmem_limit_bytes=60 << 20, collective_id=0, has_side_effects=True
        ),
    )(
        memory[0], h_in[0], g_in[0], perm_order, target, segment, mem_flag, w_q, w_k, w_v, w_r,
        lanes(r_w_bias), lanes(r_r_bias), lanes(r_s_bias), seg_embed, coarse, fine,
    )

    near = tuple(bits_of(groups))
    orders, plan = exchange_plan(groups, blocks, heads)
    job_shapes = (
        [(part // groups, width // 2)] * 2
        + [(width // groups, part // 2)] * 2
        + [(wide // groups, width)]
        + [(width // groups, 4 * HEAD_DIM)] * heads
    )
    sources = [pltpu.VMEM((groups,) + one, BF16) for one in job_shapes]
    receivers = [
        pltpu.VMEM((groups >> (k + 1),) + one, BF16) for one in job_shapes for k in range(nb)
    ]
    bits = len(bits_of(blocks)) + nb
    square = width * width // (groups * blocks * 128)
    oblong = width * hidden // (groups * blocks * 128)
    grads_shape = [
        shape((rows, width), BF16),
        shape((rows, width), BF16),
        shape((rows, width), F32),
        shape((rows, width), F32),
        shape((mem_rows, width), F32),
    ]
    parts = pl.pallas_call(
        functools.partial(main_kernel, groups, heads, mem_rows, orders, plan),
        name="main",
        in_specs=[vmem] + [hbm] * 4 + [vmem] * 3 + [hbm] * 16 + [vmem] * 6,
        out_specs=[vmem] * 11,
        out_shape=grads_shape
        + [
            shape((heads, blocks, share, 4 * HEAD_DIM), BF16),
            shape((blocks, share, part), BF16),
            shape((part // groups, width), BF16),
            shape((wide // groups, width), BF16),
            shape((SMALL_ROWS, 128), F32),
            shape((blocks, 8, wide), F32),
        ],
        scratch_shapes=[
            pltpu.VMEM((width, width), BF16),
            pltpu.VMEM((width, hidden), BF16),
            pltpu.VMEM((hidden, width), BF16),
            pltpu.VMEM((both, width), BF16),
            pltpu.VMEM((both, hidden), F32),
            pltpu.VMEM((blocks, both, part), BF16),
            pltpu.VMEM((blocks, both, part), BF16),
            pltpu.VMEM((blocks, both, width), BF16),
            pltpu.VMEM((blocks, both, width), BF16),
            pltpu.VMEM((blocks, both, width), BF16),
            pltpu.VMEM((8, hidden), F32),
            pltpu.VMEM((both, width), F32),
            pltpu.VMEM((both, width), BF16),
            pltpu.VMEM((both, width), BF16),
            pltpu.VMEM((both, width), F32),
            pltpu.VMEM((2, blocks, both, keys), BF16),
            pltpu.VMEM((blocks, both, wide), F32),
            pltpu.VMEM((blocks, both, wide), F32),
            pltpu.VMEM((heads, keys, 2 * HEAD_DIM), BF16),
            pltpu.VMEM((heads, keys, HEAD_DIM), BF16),
            pltpu.VMEM((heads, dist_count, HEAD_DIM), BF16),
            pltpu.VMEM((blocks, both, wide), BF16),
            pltpu.VMEM((blocks, rows, 2 * wide), BF16),
            pltpu.VMEM((blocks - 1, blocks - 1, rows, 2 * wide), BF16),
            pltpu.VMEM((blocks, rows, 2 * wide), BF16),
            pltpu.VMEM((blocks, rows, 2 * wide), BF16),
            pltpu.VMEM((heads, 2 * HEAD_DIM, keys), F32),
            pltpu.VMEM((heads, HEAD_DIM, dist_count), F32),
            pltpu.VMEM((keys + tok_all, 3 * HEAD_DIM), BF16),
            pltpu.VMEM((heads, blocks, rows + pair, 2 * HEAD_DIM), BF16),
            pltpu.VMEM((heads, blocks, rows + pair, 2 * HEAD_DIM), BF16),
            pltpu.VMEM((both, width), BF16),
            pltpu.VMEM((pair, 2 * width), BF16),
            pltpu.VMEM((bits + 1, SMALL_ROWS, 128), F32),
            pltpu.VMEM((bits, SMALL_ROWS, 128), F32),
            pltpu.VMEM((nb + 1, 8, wide), F32),
            pltpu.VMEM((nb, 8, wide), F32),
            pltpu.VMEM((blocks, 8, wide), F32),
        ]
        + sources
        + receivers
        + [
            pltpu.VMEM((blocks, share, part), BF16),
            pltpu.VMEM((blocks, share, part), BF16),
            pltpu.VMEM((heads, blocks, share, 4 * HEAD_DIM), BF16),
            pltpu.VMEM((heads, blocks, share, 4 * HEAD_DIM), BF16),
            pltpu.VMEM((part // groups, width), BF16),
            pltpu.VMEM((part // groups, width), BF16),
            pltpu.VMEM((wide // groups, width), BF16),
            pltpu.VMEM((wide // groups, width), BF16),
            pltpu.SemaphoreType.DMA((10 + heads + 2 * blocks,)),
            pltpu.SemaphoreType.DMA((5,)),
            pltpu.SemaphoreType.DMA((3, blocks)),
            pltpu.SemaphoreType.DMA((3, blocks)),
            pltpu.SemaphoreType.DMA((len(job_shapes), nb)),
            pltpu.SemaphoreType.DMA((len(job_shapes), nb)),
            pltpu.SemaphoreType.DMA((heads, blocks)),
            pltpu.SemaphoreType.DMA((heads, blocks)),
            pltpu.SemaphoreType.DMA((8 + nb + blocks,)),
            pltpu.SemaphoreType.DMA((8 + nb + blocks,)),
            pltpu.SemaphoreType.DMA((4 + heads, blocks)),
            pltpu.SemaphoreType.DMA((4 + heads, blocks)),
            pltpu.SemaphoreType.DMA((blocks, blocks)),
            pltpu.SemaphoreType.DMA((blocks, blocks)),
            pltpu.SemaphoreType.DMA((blocks,)),
            pltpu.SemaphoreType.DMA((blocks,)),
            pltpu.SemaphoreType.DMA((2, blocks)),
            pltpu.SemaphoreType.DMA((4,)),
        ],
        compiler_params=pltpu.CompilerParams(
            vmem_limit_bytes=60 << 20, collective_id=1, has_side_effects=True
        ),
    )(
        got_out, h_in[0], g_in[0], cot_h[0], cot_g[0], target, biases, query_info,
        w_o, w_1, w_2, w_q, w_k, w_v, probs, attn_f, q_raw, k_aug, v_all, rel_heads, attn_out,
        pack_out, x_all, pos_table,
        lanes(ln1_gain), lanes(ln1_bias), lanes(b_1), lanes(b_2), lanes(ln2_gain), lanes(ln2_bias),
    )
    outs = pl.pallas_call(
        functools.partial(finish_kernel, heads),
        name="finish",
        in_specs=[vmem] * 11,
        out_specs=[vmem] * 23,
        out_shape=grads_shape
        + [shape((square, 128), F32)] * 5
        + [shape((oblong, 128), F32)] * 2
        + [shape((tall, 128), F32)] * 3
        + [shape((2, width), F32)]
        + [shape((tall, 128), F32)] * 2
        + [shape((hidden // 128, 128), F32)]
        + [shape((tall, 128), F32)] * 3
        + [shape((6,), F32)],
        scratch_shapes=[pltpu.VMEM((5, max(8, share), width), F32)],
        compiler_params=pltpu.CompilerParams(vmem_limit_bytes=60 << 20),
    )(*parts)
    outs = list(outs)
    for k in range(5):
        outs[k] = outs[k][None]
    for k in list(range(5, 15)) + list(range(16, 22)):
        outs[k] = outs[k].reshape(-1)
    return tuple(outs)


def solution(mesh):
    rows = P("dp", "blk", None)
    ints = P("dp", "blk")
    flat = P(("dp", "blk"))
    return jax.shard_map(
        local,
        mesh=mesh,
        in_specs=(rows,) * 5 + (ints,) * 3 + (P("dp"),) + (P(),) * 17,
        out_specs=(rows,) * 5 + (flat,) * 7 + (P(),) * 11,
        check_vma=False,
    )
```

```python
import functools
import math

import jax
import jax.numpy as jnp
import numpy as np
from jax import lax
from jax.experimental import pallas as pl
from jax.experimental.pallas import tpu as pltpu
from jax.sharding import PartitionSpec as P

HEADS = 12
HEAD_DIM = 64
EPSILON = 1e-12
NEGATIVE = -1e30
SCALE = 1.0 / math.sqrt(HEAD_DIM)
F32 = jnp.float32
BF16 = jnp.bfloat16
MESH_IDS = pl.DeviceIdType.MESH


def position_units(top, dist_count, model_width, unit):
    freq = np.exp(np.arange(model_width // 2) * (-2.0 * math.log(10000.0) / model_width))
    coarse = (top - unit * np.arange(dist_count // unit))[:, None] * freq[None, :]
    fine = np.arange(unit)[:, None] * freq[None, :]
    return tuple(
        np.stack([np.sin(angle), np.cos(angle)]).astype(np.float32) for angle in (coarse, fine)
    )


def dot_nn(left, right):
    return lax.dot_general(left, right, (((1,), (0,)), ((), ())), preferred_element_type=F32)


def dot_nt(left, right):
    return lax.dot_general(left, right, (((1,), (1,)), ((), ())), preferred_element_type=F32)


def dot_tn(left, right):
    return lax.dot_general(left, right, (((0,), (0,)), ((), ())), preferred_element_type=F32)


def bits_of(count):
    return [1 << k for k in range(count.bit_length() - 1)]


def seg_columns(q_seg, embed):
    return (
        jnp.sum(q_seg * embed[0:1], axis=1, keepdims=True),
        jnp.sum(q_seg * embed[1:2], axis=1, keepdims=True),
    )


def flip(index, step):
    for bit in (1 << k for k in range(step.bit_length())):
        if step & bit:
            index = index + bit - 2 * bit * ((index // bit) % 2)
    return index


def mix(index, other, blocks):
    total = 0
    for bit in bits_of(blocks):
        left = (index // bit) % 2
        right = (other // bit) % 2
        total = total + bit * (left + right - 2 * left * right)
    return total


def row_of(ref):
    return jnp.concatenate([ref[j : j + 1, :] for j in range(ref.shape[0])], axis=1)


def put_row(ref, at, values):
    for j in range(values.shape[1] // 128):
        ref[at + j : at + j + 1, :] = values[:, 128 * j : 128 * (j + 1)]


def row_mean(values):
    return jnp.mean(values, axis=1, keepdims=True)


def norm_parts(values):
    center = values - row_mean(values)
    rate = lax.rsqrt(row_mean(center * center) + EPSILON)
    return center * rate, rate


def norm_back(unit, rate, scaled):
    return rate * (scaled - row_mean(scaled) - unit * row_mean(scaled * unit))


def gelu_pair(values):
    square = values * values
    inner = math.sqrt(2.0 / math.pi) * values * (1.0 + 0.044715 * square)
    bend = jnp.tanh(inner)
    half = 0.5 * (1.0 + bend)
    slope = half + values * (1.0 - bend * bend) * (
        0.5 * math.sqrt(2.0 / math.pi) * (1.0 + 3 * 0.044715 * square)
    )
    return values * half, slope


def column_sum(values):
    return jnp.sum(values, axis=0, keepdims=True)


def reversed_index(index, count):
    total = 0
    for bit in bits_of(count):
        total = total * 2 + (index // bit) % 2
    return total


def attn_fwd_kernel(
    heads,
    rows,
    mem_rows,
    blocks,
    mem_ref,
    h_ref,
    g_ref,
    perm_ref,
    target_ref,
    segment_ref,
    flag_ref,
    wq_hbm,
    wk_hbm,
    wv_hbm,
    wr_hbm,
    rw_ref,
    rr_ref,
    rs_ref,
    embed_ref,
    coarse_ref,
    fine_ref,
    prob_ref,
    af_ref,
    q_hbm,
    k_hbm,
    v_hbm,
    rel_hbm,
    got_ref,
    out_hbm,
    pack_hbm,
    x_hbm,
    pos_hbm,
    col_ref,
    bias_ref,
    w_buf,
    wr_buf,
    mask_ref,
    info_buf,
    x_buf,
    got_buf,
    out_ref,
    pack_ref,
    q_ref,
    k_ref,
    v_ref,
    rel_ref,
    pos_ref,
    key_order_ref,
    x_send,
    x_recv,
    info_send,
    info_recv,
    out_send,
    out_recv,
    own_sem,
    keep_sem,
    full_ref,
    full_sem,
):
    step = pl.program_id(0)
    piece = blocks - 1 - step
    block_id = lax.axis_index("blk")
    group_id = lax.axis_index("dp")
    wide = heads * HEAD_DIM
    width = mem_ref.shape[1]
    mem_all = mem_rows * blocks
    keys = k_ref.shape[1]
    span = rows + keys
    steps = bits_of(blocks)
    sources = (mem_ref, h_ref, g_ref)
    infos = (perm_ref, target_ref, segment_ref)
    keeps = [
        pltpu.make_async_copy(src, dst, keep_sem.at[k])
        for k, (src, dst) in enumerate(
            (
                (pos_ref, pos_hbm),
                (rel_ref, rel_hbm),
                (x_buf, x_hbm),
                (q_ref, q_hbm),
                (k_ref, k_hbm),
                (v_ref, v_hbm),
                (out_ref, out_hbm),
                (pack_ref, pack_hbm),
            )
        )
    ]
    sizes = (mem_rows, rows, rows)
    firsts = (0, mem_all, keys)

    def spot(part, owner):
        first = firsts[part] + owner * sizes[part]
        return pl.ds(pl.multiple_of(first, 32), sizes[part])

    def device(i):
        return (group_id, flip(block_id, i))

    def x_copy(hop, part, come):
        where = x_buf.at[spot(part, flip(block_id, come))]
        return pltpu.make_async_remote_copy(
            src_ref=sources[part] if come == 0 else where,
            dst_ref=where,
            send_sem=x_send.at[come + hop, part],
            recv_sem=x_recv.at[come + hop, part],
            device_id=device(hop),
            device_id_type=MESH_IDS,
        )

    def info_copy(i, kind):
        return pltpu.make_async_remote_copy(
            src_ref=infos[kind],
            dst_ref=info_buf.at[block_id, kind],
            send_sem=info_send.at[i, kind],
            recv_sem=info_recv.at[i, kind],
            device_id=device(i),
            device_id_type=MESH_IDS,
        )

    def own_copy(part):
        return pltpu.make_async_copy(
            sources[part], x_buf.at[spot(part, block_id)], own_sem.at[part]
        )

    def out_copy(i):
        return pltpu.make_async_remote_copy(
            src_ref=pack_ref.at[i],
            dst_ref=got_buf.at[i],
            send_sem=out_send.at[i],
            recv_sem=out_recv.at[i],
            device_id=device(i),
            device_id_type=MESH_IDS,
        )

    @pl.when(step == 0)
    def _():
        weights = [
            pltpu.make_async_copy(src, full_ref.at[k], full_sem.at[k])
            for k, src in enumerate((wr_hbm, wq_hbm, wk_hbm, wv_hbm))
        ]
        for one in weights:
            one.start()
        barrier = pltpu.get_barrier_semaphore()
        for i in range(1, blocks):
            pl.semaphore_signal(barrier, inc=1, device_id=device(i), device_id_type=MESH_IDS)
        pl.semaphore_wait(barrier, blocks - 1)
        for part in range(3):
            x_copy(steps[-1], part, 0).start()
        for hop in steps[:-1]:
            for part in range(3):
                x_copy(hop, part, 0).start()
        for i in range(1, blocks):
            for kind in range(3):
                info_copy(i, kind).start()
        own_infos = [
            pltpu.make_async_copy(infos[kind], info_buf.at[block_id, kind], own_sem.at[3 + kind])
            for kind in range(3)
        ]
        for one in own_infos:
            one.start()
        for part in range(3):
            own_copy(part).start()
        for one in weights:
            one.wait()
        for block in range(blocks):

            @pl.when(block_id == block)
            def _(block=block):
                at = slice(block * wide, (block + 1) * wide)
                for k in range(3):
                    w_buf[:, k * wide : (k + 1) * wide] = full_ref[k + 1, :, at]
                wr_buf[...] = full_ref[0, :, at]
                for k, ref in enumerate((rw_ref, rr_ref, rs_ref)):
                    bias_ref[k : k + 1, :] = row_of(ref)[:, at]
                bias_ref[3:5, :] = embed_ref[:, at]

        dist_count = pos_ref.shape[0]
        half = width // 2
        fine_sin, fine_cos = fine_ref[0], fine_ref[1]
        unit = fine_ref.shape[1]

        def fill(a, carry):
            at = pl.ds(pl.multiple_of(a * unit, unit), unit)
            big_sin, big_cos = coarse_ref[0, pl.ds(a, 1), :], coarse_ref[1, pl.ds(a, 1), :]
            pos_ref[at, :half] = (big_sin * fine_cos - big_cos * fine_sin).astype(BF16)
            pos_ref[at, half:] = (big_cos * fine_cos + big_sin * fine_sin).astype(BF16)
            return carry

        lax.fori_loop(0, dist_count // unit, fill, 0)
        keeps[0].start()
        rel = dot_nn(pos_ref[...], wr_buf[...]).astype(BF16)
        for h in range(heads):
            rel_ref[h] = rel[:, h * HEAD_DIM : (h + 1) * HEAD_DIM]
        keeps[1].start()
        for one in own_infos:
            one.wait()
        for part in range(3):
            own_copy(part).wait()

        def project(i, carry):
            for hop in steps[:-1]:

                @pl.when(i == hop)
                def _(hop=hop):
                    for part in range(3):
                        x_copy(hop, part, 0).wait_recv()

            @pl.when(i == steps[-1])
            def _():
                for part in range(3):
                    x_copy(steps[-1], part, 0).wait_recv()
                    for near in steps[:-1]:
                        x_copy(near, part, steps[-1]).start()

            for near in steps[:-1]:

                @pl.when(i == steps[-1] + near)
                def _(near=near):
                    for part in range(3):
                        x_copy(near, part, steps[-1]).wait_recv()

            owner = mix(block_id, i, blocks)
            x_own = jnp.concatenate([x_buf[spot(part, owner), :] for part in range(3)], axis=0)
            qkv = dot_nn(x_own, w_buf[...])
            q_ref[i] = qkv[mem_rows:, :wide]
            low = qkv[: mem_rows + rows, wide:].astype(BF16)
            for h in range(heads):
                k_part = low[:, h * HEAD_DIM : (h + 1) * HEAD_DIM]
                v_part = low[:, wide + h * HEAD_DIM : wide + (h + 1) * HEAD_DIM]
                k_ref[h, spot(0, owner), :HEAD_DIM] = k_part[:mem_rows]
                k_ref[h, spot(1, owner), :HEAD_DIM] = k_part[mem_rows:]
                v_ref[h, spot(0, owner), :] = v_part[:mem_rows]
                v_ref[h, spot(1, owner), :] = v_part[mem_rows:]
            return carry

        lax.fori_loop(0, blocks, project, 0)
        keeps[2].start()
        keeps[3].start()
        for i in range(1, blocks):
            for kind in range(3):
                info_copy(i, kind).wait()
        for part in range(3):
            for hop in steps:
                x_copy(hop, part, 0).wait_send()
            for near in steps[:-1]:
                x_copy(near, part, steps[-1]).wait_send()

        key_order_ref[:, :mem_all] = jnp.full(
            (8, mem_all), jnp.where(flag_ref[0] > 0, -2.0, 1e9), F32
        )
        for block in range(blocks):
            at = slice(mem_all + block * rows, mem_all + (block + 1) * rows)
            order = jnp.where(info_buf[block, 1] > 0, info_buf[block, 0], -1).astype(F32)
            order = jnp.broadcast_to(order, (8, rows))
            key_order_ref[:, at] = order
            ids = jnp.broadcast_to(info_buf[block, 2].astype(F32), (8, rows))
            place = lax.broadcasted_iota(jnp.int32, (8, rows), 0)
            col_ref[pl.ds(block * rows, rows), :] = jnp.where(place == 0, order, ids).T
        lane = lax.broadcasted_iota(jnp.int32, (mem_all, HEAD_DIM), 1)
        mem_extra = jnp.where(lane < 2, 1.0, 0.0).astype(BF16)
        lane = lax.broadcasted_iota(jnp.int32, (keys - mem_all, HEAD_DIM), 1)
        tok_extra = jnp.where(
            lane < 2, 1.0, jnp.where(lane < 4, col_ref[:, 1:2], 0.0)
        ).astype(BF16)
        for h in range(heads):
            k_ref[h, :mem_all, HEAD_DIM:] = mem_extra
            k_ref[h, mem_all:, HEAD_DIM:] = tok_extra
        keeps[4].start()
        keeps[5].start()

    owner = mix(block_id, piece, blocks)
    tok_at = pl.ds(pl.multiple_of(owner * rows, 32), rows)
    info = col_ref[tok_at, :]
    visible = key_order_ref[0:1, :] <= info[:, 0:1]
    key_at = lax.broadcasted_iota(jnp.int32, (rows, keys), 1) - mem_all - owner * rows
    other = key_at != lax.broadcasted_iota(jnp.int32, (rows, keys), 0)
    mask_ref[:rows, :] = jnp.where(visible, 0.0, NEGATIVE)
    mask_ref[rows:, :] = jnp.where(visible & other, 0.0, NEGATIVE)
    seg = jnp.concatenate([info[:, 1:2], info[:, 1:2]], axis=0)
    rel_at = pl.ds(pl.multiple_of((blocks - 1) * rows - owner * rows, 32), span)
    lane = lax.broadcasted_iota(jnp.int32, (2 * rows, HEAD_DIM), 1)
    for h in range(heads):
        own = slice(h * HEAD_DIM, (h + 1) * HEAD_DIM)
        raw = q_ref[piece, :, own]
        q_word = ((raw + bias_ref[0:1, own]).astype(BF16) * SCALE).astype(BF16)
        q_rel = ((raw + bias_ref[1:2, own]).astype(BF16) * SCALE).astype(BF16)
        same, differ = seg_columns((raw + bias_ref[2:3, own]) * SCALE, bias_ref[3:5, own])
        gap = differ - same
        base = same + gap * seg
        slope = gap * (1.0 - 2.0 * seg)
        base_high = base.astype(BF16).astype(F32)
        slope_high = slope.astype(BF16).astype(F32)
        extra = jnp.where(
            lane == 0,
            base_high,
            jnp.where(
                lane == 1,
                base - base_high,
                jnp.where(lane == 2, slope_high, jnp.where(lane == 3, slope - slope_high, 0.0)),
            ),
        ).astype(BF16)
        q_aug = jnp.concatenate([q_word, extra], axis=1)
        rel = dot_nt(q_rel, rel_ref[h, rel_at, :])
        shift = span - (rows - 1)
        rel = jnp.concatenate(
            [
                pltpu.roll(rel[:rows], shift, 1, stride=1, stride_axis=0)[:, :keys],
                pltpu.roll(rel[rows:], shift, 1, stride=1, stride_axis=0)[:, :keys],
            ],
            axis=0,
        )
        scores = dot_nt(q_aug, k_ref[h]) + rel + mask_ref[...]
        weight = jnp.exp(scores - jnp.max(scores, axis=1, keepdims=True))
        probs = (weight * (1.0 / jnp.sum(weight, axis=1, keepdims=True))).astype(BF16)
        prob_ref[h, 0] = probs
        attn_f = dot_nn(probs, v_ref[h])
        af_ref[0, :, own] = attn_f
        low = attn_f.astype(BF16)
        out_ref[piece, :, own] = low
        pack_ref[piece, :, own] = low[:rows]
        pack_ref[piece, :, wide + h * HEAD_DIM : wide + (h + 1) * HEAD_DIM] = low[rows:]

    for i in range(1, blocks):

        @pl.when(piece == i)
        def _(i=i):
            out_copy(i).start()

    @pl.when(step == blocks - 1)
    def _():
        keeps[6].start()
        keeps[7].start()
        got_ref[0] = pack_ref[0]
        for i in range(1, blocks):
            out_copy(i).wait()
            got_ref[i] = got_buf[i]
        for one in keeps:
            one.wait()


def flip_eights(values):
    index = 7 - lax.broadcasted_iota(jnp.int32, (8, values.shape[1]), 0)
    return jnp.take_along_axis(values, index, axis=0)


def spread_rows(values, rows, keys):
    span = rows + keys
    padded = jnp.concatenate([values, jnp.zeros((rows, rows), F32)], axis=1)
    groups = []
    for a in range(rows // 8):
        group = flip_eights(padded[8 * a : 8 * a + 8])
        group = pltpu.roll(group, (rows - 8 - 8 * a) % span, 1, stride=1, stride_axis=0)
        groups.append(flip_eights(group))
    return jnp.concatenate(groups, axis=0)


SMALL_ROWS = 64


def place_of(index, order):
    total = 0
    for bit in order:
        total = total * 2 + (index // bit) % 2
    return total


def main_kernel(
    groups,
    heads,
    mem_rows,
    orders,
    plan,
    got_ref,
    h_hbm,
    g_hbm,
    cot_h_hbm,
    cot_g_hbm,
    target_ref,
    bias_ref,
    info_ref,
    wo_hbm,
    w1_hbm,
    w2_hbm,
    wq_hbm,
    wk_hbm,
    wv_hbm,
    prob_hbm,
    af_hbm,
    q_hbm,
    k_hbm,
    v_hbm,
    rel_hbm,
    out_hbm,
    pack_hbm,
    x_hbm,
    pos_hbm,
    ln1_gain_ref,
    ln1_bias_ref,
    b1_ref,
    b2_ref,
    ln2_gain_ref,
    ln2_bias_ref,
    h_out_hbm,
    g_out_hbm,
    h_grad_hbm,
    g_grad_hbm,
    mem_grad_hbm,
    head_out_ref,
    w1_out_ref,
    w2_out_ref,
    wo_out_ref,
    small_out_ref,
    late_out_ref,
    wo_ref,
    w1_ref,
    w2_ref,
    attn_ref,
    slope_ref,
    act_ref,
    gpre_ref,
    ffn_all,
    gf_all,
    gb_all,
    b1_row_ref,
    acc_ref,
    streams_ref,
    cot_ref,
    resid_grad_ref,
    prob_ref,
    af_ref,
    q_ref,
    k_ref,
    v_ref,
    rel_ref,
    out_ref,
    own_ref,
    far_ref,
    ga_send_ref,
    ga_ref,
    kv_acc,
    rel_acc,
    turned_ref,
    pack_ref,
    pack_got,
    dq_all,
    dkv_all,
    small_ref,
    small_got,
    late_ref,
    late_got,
    late_all,
    *rest,
):
    jobs_count = len(orders)
    nb = len(orders[0])
    src_refs = rest[:jobs_count]
    recv_refs = [
        rest[jobs_count + k * nb : jobs_count + (k + 1) * nb] for k in range(jobs_count)
    ]
    (
        w1_cut,
        w1_got,
        head_cut,
        head_got,
        w2_cut,
        w2_got,
        wo_cut,
        wo_got,
        load_sem,
        late_load_sem,
        send_sem,
        recv_sem,
        job_send,
        job_recv,
        pack_send,
        pack_recv,
        small_send,
        small_recv,
        end_send,
        end_recv,
        far_send,
        far_recv,
        ga_sem_send,
        ga_sem_recv,
        weight_sem,
        entry_sem,
        h_out_ref,
        g_out_ref,
        h_grad_ref,
        g_grad_ref,
        mem_grad_ref,
        result_sem,
    ) = rest[jobs_count + jobs_count * nb :]
    block_id = lax.axis_index("blk")
    group_id = lax.axis_index("dp")
    both, width = attn_ref.shape
    rows = both // 2
    wide = heads * HEAD_DIM
    blocks = act_ref.shape[0]
    part = act_ref.shape[2]
    steps = bits_of(blocks)
    mem_all = mem_rows * blocks
    pair = mem_rows + rows
    keys = k_ref.shape[1]
    span = rows + keys
    dist_count = rel_ref.shape[1]
    share = width // (groups * blocks)

    def device(i):
        return (group_id, flip(block_id, i))

    held = groups * block_id + group_id
    owner_id = (held // blocks, held % blocks)
    mine = blocks * group_id + block_id
    source_id = (mine % groups, mine // groups)
    moves = held != mine

    loads = [
        pltpu.make_async_copy(src, dst, load_sem.at[k])
        for k, (src, dst) in enumerate(
            (
                (wo_hbm, wo_ref),
                (out_hbm, out_ref),
                (af_hbm, af_ref),
                (q_hbm, q_ref),
                (k_hbm, k_ref),
                (v_hbm, v_ref),
                (rel_hbm, rel_ref),
                (pack_hbm, own_ref),
            )
        )
    ]
    prob_loads = [
        pltpu.make_async_copy(prob_hbm.at[h], prob_ref.at[h % 2], load_sem.at[len(loads) + h])
        for h in range(heads)
    ]
    row_loads = [
        pltpu.make_async_copy(
            x_hbm.at[pl.ds(pl.multiple_of(first + flip(block_id, i) * rows, 32), rows)],
            ffn_all.at[i, pl.ds(to, rows)],
            load_sem.at[len(loads) + heads + 2 * i + k],
        )
        for i in range(1, blocks)
        for k, (first, to) in enumerate(((mem_all, 0), (keys, rows)))
    ]
    def columns(c):
        return pl.ds(pl.multiple_of(c * part, 128), part)

    def weight_loads(c):
        return (
            pltpu.make_async_copy(
                w1_hbm.at[:, columns(c)], w1_ref.at[:, columns(c)], weight_sem.at[0, c]
            ),
            pltpu.make_async_copy(w2_hbm.at[columns(c)], w2_ref.at[columns(c)], weight_sem.at[1, c]),
        )

    loads[0].start()
    entry_loads = [
        pltpu.make_async_copy(src, dst.at[pl.ds(first, rows)], entry_sem.at[k])
        for k, (src, dst, first) in enumerate(
            (
                (h_hbm, streams_ref, 0),
                (g_hbm, streams_ref, rows),
                (cot_h_hbm, cot_ref, 0),
                (cot_g_hbm, cot_ref, rows),
            )
        )
    ]
    for one in entry_loads:
        one.start()
    for c in range(blocks):
        for one in weight_loads(c):
            one.start()
    for one in loads[7:] + row_loads:
        one.start()
    barrier = pltpu.get_barrier_semaphore()
    for i in range(1, blocks):
        pl.semaphore_signal(barrier, inc=1, device_id=device(i), device_id_type=MESH_IDS)
    for bit in orders[0]:
        pl.semaphore_signal(
            barrier, inc=1, device_id=(flip(group_id, bit), block_id), device_id_type=MESH_IDS
        )

    @pl.when(moves)
    def _():
        pl.semaphore_signal(barrier, inc=1, device_id=source_id, device_id_type=MESH_IDS)
        pl.semaphore_wait(barrier, blocks + nb)

    @pl.when(held == mine)
    def _():
        pl.semaphore_wait(barrier, blocks - 1 + nb)

    def remote(src, dst, send, recv, target):
        return pltpu.make_async_remote_copy(
            src_ref=src,
            dst_ref=dst,
            send_sem=send,
            recv_sem=recv,
            device_id=target,
            device_id_type=MESH_IDS,
        )

    def piece_copy(ref, which, hop, come):
        at = come + hop
        return remote(
            ref.at[come], ref.at[at], send_sem.at[which, at], recv_sem.at[which, at], device(hop)
        )

    def far_copy(i, q):
        if i == steps[-1] + 1:
            src = got_ref.at[steps[-1]] if q == 1 else far_ref.at[1, (q ^ 1) - 1]
            target = device(1)
        else:
            src = pack_hbm.at[q ^ i]
            target = device(i)
        return remote(
            src, far_ref.at[i - 1, q - 1], far_send.at[i, q], far_recv.at[i, q], target
        )

    for q in range(1, blocks):
        far_copy(2, q).start()
    for q in range(1, blocks):
        far_copy(1, q).start()
    far_copy(3, 1).start()

    def spread(ref, which):
        for hop in reversed(steps):
            piece_copy(ref, which, hop, 0).start()

    def near_ready(ref, which):
        for hop in steps[:-1]:
            piece_copy(ref, which, hop, 0).wait_recv()

    def relay(ref, which):
        far = steps[-1]
        piece_copy(ref, which, far, 0).wait_recv()
        for hop in steps[:-1]:
            piece_copy(ref, which, hop, far).start()

    def collect(ref, which):
        for hop in steps[:-1]:
            piece_copy(ref, which, hop, steps[-1]).wait_recv()

    def finish(ref, which):
        for hop in steps:
            piece_copy(ref, which, hop, 0).wait_send()
        for hop in steps[:-1]:
            piece_copy(ref, which, hop, steps[-1]).wait_send()

    def job_source(job, stage):
        return src_refs[job] if stage == 0 else recv_refs[job][stage - 1]

    def job_half(job, stage, own):
        half = groups >> (stage + 1)
        bit = (group_id // orders[job][stage]) % 2
        which = bit if own else 1 - bit
        return pl.ds(which * half, half)

    def job_copy(job, stage):
        return remote(
            job_source(job, stage).at[job_half(job, stage, False)],
            recv_refs[job][stage],
            job_send.at[job, stage],
            job_recv.at[job, stage],
            (flip(group_id, orders[job][stage]), block_id),
        )

    def job_start(job):
        job_copy(job, 0).start()

    def job_next(job, stage):
        job_copy(job, stage).wait_recv()
        keep = job_source(job, stage)[job_half(job, stage, True)]
        into = recv_refs[job][stage]
        total = keep.astype(F32) + into[...].astype(F32)
        if stage < nb - 1:
            into[...] = total.astype(BF16)
            job_copy(job, stage + 1).start()
            return None
        return total[0]

    def job_done(job):
        for stage in range(nb):
            job_copy(job, stage).wait_send()

    def cut_copy(cut, got, which, i):
        return remote(
            cut.at[i], got.at[i], end_send.at[which, i], end_recv.at[which, i], device(i)
        )

    def cut_start(cut, first, values):
        low = values.astype(BF16)
        for k in range(blocks):
            at = mix(block_id, k, blocks)
            cut[at, :, first : first + values.shape[1]] = low[k * share : (k + 1) * share]

    def cut_send(cut, got, which):
        for i in range(1, blocks):
            cut_copy(cut, got, which, i).start()

    def owner_copy(cut, got, which):
        return remote(cut, got, end_send.at[which, 0], end_recv.at[which, 0], owner_id)

    def owner_send(cut, got, which):
        @pl.when(moves)
        def _():
            owner_copy(cut, got, which).start()

        @pl.when(held == mine)
        def _():
            got[...] = cut[...]

    def owner_wait(cut, got, which):
        @pl.when(moves)
        def _():
            owner_copy(cut, got, which).wait()

    def assemble(pieces):
        for block in range(blocks):

            @pl.when(block_id == block)
            def _(block=block):
                for i in range(blocks):
                    at = slice((block ^ i) * wide, ((block ^ i) + 1) * wide)
                    piece = pieces(i)
                    attn_ref[:rows, at] = piece[:, :wide]
                    attn_ref[rows:, at] = piece[:, wide:]

    assemble(lambda i: got_ref[i])
    small_ref[0] = jnp.zeros(small_ref.shape[1:], F32)
    b1_row_ref[0:1, :] = row_of(b1_ref)
    target = jnp.broadcast_to(target_ref[...].astype(F32), (8, rows)).T[:, 0:1]
    weight = jnp.concatenate([jnp.ones((rows, 1), F32), target], axis=0)

    def squares(values):
        weighted = jnp.sum(values * values, axis=1, keepdims=True) * weight
        return column_sum(weighted[:rows]), column_sum(weighted[rows:])

    loads[0].wait()
    branch = dot_nn(attn_ref[...], wo_ref[...])
    att_stat = squares(branch)
    for one in entry_loads:
        one.wait()
    streams = streams_ref[...].astype(F32)
    unit_one, rate_one = norm_parts(branch + streams)
    gain_one = row_of(ln1_gain_ref)
    out_one = unit_one * gain_one + row_of(ln1_bias_ref)
    ffn_all[0] = out_one.astype(BF16)
    for one in loads[1:7] + prob_loads[:2]:
        one.start()
    acc_ref[...] = jnp.broadcast_to(row_of(b2_ref), acc_ref.shape)

    def ffn_part(c, carry):
        for one in weight_loads(c):
            one.wait()
        at = columns(c)
        act, slope = gelu_pair(dot_nn(ffn_all[0], w1_ref[:, at]) + b1_row_ref[0:1, at])
        slope_ref[:, at] = slope
        act = act.astype(BF16)
        act_ref[c] = act
        acc_ref[...] += dot_nn(act, w2_ref[at, :])
        return carry

    lax.fori_loop(0, blocks, ffn_part, 0, unroll=True)
    branch_ffn = acc_ref[...]
    ffn_stat = squares(branch_ffn)
    unit_two, rate_two = norm_parts(branch_ffn + out_one)
    gain_two = row_of(ln2_gain_ref)
    out_two = unit_two * gain_two + row_of(ln2_bias_ref)
    out_stat = squares(out_two)
    h_out_ref[...] = out_two[:rows].astype(BF16)
    g_out_ref[...] = out_two[rows:].astype(BF16)
    results = [
        pltpu.make_async_copy(src, dst, result_sem.at[k])
        for k, (src, dst) in enumerate(
            (
                (h_out_ref, h_out_hbm),
                (g_out_ref, g_out_hbm),
                (h_grad_ref, h_grad_hbm),
                (g_grad_ref, g_grad_hbm),
                (mem_grad_ref, mem_grad_hbm),
            )
        )
    ]
    results[0].start()
    results[1].start()
    cot = cot_ref[...].astype(F32)
    grad_two = norm_back(unit_two, rate_two, cot * gain_two)
    grad_ffn = grad_two.astype(BF16)
    gf_all[0] = grad_ffn
    spread(gf_all, 1)
    for q in (2, 3):
        far_copy(2, q).wait_recv()
        far_copy(3, q ^ 1).start()
    tall = width // 128
    tall_part = part // 128
    stat_row = 5 * tall + blocks * tall_part
    early = small_ref.at[0]
    put_row(early, 0, column_sum(cot * unit_two))
    put_row(early, tall, column_sum(cot))
    put_row(early, 2 * tall, column_sum(grad_ffn.astype(F32)))
    acc_ref[...] = grad_two

    def ffn_back(c, carry):
        at = columns(c)
        grad_pre = (dot_nt(gf_all[0], w2_ref[at, :]) * slope_ref[:, at]).astype(BF16)
        gpre_ref[c] = grad_pre
        b1_row_ref[1:2, at] = column_sum(grad_pre.astype(F32))
        acc_ref[...] += dot_nt(grad_pre, w1_ref[:, at])
        return carry

    lax.fori_loop(0, blocks, ffn_back, 0, unroll=True)
    grad_out_one = acc_ref[...]
    put_row(early, 5 * tall, b1_row_ref[1:2, :])
    put_row(early, 3 * tall, column_sum(grad_out_one * unit_one))
    put_row(early, 4 * tall, column_sum(grad_out_one))
    grad_one = norm_back(unit_one, rate_one, grad_out_one * gain_one)
    resid_grad_ref[...] = grad_one
    grad_branch = grad_one.astype(BF16)
    gb_all[0] = grad_branch
    grad_attn = dot_nt(grad_branch, wo_ref[...]).astype(BF16)
    for block in range(blocks):

        @pl.when(block_id == block)
        def _(block=block):
            for i in range(blocks):
                at = slice((block ^ i) * wide, ((block ^ i) + 1) * wide)
                ga_send_ref[i, :, :wide] = grad_attn[:rows, at]
                ga_send_ref[i, :, wide:] = grad_attn[rows:, at]

    def ga_copy(i):
        return remote(
            ga_send_ref.at[i], ga_ref.at[i], ga_sem_send.at[i], ga_sem_recv.at[i], device(i)
        )

    for i in range(blocks - 1, 0, -1):
        ga_copy(i).start()
    spread(gb_all, 2)
    ga_ref[0] = ga_send_ref[0]
    lane = lax.broadcasted_iota(jnp.int32, (1, 128), 1)
    stats = jnp.zeros((1, 128), F32)
    terms = [att_stat[0], ffn_stat[0], out_stat[0], att_stat[1], ffn_stat[1], out_stat[1]]
    terms += [jnp.full((1, 1), float(rows), F32), column_sum(target)]
    for k, term in enumerate(terms):
        stats = jnp.where(lane == k, term, stats)
    early[stat_row : stat_row + 1, :] = stats

    small_steps = [("blk", bit) for bit in steps] + [("dp", bit) for bit in bits_of(groups)]

    def small_copy(k):
        axis, bit = small_steps[k]
        target_id = device(bit) if axis == "blk" else (flip(group_id, bit), block_id)
        return remote(
            small_ref.at[k], small_got.at[k], small_send.at[k], small_recv.at[k], target_id
        )

    def small_next(k):
        small_copy(k).wait_recv()
        small_ref[k + 1] = small_ref[k] + small_got[k]
        if k + 1 < len(small_steps):
            small_copy(k + 1).start()

    small_copy(0).start()

    def late_copy(k, i=0):
        bits = bits_of(groups)
        if k < nb:
            return remote(
                late_ref.at[k],
                late_got.at[k],
                small_send.at[8 + k],
                small_recv.at[8 + k],
                (flip(group_id, bits[k]), block_id),
            )
        return remote(
            late_ref.at[nb],
            late_all.at[i],
            small_send.at[8 + nb + i],
            small_recv.at[8 + nb + i],
            device(i),
        )

    def late_next(k):
        late_copy(k).wait_recv()
        late_ref[k + 1] = late_ref[k] + late_got[k]
        if k + 1 < nb:
            late_copy(k + 1).start()
        else:
            for i in range(1, blocks):
                late_copy(nb, i).start()

    x_rows = keys + rows * blocks

    done = set()

    def job_event(job, stage):
        value = job_next(job, stage)
        if stage < nb - 1:
            return
        done.add(job)
        if job < 2:
            w2_cut[:, job * (width // 2) : (job + 1) * (width // 2)] = value.astype(BF16)
            if {0, 1} <= done:
                owner_send(w2_cut, w2_got, 2)
        elif job < 4:
            cut_start(w1_cut, (job - 2) * (part // 2), value)
            if {2, 3} <= done:
                cut_send(w1_cut, w1_got, 0)
        elif job == 4:
            wo_cut[...] = value.astype(BF16)
            owner_send(wo_cut, wo_got, 3)
        else:
            cut_start(head_cut.at[job - 5], 0, value)
            cut_send(head_cut.at[job - 5], head_got.at[job - 5], 4 + job - 5)

    def happen(spot):
        for kind, first, *more in plan.get(spot, ()):
            if kind == "job":
                job_event(first, *more)
            elif kind == "small":
                small_next(first)
            else:
                late_next(first)

    own_at = columns(block_id)
    act_ref[0] = act_ref[block_id]
    gpre_ref[0] = gpre_ref[block_id]
    loads[7].wait()
    for one in row_loads:
        one.wait()
    far_copy(2, 1).wait_recv()
    for q in range(1, blocks):
        far_copy(1, q).wait_recv()
        far_copy(3, q).wait_recv()

    def slice_front(i, carry):
        assemble(lambda k: own_ref[i] if k == 0 else far_ref[k - 1, i - 1])
        other = dot_nn(attn_ref[...], wo_ref[...]) + ffn_all[i].astype(F32)
        other = norm_parts(other)[0] * row_of(ln1_gain_ref) + row_of(ln1_bias_ref)
        ffn_all[i] = other.astype(BF16)
        act, slope = gelu_pair(dot_nn(ffn_all[i], w1_ref[:, own_at]) + b1_row_ref[0:1, own_at])
        act_ref[i] = act.astype(BF16)
        slope_ref[:, columns(i)] = slope
        return carry

    lax.fori_loop(1, blocks, slice_front, 0)

    def slice_back(i, carry):
        @pl.when(i == 1)
        def _():
            near_ready(gf_all, 1)

        @pl.when(i == steps[-1])
        def _():
            relay(gf_all, 1)

        @pl.when(i == steps[-1] + 1)
        def _():
            collect(gf_all, 1)

        grad_pre = dot_nt(gf_all[i], w2_ref[own_at, :]) * slope_ref[:, columns(i)]
        gpre_ref[i] = grad_pre.astype(BF16)
        return carry

    lax.fori_loop(1, blocks, slice_back, 0)

    def flat(ref):
        return ref[...].reshape(blocks * both, ref.shape[2])

    def put_shares(first, count, values):
        tall_share = values.shape[0] // groups
        lanes_here = values.shape[1] // count
        low = values.astype(BF16)
        for k in range(count):
            for d in range(groups):
                src_refs[first + k][place_of(d, orders[first + k])] = low[
                    d * tall_share : (d + 1) * tall_share,
                    k * lanes_here : (k + 1) * lanes_here,
                ]
            job_start(first + k)

    put_shares(0, 2, dot_tn(flat(act_ref), flat(gf_all)))
    put_shares(2, 2, dot_tn(flat(ffn_all), flat(gpre_ref)))
    happen("ffn")

    x_loads = [
        pltpu.make_async_copy(
            src, w2_ref.at[pl.ds(first, src.shape[0])], late_load_sem.at[k]
        )
        for k, (src, first) in enumerate(((x_hbm, 0), (pos_hbm, x_rows)))
    ]
    for one in x_loads:
        one.start()

    def turn(c, carry):
        at = pl.ds(pl.multiple_of(c * 128, 128), 128)
        w1_ref[:, at] = w2_ref[at, :].T
        return carry

    x_loads[0].wait()
    lax.fori_loop(0, x_rows // 128, turn, 0)
    x_loads[1].wait()
    lax.fori_loop(x_rows // 128, (x_rows + dist_count) // 128, turn, 0)
    late_loads = [
        pltpu.make_async_copy(
            src, w2_ref.at[pl.ds(k * width, width)], late_load_sem.at[2 + k]
        )
        for k, src in enumerate((wq_hbm, wk_hbm, wv_hbm))
    ]
    for one in late_loads:
        one.start()
    for one in loads[1:7]:
        one.wait()
    kv_acc[...] = jnp.zeros_like(kv_acc)
    rel_acc[...] = jnp.zeros_like(rel_acc)
    late_ref[0] = jnp.zeros(late_ref.shape[1:], F32)
    for i in range(1, blocks):
        ga_copy(i).wait_recv()
    turned_ref[...] = jnp.zeros_like(turned_ref)
    happen("pre")

    def pack_copy(h, i):
        return remote(
            pack_ref.at[h, i], pack_got.at[h, i], pack_send.at[h, i], pack_recv.at[h, i], device(i)
        )


    for h in range(heads):
        own = slice(h * HEAD_DIM, (h + 1) * HEAD_DIM)

        def tile(piece, carry, h=h, own=own):
            for slot in range(blocks):
                if plan.get((h, slot)):

                    @pl.when(piece == slot)
                    def _(slot=slot):
                        happen((h, slot))

            owner = mix(block_id, piece, blocks)
            tok_at = pl.ds(pl.multiple_of(owner * rows, 32), rows)
            rel_start = pl.multiple_of((blocks - 1) * rows - owner * rows, 128)
            rel_at = pl.ds(rel_start, span)
            seg = info_ref[tok_at, 1:2]
            seg = jnp.concatenate([seg, seg], axis=0)
            raw = q_ref[piece, :, own]
            q_word = (raw + bias_ref[0:1, own]).astype(BF16)
            q_rel = (raw + bias_ref[1:2, own]).astype(BF16)
            q_seg = raw + bias_ref[2:3, own]
            embed = bias_ref[3:5, own]
            other = slice(wide + h * HEAD_DIM, wide + (h + 1) * HEAD_DIM)
            ga = jnp.concatenate([ga_ref[piece, :, own], ga_ref[piece, :, other]], axis=0)
            probs = prob_ref[h % 2, piece]
            ga_f = ga.astype(F32) * SCALE
            row_dot = jnp.sum(ga_f * af_ref[piece, :, own], axis=1, keepdims=True)
            grad_prob = dot_nt(ga_f.astype(BF16), v_ref[h])
            grad_score = probs.astype(F32) * (grad_prob - row_dot)
            grad_low = grad_score.astype(BF16)
            wide_word = dot_nn(grad_low, k_ref[h])
            grad_word = wide_word[:, :HEAD_DIM]
            total = wide_word[:, HEAD_DIM : HEAD_DIM + 1]
            ones = wide_word[:, HEAD_DIM + 2 : HEAD_DIM + 3]
            differ = ones + seg * (total - 2.0 * ones)
            same = total - differ
            grad_seg = same * embed[0:1] + differ * embed[1:2]
            wind = jnp.concatenate(
                [
                    spread_rows(grad_score[:rows], rows, keys),
                    spread_rows(grad_score[rows:], rows, keys),
                ],
                axis=0,
            ).astype(BF16)
            grad_rel = dot_nn(wind, rel_ref[h, rel_at, :])
            kv_acc[h, :HEAD_DIM] += dot_tn(q_word, grad_low)
            kv_acc[h, HEAD_DIM:] += dot_tn(ga, probs)
            rel_acc[h, :, rel_at] += dot_tn(q_rel, wind)
            grad_q = (grad_word + grad_rel + grad_seg).astype(BF16)
            for first, part_q in ((mem_all, grad_q[:rows]), (keys, grad_q[rows:])):
                at = pl.ds(pl.multiple_of(first + owner * rows, 32), rows)
                turned_ref[at, 2 * HEAD_DIM :] = part_q
            pack_ref[h, piece, :rows, :HEAD_DIM] = grad_q[:rows]
            pack_ref[h, piece, :rows, HEAD_DIM:] = grad_q[rows:]
            late_ref[0, :, own] += jnp.concatenate(
                [
                    column_sum(grad_word),
                    column_sum(grad_rel),
                    column_sum(grad_seg),
                    column_sum(same * q_seg),
                    column_sum(differ * q_seg),
                    jnp.zeros((3, HEAD_DIM), F32),
                ],
                axis=0,
            )
            return carry

        prob_loads[h].wait()
        lax.fori_loop(0, blocks, tile, 0)
        if h + 2 < heads:
            prob_loads[h + 2].start()
        if h == 0:
            near_ready(gb_all, 2)
            relay(gb_all, 2)
        if h == 1:
            collect(gb_all, 2)
            put_shares(4, 1, dot_tn(flat(out_ref), flat(gb_all)))
        full = kv_acc[h].T.astype(BF16)
        turned_ref[:keys, : 2 * HEAD_DIM] = full
        for k in range(blocks):
            at = mix(block_id, k, blocks)
            mem_part = full[k * mem_rows : (k + 1) * mem_rows]
            tok_part = full[mem_all + k * rows : mem_all + (k + 1) * rows]
            pack_ref[h, at, rows : rows + mem_rows, :] = mem_part
            pack_ref[h, at, rows + mem_rows :, :] = tok_part
        for i in range(blocks - 1, 0, -1):
            pack_copy(h, i).start()
        if h == heads - 1:
            late_copy(0).start()
        happen(("packed", h))
        grad_wr = dot_nn(
            w1_ref[:, x_rows : x_rows + dist_count], rel_acc[h].T.astype(BF16)
        )
        grad_kvq = dot_nn(w1_ref[:, :x_rows], turned_ref[...])
        put_shares(5 + h, 1, jnp.concatenate([grad_kvq, grad_wr], axis=1))
        happen(("head", h))

    happen("tail")

    for h in range(heads - 1):
        for i in range(1, blocks):
            pack_copy(h, i).wait_recv()
    happen("pack")
    for one in late_loads:
        one.wait()
    for i in range(1, blocks):
        pack_copy(heads - 1, i).wait_recv()
    for block in range(blocks):

        @pl.when(block_id == block)
        def _(block=block):
            for h in range(heads):
                for i in range(blocks):
                    at = (block ^ i) * wide + h * HEAD_DIM
                    to = slice(at, at + HEAD_DIM)
                    piece = pack_ref[h, 0] if i == 0 else pack_got[h, i]
                    dq_all[:rows, to] = piece[:rows, :HEAD_DIM]
                    dq_all[rows:, to] = piece[:rows, HEAD_DIM:]
                    dkv_all[:, to] = piece[rows:, :HEAD_DIM]
                    dkv_all[:, width + at : width + at + HEAD_DIM] = piece[rows:, HEAD_DIM:]

    grad_rows = dot_nt(dkv_all[:, :width], w2_ref[width : 2 * width, :]) + dot_nt(
        dkv_all[:, width:], w2_ref[2 * width : 3 * width, :]
    )
    grad_streams = resid_grad_ref[...] + dot_nt(dq_all[...], w2_ref[:width, :])
    h_grad_ref[...] = grad_streams[:rows] + grad_rows[mem_rows:]
    g_grad_ref[...] = grad_streams[rows:]
    mem_grad_ref[...] = grad_rows[:mem_rows]
    for one in results[2:]:
        one.start()

    happen("end")
    owner_wait(w2_cut, w2_got, 2)
    owner_wait(wo_cut, wo_got, 3)
    w2_out_ref[...] = w2_got[...]
    wo_out_ref[...] = wo_got[...]
    w1_out_ref[0] = w1_cut[0]
    for i in range(1, blocks):
        cut_copy(w1_cut, w1_got, 0, i).wait()
        w1_out_ref[i] = w1_got[i]
    for h in range(heads):
        head_out_ref[h, 0] = head_cut[h, 0]
        for i in range(1, blocks):
            cut_copy(head_cut.at[h], head_got.at[h], 4 + h, i).wait()
            head_out_ref[h, i] = head_got[h, i]

    small_out_ref[...] = small_ref[len(small_steps)]
    for i in range(1, blocks):
        late_copy(nb, i).wait()
        late_out_ref[i] = late_all[i]
    late_out_ref[0] = late_ref[nb]

    for k in range(len(small_steps)):
        small_copy(k).wait_send()
    for k in range(nb):
        late_copy(k).wait_send()
    for h in range(heads):
        for i in range(1, blocks):
            pack_copy(h, i).wait_send()
    for one in results:
        one.wait()
    for job in range(jobs_count):
        job_done(job)
    for i in range(1, blocks):
        ga_copy(i).wait_send()
        for q in range(1, blocks):
            far_copy(i, q).wait_send()
    finish(gf_all, 1)
    finish(gb_all, 2)


def finish_kernel(
    heads,
    h_ref,
    g_ref,
    h_grad_ref,
    g_grad_ref,
    mem_grad_ref,
    head_ref,
    w1_ref,
    w2_ref,
    wo_ref,
    small_ref,
    late_ref,
    h_out_ref,
    g_out_ref,
    h_grad_out_ref,
    g_grad_out_ref,
    mem_grad_out_ref,
    wq_out_ref,
    wk_out_ref,
    wv_out_ref,
    wr_out_ref,
    wo_out_ref,
    w1_out_ref,
    w2_out_ref,
    rw_out_ref,
    rr_out_ref,
    rs_out_ref,
    embed_out_ref,
    ln1_gain_out_ref,
    ln1_bias_out_ref,
    b1_out_ref,
    b2_out_ref,
    ln2_gain_out_ref,
    ln2_bias_out_ref,
    rms_out_ref,
    rows_ref,
):
    block_id = lax.axis_index("blk")
    blocks, share, part = w1_ref.shape
    width = h_ref.shape[1]
    wide = heads * HEAD_DIM
    tall = width // 128
    tall_part = part // 128
    stat_row = 5 * tall + blocks * tall_part

    def put_lanes(out, values, stride, first):
        count = values.shape[0]
        for j in range(values.shape[1] // 128):
            out[pl.ds(first + j, count, stride=stride), :] = values[:, 128 * j : 128 * (j + 1)]

    h_out_ref[...] = h_ref[...]
    g_out_ref[...] = g_ref[...]
    h_grad_out_ref[...] = h_grad_ref[...]
    g_grad_out_ref[...] = g_grad_ref[...]
    mem_grad_out_ref[...] = mem_grad_ref[...]
    put_lanes(w2_out_ref, w2_ref[...].astype(F32), tall, 0)
    put_lanes(wo_out_ref, wo_ref[...].astype(F32), tall, 0)
    for i in range(blocks):
        first = mix(block_id, i, blocks) * tall_part
        put_lanes(w1_out_ref, w1_ref[i].astype(F32), blocks * tall_part, first)
    for block in range(blocks):

        @pl.when(block_id == block)
        def _(block=block):
            for i in range(blocks):
                at = slice((block ^ i) * wide, ((block ^ i) + 1) * wide)
                for h in range(heads):
                    first = (block ^ i) * wide + h * HEAD_DIM
                    for k in range(4):
                        rows_ref[k, :share, first : first + HEAD_DIM] = head_ref[
                            h, i, :, k * HEAD_DIM : (k + 1) * HEAD_DIM
                        ].astype(F32)
                rows_ref[4, :8, at] = late_ref[i]

    for k, out in enumerate((wk_out_ref, wv_out_ref, wq_out_ref, wr_out_ref)):
        put_lanes(out, rows_ref[k, :share, :], tall, 0)
    put_row(rw_out_ref, 0, rows_ref[4, 0:1, :])
    put_row(rr_out_ref, 0, rows_ref[4, 1:2, :])
    put_row(rs_out_ref, 0, rows_ref[4, 2:3, :])
    embed_out_ref[...] = rows_ref[4, 3:5, :]
    ln2_gain_out_ref[...] = small_ref[:tall]
    ln2_bias_out_ref[...] = small_ref[tall : 2 * tall]
    b2_out_ref[...] = small_ref[2 * tall : 3 * tall]
    ln1_gain_out_ref[...] = small_ref[3 * tall : 4 * tall]
    ln1_bias_out_ref[...] = small_ref[4 * tall : 5 * tall]
    b1_out_ref[...] = small_ref[5 * tall : stat_row]
    stats = small_ref[stat_row : stat_row + 1]
    lane = lax.broadcasted_iota(jnp.int32, (1, 128), 1)
    counts = jnp.where(lane < 3, stats[:, 6:7], stats[:, 7:8]) * float(width)
    rms_out_ref[...] = jnp.sqrt(stats / counts)[0, :6]


def exchange_plan(groups, blocks, heads):
    near = tuple(bits_of(groups))
    jobs = 5 + heads
    smalls = len(near) + len(bits_of(blocks))
    if (groups, blocks, heads) == (8, 4, 3):
        orders = (
            (2, 4, 1),
            (1, 2, 4),
            (1, 2, 4),
            (2, 4, 1),
            (1, 2, 4),
            (2, 4, 1),
            (1, 2, 4),
            (1, 2, 4),
        )
        plan = {
            "ffn": [("small", 0)],
            "pre": [("small", 1)],
            (0, 2): [("job", 0, 0), ("job", 1, 0)],
            (0, 3): [("small", 2)],
            (1, 1): [("small", 3)],
            (1, 2): [("job", 2, 0), ("job", 3, 0)],
            ("packed", 1): [("small", 4)],
            ("head", 1): [("job", 1, 1)],
            (2, 1): [("job", 0, 1)],
            ("packed", 2): [("job", 5, 0), ("job", 4, 0)],
            "end": [("job", 2, 1), ("late", 0), ("job", 6, 0), ("job", 0, 2), ("job", 3, 1), ("job", 7, 0), ("late", 1), ("job", 1, 2), ("job", 3, 2), ("late", 2), ("job", 4, 1), ("job", 5, 1), ("job", 6, 1), ("job", 2, 2), ("job", 5, 2), ("job", 7, 1), ("job", 4, 2), ("job", 6, 2), ("job", 7, 2)],
        }
        return orders, plan
    plan = {"end": [("job", job, stage) for stage in range(len(near)) for job in range(jobs)]}
    plan["end"] += [("small", k) for k in range(smalls)] + [("late", k) for k in range(len(near))]
    return (near,) * jobs, plan


def whole(shape):
    return pl.BlockSpec(shape, lambda *_: (0,) * len(shape))


def local(
    h_in,
    g_in,
    memory,
    cot_h,
    cot_g,
    perm_order,
    target,
    segment,
    mem_flag,
    w_q,
    w_k,
    w_v,
    w_r,
    w_o,
    r_w_bias,
    r_r_bias,
    r_s_bias,
    seg_embed,
    ln1_gain,
    ln1_bias,
    w_1,
    b_1,
    w_2,
    b_2,
    ln2_gain,
    ln2_bias,
):
    _, rows, width = h_in.shape
    mem_rows = memory.shape[1]
    hidden = w_1.shape[1]
    blocks = lax.axis_size("blk")
    groups = lax.axis_size("dp")
    tok_all = rows * blocks
    mem_all = mem_rows * blocks
    keys = mem_all + tok_all
    dist_count = tok_all + keys
    heads = HEADS // blocks
    wide = heads * HEAD_DIM
    both = 2 * rows
    pair = mem_rows + rows
    part = hidden // blocks
    tall = width // 128
    share = width // (groups * blocks)
    nb = len(bits_of(groups))
    hbm = pl.BlockSpec(memory_space=pltpu.HBM)
    vmem = pl.BlockSpec(memory_space=pltpu.VMEM)
    shape = jax.ShapeDtypeStruct

    def lanes(values):
        return values.reshape(-1, 128)

    coarse, fine = position_units(keys - 1, dist_count, width, 32)
    (
        probs, attn_f, q_raw, k_aug, v_all, rel_heads, got_out, attn_out, pack_out, x_all, pos_table,
        query_info, biases,
    ) = pl.pallas_call(
        functools.partial(attn_fwd_kernel, heads, rows, mem_rows, blocks),
        name="attn_fwd",
        grid=(blocks,),
        in_specs=[hbm] * 3
        + [whole((1, rows))] * 3
        + [pl.BlockSpec(memory_space=pltpu.SMEM)]
        + [hbm] * 4
        + [whole((tall, 128))] * 3
        + [whole((2, width)), whole(coarse.shape), whole(fine.shape)],
        out_specs=[
            pl.BlockSpec((heads, 1, both, keys), lambda s: (0, blocks - 1 - s, 0, 0)),
            pl.BlockSpec((1, both, wide), lambda s: (blocks - 1 - s, 0, 0)),
            hbm,
            hbm,
            hbm,
            hbm,
            whole((blocks, rows, 2 * wide)),
            hbm,
            hbm,
            hbm,
            hbm,
            whole((tok_all, 8)),
            whole((8, wide)),
        ],
        out_shape=[
            shape((heads, blocks, both, keys), BF16),
            shape((blocks, both, wide), F32),
            shape((blocks, both, wide), F32),
            shape((heads, keys, 2 * HEAD_DIM), BF16),
            shape((heads, keys, HEAD_DIM), BF16),
            shape((heads, dist_count, HEAD_DIM), BF16),
            shape((blocks, rows, 2 * wide), BF16),
            shape((blocks, both, wide), BF16),
            shape((blocks, rows, 2 * wide), BF16),
            shape((keys + tok_all, width), BF16),
            shape((dist_count, width), BF16),
            shape((tok_all, 8), F32),
            shape((8, wide), F32),
        ],
        scratch_shapes=[
            pltpu.VMEM((width, 3 * wide), BF16),
            pltpu.VMEM((width, wide), BF16),
            pltpu.VMEM((both, keys), F32),
            pltpu.VMEM((blocks, 3, 1, rows), jnp.int32),
            pltpu.VMEM((keys + tok_all, width), BF16),
            pltpu.VMEM((blocks, rows, 2 * wide), BF16),
            pltpu.VMEM((blocks, both, wide), BF16),
            pltpu.VMEM((blocks, rows, 2 * wide), BF16),
            pltpu.VMEM((blocks, both, wide), F32),
            pltpu.VMEM((heads, keys, 2 * HEAD_DIM), BF16),
            pltpu.VMEM((heads, keys, HEAD_DIM), BF16),
            pltpu.VMEM((heads, dist_count, HEAD_DIM), BF16),
            pltpu.VMEM((dist_count, width), BF16),
            pltpu.VMEM((8, keys), F32),
            pltpu.SemaphoreType.DMA((blocks, 3)),
            pltpu.SemaphoreType.DMA((blocks, 3)),
            pltpu.SemaphoreType.DMA((blocks, 3)),
            pltpu.SemaphoreType.DMA((blocks, 3)),
            pltpu.SemaphoreType.DMA((blocks,)),
            pltpu.SemaphoreType.DMA((blocks,)),
            pltpu.SemaphoreType.DMA((6,)),
            pltpu.SemaphoreType.DMA((8,)),
            pltpu.VMEM((4, width, width), BF16),
            pltpu.SemaphoreType.DMA((4,)),
        ],
        compiler_params=pltpu.CompilerParams(
            vmem_limit_bytes=60 << 20, collective_id=0, has_side_effects=True
        ),
    )(
        memory[0], h_in[0], g_in[0], perm_order, target, segment, mem_flag, w_q, w_k, w_v, w_r,
        lanes(r_w_bias), lanes(r_r_bias), lanes(r_s_bias), seg_embed, coarse, fine,
    )

    near = tuple(bits_of(groups))
    orders, plan = exchange_plan(groups, blocks, heads)
    job_shapes = (
        [(part // groups, width // 2)] * 2
        + [(width // groups, part // 2)] * 2
        + [(wide // groups, width)]
        + [(width // groups, 4 * HEAD_DIM)] * heads
    )
    sources = [pltpu.VMEM((groups,) + one, BF16) for one in job_shapes]
    receivers = [
        pltpu.VMEM((groups >> (k + 1),) + one, BF16) for one in job_shapes for k in range(nb)
    ]
    bits = len(bits_of(blocks)) + nb
    square = width * width // (groups * blocks * 128)
    oblong = width * hidden // (groups * blocks * 128)
    grads_shape = [
        shape((rows, width), BF16),
        shape((rows, width), BF16),
        shape((rows, width), F32),
        shape((rows, width), F32),
        shape((mem_rows, width), F32),
    ]
    parts = pl.pallas_call(
        functools.partial(main_kernel, groups, heads, mem_rows, orders, plan),
        name="main",
        in_specs=[vmem] + [hbm] * 4 + [vmem] * 3 + [hbm] * 16 + [vmem] * 6,
        out_specs=[hbm] * 5 + [vmem] * 6,
        out_shape=grads_shape
        + [
            shape((heads, blocks, share, 4 * HEAD_DIM), BF16),
            shape((blocks, share, part), BF16),
            shape((part // groups, width), BF16),
            shape((wide // groups, width), BF16),
            shape((SMALL_ROWS, 128), F32),
            shape((blocks, 8, wide), F32),
        ],
        scratch_shapes=[
            pltpu.VMEM((width, width), BF16),
            pltpu.VMEM((width, hidden), BF16),
            pltpu.VMEM((hidden, width), BF16),
            pltpu.VMEM((both, width), BF16),
            pltpu.VMEM((both, hidden), F32),
            pltpu.VMEM((blocks, both, part), BF16),
            pltpu.VMEM((blocks, both, part), BF16),
            pltpu.VMEM((blocks, both, width), BF16),
            pltpu.VMEM((blocks, both, width), BF16),
            pltpu.VMEM((blocks, both, width), BF16),
            pltpu.VMEM((8, hidden), F32),
            pltpu.VMEM((both, width), F32),
            pltpu.VMEM((both, width), BF16),
            pltpu.VMEM((both, width), BF16),
            pltpu.VMEM((both, width), F32),
            pltpu.VMEM((2, blocks, both, keys), BF16),
            pltpu.VMEM((blocks, both, wide), F32),
            pltpu.VMEM((blocks, both, wide), F32),
            pltpu.VMEM((heads, keys, 2 * HEAD_DIM), BF16),
            pltpu.VMEM((heads, keys, HEAD_DIM), BF16),
            pltpu.VMEM((heads, dist_count, HEAD_DIM), BF16),
            pltpu.VMEM((blocks, both, wide), BF16),
            pltpu.VMEM((blocks, rows, 2 * wide), BF16),
            pltpu.VMEM((blocks - 1, blocks - 1, rows, 2 * wide), BF16),
            pltpu.VMEM((blocks, rows, 2 * wide), BF16),
            pltpu.VMEM((blocks, rows, 2 * wide), BF16),
            pltpu.VMEM((heads, 2 * HEAD_DIM, keys), F32),
            pltpu.VMEM((heads, HEAD_DIM, dist_count), F32),
            pltpu.VMEM((keys + tok_all, 3 * HEAD_DIM), BF16),
            pltpu.VMEM((heads, blocks, rows + pair, 2 * HEAD_DIM), BF16),
            pltpu.VMEM((heads, blocks, rows + pair, 2 * HEAD_DIM), BF16),
            pltpu.VMEM((both, width), BF16),
            pltpu.VMEM((pair, 2 * width), BF16),
            pltpu.VMEM((bits + 1, SMALL_ROWS, 128), F32),
            pltpu.VMEM((bits, SMALL_ROWS, 128), F32),
            pltpu.VMEM((nb + 1, 8, wide), F32),
            pltpu.VMEM((nb, 8, wide), F32),
            pltpu.VMEM((blocks, 8, wide), F32),
        ]
        + sources
        + receivers
        + [
            pltpu.VMEM((blocks, share, part), BF16),
            pltpu.VMEM((blocks, share, part), BF16),
            pltpu.VMEM((heads, blocks, share, 4 * HEAD_DIM), BF16),
            pltpu.VMEM((heads, blocks, share, 4 * HEAD_DIM), BF16),
            pltpu.VMEM((part // groups, width), BF16),
            pltpu.VMEM((part // groups, width), BF16),
            pltpu.VMEM((wide // groups, width), BF16),
            pltpu.VMEM((wide // groups, width), BF16),
            pltpu.SemaphoreType.DMA((10 + heads + 2 * blocks,)),
            pltpu.SemaphoreType.DMA((5,)),
            pltpu.SemaphoreType.DMA((3, blocks)),
            pltpu.SemaphoreType.DMA((3, blocks)),
            pltpu.SemaphoreType.DMA((len(job_shapes), nb)),
            pltpu.SemaphoreType.DMA((len(job_shapes), nb)),
            pltpu.SemaphoreType.DMA((heads, blocks)),
            pltpu.SemaphoreType.DMA((heads, blocks)),
            pltpu.SemaphoreType.DMA((8 + nb + blocks,)),
            pltpu.SemaphoreType.DMA((8 + nb + blocks,)),
            pltpu.SemaphoreType.DMA((4 + heads, blocks)),
            pltpu.SemaphoreType.DMA((4 + heads, blocks)),
            pltpu.SemaphoreType.DMA((blocks, blocks)),
            pltpu.SemaphoreType.DMA((blocks, blocks)),
            pltpu.SemaphoreType.DMA((blocks,)),
            pltpu.SemaphoreType.DMA((blocks,)),
            pltpu.SemaphoreType.DMA((2, blocks)),
            pltpu.SemaphoreType.DMA((4,)),
            pltpu.VMEM((rows, width), BF16),
            pltpu.VMEM((rows, width), BF16),
            pltpu.VMEM((rows, width), F32),
            pltpu.VMEM((rows, width), F32),
            pltpu.VMEM((mem_rows, width), F32),
            pltpu.SemaphoreType.DMA((5,)),
        ],
        compiler_params=pltpu.CompilerParams(
            vmem_limit_bytes=60 << 20, collective_id=1, has_side_effects=True
        ),
    )(
        got_out, h_in[0], g_in[0], cot_h[0], cot_g[0], target, biases, query_info,
        w_o, w_1, w_2, w_q, w_k, w_v, probs, attn_f, q_raw, k_aug, v_all, rel_heads, attn_out,
        pack_out, x_all, pos_table,
        lanes(ln1_gain), lanes(ln1_bias), lanes(b_1), lanes(b_2), lanes(ln2_gain), lanes(ln2_bias),
    )
    outs = pl.pallas_call(
        functools.partial(finish_kernel, heads),
        name="finish",
        in_specs=[vmem] * 11,
        out_specs=[vmem] * 23,
        out_shape=grads_shape
        + [shape((square, 128), F32)] * 5
        + [shape((oblong, 128), F32)] * 2
        + [shape((tall, 128), F32)] * 3
        + [shape((2, width), F32)]
        + [shape((tall, 128), F32)] * 2
        + [shape((hidden // 128, 128), F32)]
        + [shape((tall, 128), F32)] * 3
        + [shape((6,), F32)],
        scratch_shapes=[pltpu.VMEM((5, max(8, share), width), F32)],
        compiler_params=pltpu.CompilerParams(vmem_limit_bytes=60 << 20),
    )(*parts)
    outs = list(outs)
    for k in range(5):
        outs[k] = outs[k][None]
    for k in list(range(5, 15)) + list(range(16, 22)):
        outs[k] = outs[k].reshape(-1)
    return tuple(outs)


def solution(mesh):
    rows = P("dp", "blk", None)
    ints = P("dp", "blk")
    flat = P(("dp", "blk"))
    return jax.shard_map(
        local,
        mesh=mesh,
        in_specs=(rows,) * 5 + (ints,) * 3 + (P("dp"),) + (P(),) * 17,
        out_specs=(rows,) * 5 + (flat,) * 7 + (P(),) * 11,
        check_vma=False,
    )
```
